32 devices in a mesh: ctx: 16 (over z, x, core), head: 2 (over y).
Axes of the slice: x: 2, y: 2, z: 4, core: 2. Of those that a mesh axis runs over, the one named last changes fastest.
Arguments:
- latent: bfloat16 [6144, 5120], P('ctx', 'head'), may hold values from -6 to 6
- probe: bfloat16 [6144, 5120], P('ctx'), may hold values from -6 to 6
- norm_gain: float32 [5120], replicated, may hold values from 0.25 to 1.75
- w_query: bfloat16 [5120, 3072], P('ctx', 'head'), may hold values from -2 to 2, as said below
- w_key: bfloat16 [5120, 3072], P('ctx', 'head'), may hold values from -2 to 2, as said below
- w_value: bfloat16 [5120, 3072], P('ctx', 'head'), may hold values from -0.078125 to 0.078125
- w_out: bfloat16 [3072, 5120], P('head', 'ctx'), may hold values from -0.109375 to 0.109375
- tile_mask: int32 [48, 48], replicated, may hold values from 0 to 1, as said below
Outputs:
- mixed: bfloat16 [6144, 5120], P('ctx', 'head')
- branch_tangent: bfloat16 [6144, 5120], P('ctx', 'head')
- trace_terms: float32 [6144], P('ctx')
The draws below stay inside these ranges and needn't reach their ends.
Inputs may be any that keep to these rules, and one draw needn't show every extreme that they name: `tile_mask`: entry [q, k] is 0 where |q - k| > 3, and 1 where q == k or |q - k| == 3. `w_query`: entries of order 5120^-0.5. `w_key`: entries of order 5120^-0.5.
All inputs are finite; a program needn't handle non-finite values.
Results may differ from the reference program's by a relative error of at most 0.011.
Values may be sent and summed in bfloat16 or wider, within the bound.
A program may use at most 192 MiB of HBM per device.

```python
import jax
import jax.numpy as jnp
from jax import lax

D = 5120
HD = 128
HEADS = 24
TILE = 128
TILES_DEV = 3
TOK_DEV = 384
TOKENS = 6144
NT = 48
N_CTX = 16
N_HEAD = 2


def pair_weights(key):
    base = jax.random.fold_in(key, 11)
    shared = jnp.clip(jax.random.normal(jax.random.fold_in(base, 1), (D, HEADS * HD), jnp.float32), -6.0, 6.0)
    others = jnp.clip(jax.random.normal(jax.random.fold_in(base, 2), (D, HEADS * HD), jnp.float32), -6.0, 6.0)
    return (shared, others)


def draw_w_key(key, part):
    shared, others = pair_weights(key)
    return jnp.clip(shared * D ** (-0.5), -2.0, 2.0).astype(jnp.bfloat16)


def draw_w_query(key, part):
    shared, others = pair_weights(key)
    blended = others
    return jnp.clip(blended * D ** (-0.5), -2.0, 2.0).astype(jnp.bfloat16)


def draw_tile_mask(key, part):
    rows_idx = jnp.arange(NT, dtype=jnp.int32)[:, None]
    cols_idx = jnp.arange(NT, dtype=jnp.int32)[None, :]
    levels = jax.random.randint(jax.random.fold_in(key, 1), (NT // TILES_DEV,), 1, 5)
    row_level = levels[rows_idx // TILES_DEV]
    coins = jax.random.randint(jax.random.fold_in(key, 2), (NT, NT), 0, 4)
    keeper = coins < row_level
    distance = jnp.abs(rows_idx - cols_idx)
    banded = distance <= TILES_DEV
    forced = (distance == 0) | (distance == TILES_DEV)
    return jnp.where(banded & (keeper | forced), 1, 0).astype(jnp.int32)


def shard_levels(own_key, dims, pieces, smallest, largest):
    gain = 1.0
    for dim, parts in pieces:
        steps = jax.random.uniform(jax.random.fold_in(jax.random.fold_in(own_key, 6), dim), (parts,), jnp.float32, smallest / len(pieces), largest / len(pieces))
        gain = gain * jnp.repeat(jnp.exp(steps), dims[dim] // parts).reshape((-1,) + (1,) * (len(dims) - 1 - dim))
    return gain


def centred(stream_key, dims, deviation, most, cuts=(), kind=jnp.bfloat16):
    drawn = deviation * jax.random.normal(stream_key, dims, jnp.float32)
    if cuts:
        drawn = drawn * shard_levels(stream_key, dims, cuts, -0.22, 0.18)
    return jnp.clip(drawn, -most, most).astype(kind)


def setup_inputs(seed: int = 0) -> dict:
    arg_keys = jax.random.split(jax.random.key(seed), 9)
    return {
        "latent": centred(arg_keys[0], (TOKENS, D), 1.0, 6.0, ((0, 16), (1, 2))),
        "probe": centred(arg_keys[1], (TOKENS, D), 1.0, 6.0, ((0, 16),)),
        "norm_gain": jnp.clip(1.0 + 0.15 * jax.random.normal(arg_keys[2], (D,), jnp.float32), 0.25, 1.75),
        "w_query": draw_w_query(jax.random.fold_in(arg_keys[8], 71), 0),
        "w_key": draw_w_key(jax.random.fold_in(arg_keys[8], 71), 0),
        "w_value": centred(arg_keys[5], (D, HEADS * HD), D ** -0.5, 0.078125, ((0, 16), (1, 2))),
        "w_out": centred(arg_keys[6], (HEADS * HD, D), (HEADS * HD) ** -0.5, 0.109375, ((0, 2), (1, 16))),
        "tile_mask": draw_tile_mask(jax.random.fold_in(arg_keys[8], 71), 0),
    }


def attend_block(queries, queries_t, keys, values, keys_t, values_t, allowed):
    score_scale = HD ** (-0.5)
    scores = jnp.einsum('qhd,khd->hqk', queries.astype(jnp.float32), keys.astype(jnp.float32)) * score_scale
    masked = jnp.where(allowed[None], scores, -jnp.inf)
    highest = lax.optimization_barrier(jnp.max(masked, -1, keepdims=True))
    expos = jnp.exp(masked - highest)
    probs = expos / lax.optimization_barrier(jnp.sum(expos, -1, keepdims=True))
    scores_t = jnp.einsum('qhd,khd->hqk', queries_t.astype(jnp.float32), keys.astype(jnp.float32))
    scores_t = (scores_t + jnp.einsum('qhd,khd->hqk', queries.astype(jnp.float32), keys_t.astype(jnp.float32))) * score_scale
    probs_t = probs * (scores_t - lax.optimization_barrier(jnp.sum(probs * scores_t, -1, keepdims=True)))
    probs_b = probs.astype(jnp.bfloat16).astype(jnp.float32)
    probs_tb = probs_t.astype(jnp.bfloat16).astype(jnp.float32)
    attended = jnp.einsum('hqk,khd->qhd', probs_b, values.astype(jnp.float32)).astype(jnp.bfloat16)
    attended_t = jnp.einsum('hqk,khd->qhd', probs_b, values_t.astype(jnp.float32))
    attended_t = (attended_t + jnp.einsum('hqk,khd->qhd', probs_tb, values.astype(jnp.float32))).astype(jnp.bfloat16)
    return (attended, attended_t)

def reference(latent, probe, norm_gain, w_query, w_key, w_value, w_out, tile_mask):
    tangent = probe.astype(jnp.float32)
    latent_f = latent.astype(jnp.float32)
    inverse = lax.rsqrt(lax.optimization_barrier(jnp.sum(latent_f * latent_f, -1, keepdims=True)) / D + 1e-06)
    along = lax.optimization_barrier(jnp.sum(latent_f * tangent, -1, keepdims=True)) / D
    normed = (latent_f * inverse * norm_gain).astype(jnp.bfloat16)
    normed_t = ((tangent * inverse - latent_f * inverse ** 3 * along) * norm_gain).astype(jnp.bfloat16)

    def project(weight):
        first = jnp.dot(normed, weight, preferred_element_type=jnp.float32).astype(jnp.bfloat16)
        second = jnp.dot(normed_t, weight, preferred_element_type=jnp.float32).astype(jnp.bfloat16)
        return (first.reshape(TOKENS, HEADS, HD), second.reshape(TOKENS, HEADS, HD))
    query, query_t = project(w_query)
    key_all, key_t = project(w_key)
    value_all, value_t = project(w_value)

    def padded(field):
        return jnp.pad(field, ((TOK_DEV, TOK_DEV), (0, 0), (0, 0)))
    key_pad, key_t_pad = (padded(key_all), padded(key_t))
    value_pad, value_t_pad = (padded(value_all), padded(value_t))
    mask_pad = jnp.pad(tile_mask, TILES_DEV)

    def shard_attend(shard):
        first = shard * TOK_DEV
        queries = lax.dynamic_slice_in_dim(query, first, TOK_DEV, 0)
        queries_t = lax.dynamic_slice_in_dim(query_t, first, TOK_DEV, 0)
        keys = lax.dynamic_slice_in_dim(key_pad, first, 3 * TOK_DEV, 0)
        keys_t = lax.dynamic_slice_in_dim(key_t_pad, first, 3 * TOK_DEV, 0)
        values = lax.dynamic_slice_in_dim(value_pad, first, 3 * TOK_DEV, 0)
        values_t = lax.dynamic_slice_in_dim(value_t_pad, first, 3 * TOK_DEV, 0)
        tile_rows = lax.dynamic_slice(mask_pad, (shard * TILES_DEV + TILES_DEV, shard * TILES_DEV), (TILES_DEV, 3 * TILES_DEV))
        allowed = jnp.repeat(jnp.repeat(tile_rows, TILE, 0), TILE, 1) == 1
        return attend_block(queries, queries_t, keys, values, keys_t, values_t, allowed)
    attended, attended_t = lax.map(shard_attend, jnp.arange(N_CTX, dtype=jnp.int32))
    attended = attended.reshape(TOKENS, HEADS * HD)
    attended_t = attended_t.reshape(TOKENS, HEADS * HD)
    group = HEADS * HD // N_HEAD
    branch = jnp.zeros((TOKENS, D), jnp.float32)
    branch_t = jnp.zeros((TOKENS, D), jnp.float32)
    for member in range(N_HEAD):
        rows_out = w_out[member * group:(member + 1) * group]
        part_one = jnp.dot(attended[:, member * group:(member + 1) * group], rows_out, preferred_element_type=jnp.float32)
        part_two = jnp.dot(attended_t[:, member * group:(member + 1) * group], rows_out, preferred_element_type=jnp.float32)
        part_one = lax.optimization_barrier(part_one.astype(jnp.bfloat16))
        part_two = lax.optimization_barrier(part_two.astype(jnp.bfloat16))
        branch = branch + part_one.astype(jnp.float32)
        branch_t = branch_t + part_two.astype(jnp.float32)
    mixed = (latent_f + branch).astype(jnp.bfloat16)
    trace_terms = lax.optimization_barrier(jnp.sum(tangent * branch_t, -1))
    return (mixed, branch_t.astype(jnp.bfloat16), trace_terms)
```

```python
import functools

import jax
import jax.numpy as jnp
from jax import lax
from jax.experimental import pallas as pl
from jax.experimental.pallas import tpu as pltpu
from jax.sharding import PartitionSpec as P

D = 5120
HD = 128
TILE = 128
MESH = pl.DeviceIdType.MESH
MIB = 1 << 20


def chip_of(pos, chips):
    half = pos // (chips // 2)
    return (1 - half) * 2 * pos + half * (2 * (chips - 1 - pos) + 1)


def project_kernel(
    n, heads, lat_ref, probe_ref, gain_ref, w_ref,
    qkv_ref, wo_ref, proj_ref, halo_ref,
    lat_all, x_ref, wbuf, obuf,
    local_sem, ring_send, ring_recv, flip_send, flip_recv, own_send, own_recv,
    lat_send, lat_recv, lat_local, load_sem, store_sem, halo_send, halo_recv, halo_local,
):
    chips = n // 2
    hops = chips - 1
    tok, own = lat_ref.shape
    cols = proj_ref.shape[-1]
    width = wbuf.shape[-1]
    pieces = cols // width
    me = lax.axis_index("ctx")
    head = lax.axis_index("head")
    core = me % 2
    chip = me // 2
    cx = chip % 2
    cz = chip // 2
    pos = (1 - cx) * cz + cx * (chips - 1 - cz)
    ahead = chip_of((pos + 1) % chips, chips) * 2 + core
    behind = chip_of((pos + chips - 1) % chips, chips) * 2 + core
    twin = me + 1 - 2 * core
    right = (me + 1) % n
    left = (me + n - 1) % n

    barrier = pltpu.get_barrier_semaphore()
    for other in (ahead, behind, twin, right, left):
        pl.semaphore_signal(barrier, inc=1, device_id={"ctx": other}, device_id_type=MESH)
    for k in range(1, heads):
        pl.semaphore_signal(
            barrier, inc=1, device_id={"head": (head + k) % heads}, device_id_type=MESH
        )

    def full(w):
        return wo_ref if w == 3 else qkv_ref.at[w]

    def local_copy(w):
        return pltpu.make_async_copy(w_ref.at[w], full(w).at[me], local_sem.at[w])

    for w in range(4):
        local_copy(w).start()
    mine = pltpu.make_async_copy(lat_ref, lat_all.at[head], lat_local)
    mine.start()
    pl.semaphore_wait(barrier, 5 + heads - 1)

    def ring(w, hop, way, first=False):
        source = (pos + chips - hop) % chips if way == 0 else (pos + hop) % chips
        owner = chip_of(source, chips) * 2 + core
        block = full(w).at[owner, way]
        return pltpu.make_async_remote_copy(
            src_ref=w_ref.at[w, way] if first else block, dst_ref=block,
            send_sem=ring_send.at[w, hop, way], recv_sem=ring_recv.at[w, hop, way],
            device_id={"ctx": ahead if way == 0 else behind}, device_id_type=MESH,
        )

    def arrived(w, hop, way):
        source = (pos + chips - hop - 1) % chips if way == 0 else (pos + hop + 1) % chips
        return full(w).at[chip_of(source, chips) * 2 + core, way]

    def ring_wait(w, hop, way):
        block = arrived(w, hop, way)
        pltpu.make_async_remote_copy(
            src_ref=block, dst_ref=block,
            send_sem=ring_send.at[w, hop, way], recv_sem=ring_recv.at[w, hop, way],
            device_id={"ctx": ahead if way == 0 else behind}, device_id_type=MESH,
        ).wait_recv()

    def flip(w, hop, way):
        block = arrived(w, hop, way)
        return pltpu.make_async_remote_copy(
            src_ref=block, dst_ref=block,
            send_sem=flip_send.at[w, hop, way], recv_sem=flip_recv.at[w, hop, way],
            device_id={"ctx": twin}, device_id_type=MESH,
        )

    def flip_wait(w, hop, way):
        source = (pos + chips - hop - 1) % chips if way == 0 else (pos + hop + 1) % chips
        block = full(w).at[chip_of(source, chips) * 2 + 1 - core, way]
        pltpu.make_async_remote_copy(
            src_ref=block, dst_ref=block,
            send_sem=flip_send.at[w, hop, way], recv_sem=flip_recv.at[w, hop, way],
            device_id={"ctx": twin}, device_id_type=MESH,
        ).wait_recv()

    def own_flip(w, who):
        return pltpu.make_async_remote_copy(
            src_ref=w_ref.at[w], dst_ref=full(w).at[who],
            send_sem=own_send.at[w], recv_sem=own_recv.at[w],
            device_id={"ctx": twin}, device_id_type=MESH,
        )

    def begin(w):
        ring(w, 0, 0, True).start()
        ring(w, 0, 1, True).start()
        own_flip(w, me).start()

    def advance(w, hop):
        for way in range(2):
            ring_wait(w, hop - 1, way)
            ring(w, hop, way).start()
            flip(w, hop - 1, way).start()

    def finish(w):
        for way in range(2):
            ring_wait(w, hops - 1, way)
            flip(w, hops - 1, way).start()

    def settle(w):
        local_copy(w).wait()
        own_flip(w, twin).wait_recv()

        @pl.loop(0, hops)
        def _(hop):
            for way in range(2):
                flip_wait(w, hop, way)

    def drain(w):
        own_flip(w, me).wait_send()

        @pl.loop(0, hops)
        def _(hop):
            for way in range(2):
                ring(w, hop, way).wait_send()
                flip(w, hop, way).wait_send()

    def lat_copy(k):
        return pltpu.make_async_remote_copy(
            src_ref=lat_ref, dst_ref=lat_all.at[head],
            send_sem=lat_send.at[k - 1], recv_sem=lat_recv.at[k - 1],
            device_id={"head": (head + k) % heads}, device_id_type=MESH,
        )

    def norm():
        mine.wait()
        for k in range(1, heads):
            came = lat_all.at[(head + heads - k) % heads]
            pltpu.make_async_remote_copy(
                src_ref=lat_ref, dst_ref=came,
                send_sem=lat_send.at[k - 1], recv_sem=lat_recv.at[k - 1],
                device_id={"head": (head + k) % heads}, device_id_type=MESH,
            ).wait_recv()
        step = 16

        @pl.loop(0, tok // step)
        def _(i):
            rows = pl.ds(pl.multiple_of(i * step, step), step)
            squares = jnp.zeros((step, 1), jnp.float32)
            crossed = jnp.zeros((step, 1), jnp.float32)
            for h in range(heads):
                part = lat_all[h, rows, :].astype(jnp.float32)
                tang = probe_ref[rows, h * own:(h + 1) * own].astype(jnp.float32)
                squares = squares + jnp.sum(part * part, -1, keepdims=True)
                crossed = crossed + jnp.sum(part * tang, -1, keepdims=True)
            inverse = lax.rsqrt(squares / D + 1e-06)
            along = crossed / D
            second = inverse * inverse * inverse * along
            rows_t = pl.ds(pl.multiple_of(tok + i * step, step), step)
            for h in range(heads):
                part = lat_all[h, rows, :].astype(jnp.float32)
                tang = probe_ref[rows, h * own:(h + 1) * own].astype(jnp.float32)
                gain = gain_ref[:, h * own:(h + 1) * own]
                x_ref[rows, h * own:(h + 1) * own] = (part * inverse * gain).astype(jnp.bfloat16)
                x_ref[rows_t, h * own:(h + 1) * own] = (
                    (tang * inverse - part * second) * gain
                ).astype(jnp.bfloat16)

    def load(w, piece, slot):
        at = pl.ds(pl.multiple_of(piece * width, width), width)
        return pltpu.make_async_copy(
            qkv_ref.at[w, :, :, :, at], wbuf.at[slot], load_sem.at[slot]
        )

    def multiply(w, piece, slot):
        load(w, piece, slot).wait()
        weight = wbuf[slot].reshape(D, width)
        rows = 128

        @pl.loop(0, 2 * tok // rows)
        def _(i):
            at = pl.ds(pl.multiple_of(i * rows, rows), rows)
            obuf[slot, at, :] = jnp.dot(
                x_ref[at, :], weight, preferred_element_type=jnp.float32
            ).astype(jnp.bfloat16)

        at = pl.ds(pl.multiple_of(piece * width, width), width)
        store = pltpu.make_async_copy(
            obuf.at[slot], proj_ref.at[w, :, at], store_sem.at[slot]
        )
        store.start()
        store.wait()

    def fetch(q, slot):
        @pl.when(q < 2 * pieces)
        def _():
            load(q // pieces, q % pieces, slot).start()

    def work(q, slot):
        @pl.when(q < 2 * pieces)
        def _():
            multiply(q // pieces, q % pieces, slot)

    def halo(side, a):
        return pltpu.make_async_remote_copy(
            src_ref=proj_ref.at[a], dst_ref=halo_ref.at[side, a],
            send_sem=halo_send.at[side, a], recv_sem=halo_recv.at[side, a],
            device_id={"ctx": right if side == 0 else left}, device_id_type=MESH,
        )

    def halo_fill(side, a):
        return pltpu.make_async_copy(proj_ref.at[a], halo_ref.at[side, a], halo_local.at[a])

    def halo_start(a):
        @pl.when(me < n - 1)
        def _():
            halo(0, a).start()

        @pl.when(me > 0)
        def _():
            halo(1, a).start()

        @pl.when(me == 0)
        def _():
            halo_fill(0, a).start()

        @pl.when(me == n - 1)
        def _():
            halo_fill(1, a).start()

    def halo_end(a):
        @pl.when(me < n - 1)
        def _():
            halo(0, a).wait_send()
            halo(1, a).wait_recv()

        @pl.when(me > 0)
        def _():
            halo(1, a).wait_send()
            halo(0, a).wait_recv()

        @pl.when(me == 0)
        def _():
            halo_fill(0, a).wait()

        @pl.when(me == n - 1)
        def _():
            halo_fill(1, a).wait()

    begin(0)
    begin(1)
    for k in range(1, heads):
        lat_copy(k).start()

    @pl.loop(1, hops)
    def _(hop):
        advance(0, hop)
        advance(1, hop)

        @pl.when(hop == hops - 1)
        def _():
            norm()

    begin(2)
    begin(3)
    finish(0)
    finish(1)
    settle(0)
    settle(1)

    @pl.loop(1, hops)
    def _(hop):
        q = (hop - 1) * 4
        fetch(q, 0)
        fetch(q + 1, 1)
        advance(2, hop)
        work(q, 0)
        fetch(q + 2, 0)
        work(q + 1, 1)
        fetch(q + 3, 1)
        advance(3, hop)
        work(q + 2, 0)
        work(q + 3, 1)
        for a in range(2):

            @pl.when(hop == -(-(a + 1) * pieces // 4))
            def _(a=a):
                halo_start(a)

    finish(2)
    finish(3)
    settle(2)

    load(2, 0, 0).start()
    for piece in range(pieces):
        if piece + 1 < pieces:
            load(2, piece + 1, (piece + 1) % 2).start()
        multiply(2, piece, piece % 2)

    settle(3)
    halo_end(0)
    halo_end(1)
    for w in range(4):
        drain(w)
    for k in range(1, heads):
        lat_copy(k).wait_send()


def gather_and_project(latent, probe, gain, weights):
    n = lax.axis_size("ctx")
    heads = lax.axis_size("head")
    hops = n // 2 - 1
    tok, own = latent.shape
    rows, cols = weights.shape[1:]
    weights = weights.reshape(4, 2, rows // 2, cols)
    width = 256 if cols % 256 == 0 else 128
    dma = pltpu.SemaphoreType.DMA
    bf = jnp.bfloat16
    vmem = pl.BlockSpec(memory_space=pltpu.VMEM)
    anywhere = pl.BlockSpec(memory_space=pl.ANY)
    return pl.pallas_call(
        functools.partial(project_kernel, n, heads),
        out_shape=(
            jax.ShapeDtypeStruct((3, n, 2, rows // 2, cols), bf),
            jax.ShapeDtypeStruct((n, 2, rows // 2, cols), bf),
            jax.ShapeDtypeStruct((3, 2 * tok, cols), bf),
            jax.ShapeDtypeStruct((2, 2, 2 * tok, cols), bf),
        ),
        in_specs=[vmem, vmem, vmem, anywhere],
        out_specs=(anywhere,) * 4,
        scratch_shapes=[
            pltpu.VMEM((heads, tok, own), bf),
            pltpu.VMEM((2 * tok, D), bf),
            pltpu.VMEM((2, n, 2, rows // 2, width), bf),
            pltpu.VMEM((2, 2 * tok, width), bf),
            dma((4,)), dma((4, hops, 2)), dma((4, hops, 2)), dma((4, hops, 2)), dma((4, hops, 2)),
            dma((4,)), dma((4,)),
            dma((heads - 1,)), dma((heads - 1,)), dma, dma((2,)), dma((2,)),
            dma((2, 2)), dma((2, 2)), dma((2,)),
        ],
        compiler_params=pltpu.CompilerParams(
            collective_id=0, has_side_effects=True, vmem_limit_bytes=48 * MIB
        ),
    )(latent, probe, gain, weights)


def attend_kernel(tiles, mask_ref, q_ref, own_ref, low_ref, high_ref, out_ref, k_all, v_all):
    tok = tiles * TILE
    scale = HD ** (-0.5)
    for place, ref in enumerate((low_ref, own_ref, high_ref)):
        at = slice(place * tok, (place + 1) * tok)
        k_all[at, :HD] = ref[0, :tok, :]
        k_all[at, HD:] = ref[0, tok:, :]
        v_all[at, :HD] = ref[1, :tok, :]
        v_all[at, HD:] = ref[1, tok:, :]
    contract = (((1,), (1,)), ((), ()))
    band = 2 * tiles + 1
    for i in range(tiles):
        rows = slice(i * TILE, (i + 1) * TILE)
        rows_t = slice(tok + i * TILE, tok + (i + 1) * TILE)
        query = q_ref[0, rows, :]
        query_t = q_ref[0, rows_t, :]
        keys = k_all[i * TILE:(i + band) * TILE, :]
        scores = lax.dot_general(
            query, keys[:, :HD], contract, preferred_element_type=jnp.float32
        ) * scale
        scores_t = lax.dot_general(
            jnp.concatenate([query_t, query], 1), keys, contract,
            preferred_element_type=jnp.float32,
        ) * scale
        masked = jnp.concatenate(
            [
                jnp.where(
                    mask_ref[i, i + j] == 1, scores[:, j * TILE:(j + 1) * TILE], -1e30
                )
                for j in range(band)
            ],
            1,
        )
        highest = jnp.max(masked, -1, keepdims=True)
        expos = jnp.exp(masked - highest)
        probs = expos * (1.0 / jnp.sum(expos, -1, keepdims=True))
        weighed = probs * scores_t
        probs_t = weighed - probs * jnp.sum(weighed, -1, keepdims=True)
        probs_b = probs.astype(jnp.bfloat16)
        values = v_all[i * TILE:(i + band) * TILE, :]
        first = jnp.dot(probs_b, values, preferred_element_type=jnp.float32)
        second = first[:, HD:] + jnp.dot(
            probs_t.astype(jnp.bfloat16), values[:, :HD], preferred_element_type=jnp.float32
        )
        out_ref[rows, :] = first[:, :HD].astype(jnp.bfloat16)
        out_ref[rows_t, :] = second.astype(jnp.bfloat16)


def attend(tile_rows, proj, halo):
    rows, cols = proj.shape[1:]
    tok = rows // 2
    tiles = tok // TILE
    return pl.pallas_call(
        functools.partial(attend_kernel, tiles),
        grid=(cols // HD,),
        out_shape=jax.ShapeDtypeStruct((rows, cols), jnp.bfloat16),
        in_specs=[
            pl.BlockSpec(memory_space=pltpu.SMEM),
            pl.BlockSpec((1, rows, HD), lambda h: (2, 0, h)),
            pl.BlockSpec((2, rows, HD), lambda h: (0, 0, h)),
            pl.BlockSpec((None, 2, rows, HD), lambda h: (0, 0, 0, h)),
            pl.BlockSpec((None, 2, rows, HD), lambda h: (1, 0, 0, h)),
        ],
        out_specs=pl.BlockSpec((rows, HD), lambda h: (0, h)),
        scratch_shapes=[pltpu.VMEM((3 * tok, 2 * HD), jnp.bfloat16)] * 2,
        compiler_params=pltpu.CompilerParams(vmem_limit_bytes=32 * MIB),
    )(tile_rows, proj, proj, halo, halo)


def shards(latent, probe, norm_gain, w_query, w_key, w_value, w_out, tile_mask):
    tok_rows, own_cols = latent.shape
    weights = jnp.stack([w_key, w_value, w_query, w_out.T])
    _, wo_full, proj, halo = gather_and_project(latent, probe, norm_gain.reshape(1, D), weights)
    tiles_dev = tok_rows // TILE
    ctx_slot = lax.axis_index("ctx")
    mask_pad = jnp.pad(tile_mask, tiles_dev)
    tile_rows = lax.dynamic_slice(
        mask_pad,
        (ctx_slot * tiles_dev + tiles_dev, ctx_slot * tiles_dev),
        (tiles_dev, 3 * tiles_dev),
    )
    both_rows = attend(tile_rows, proj, halo)
    w_out_t = wo_full.reshape(D, w_out.shape[0])
    terms = lax.dot_general(
        both_rows, w_out_t, (((1,), (1,)), ((), ())), preferred_element_type=jnp.float32
    ).astype(jnp.bfloat16)
    summed = lax.psum_scatter(terms, "head", scatter_dimension=1, tiled=True).astype(jnp.float32)
    branch = summed[:tok_rows]
    branch_t = summed[tok_rows:]
    latent_f = latent.astype(jnp.float32)
    col_start = lax.axis_index("head") * own_cols
    tangent_own = lax.dynamic_slice_in_dim(probe, col_start, own_cols, 1).astype(jnp.float32)
    mixed = (latent_f + branch).astype(jnp.bfloat16)
    trace_terms = lax.psum(jnp.sum(tangent_own * branch_t, -1), "head")
    return (mixed, branch_t.astype(jnp.bfloat16), trace_terms)


def layer_kernel(
    layers, mask_ref, lat_ref, probe_ref, gain_ref, wk_ref, wv_ref, wq_ref, wo_ref,
    att_ref, ofull_ref, oz_ref,
    x_all, w_all, k_all, v_all, q_all, a_all, sums, sums_in,
    in_sem, a2a_send, a2a_recv, a2a_local, z_send, z_recv, s_send, s_recv,
    n_send, n_recv, d_send, d_recv, f_send, f_recv, h_send, h_recv,
    at_send, at_recv, at_local, o_send, o_recv, o_local, of_send, of_recv,
):
    tok, own = lat_ref.shape
    cols = w_all.shape[-1]
    nheads = cols // HD
    half = wo_ref.shape[0] // 2
    me = lax.axis_index("ctx")
    y = lax.axis_index("head")
    z = me // 4
    x = (me // 2) % 2
    c = me % 2
    base = z * 4
    q = 2 * x + c
    tq = 2 * x + 1 - c
    xq = 2 * (1 - x) + c
    dq = 2 * (1 - x) + 1 - c
    weights = (wk_ref, wv_ref, wq_ref)
    bf = jnp.bfloat16

    def at(ctx, head):
        return {"ctx": ctx, "head": head}

    barrier = pltpu.get_barrier_semaphore()
    for k in range(4):
        for j in range(2):
            if k or j:
                pl.semaphore_signal(
                    barrier, inc=1, device_id=at(base + (q + k) % 4, (y + j) % 2),
                    device_id_type=MESH,
                )

    @pl.when(z < layers - 1)
    def _():
        pl.semaphore_signal(barrier, inc=1, device_id=at(me + 4, y), device_id_type=MESH)

    @pl.when(z > 0)
    def _():
        pl.semaphore_signal(barrier, inc=1, device_id=at(me - 4, y), device_id_type=MESH)

    def load_in(p):
        if p == 0:
            source = lat_ref
        else:
            source = probe_ref.at[:, pl.ds(pl.multiple_of(y * own, own), own)]
        return pltpu.make_async_copy(
            source, x_all.at[q, y, pl.ds(p * tok, tok)], in_sem.at[p]
        )

    load_in(0).start()
    load_in(1).start()

    def quarter(w, k):
        return weights[w].at[:, pl.ds(pl.multiple_of(k * cols, cols), cols)]

    def a2a_own(w):
        return pltpu.make_async_copy(quarter(w, q), w_all.at[w, z, q], a2a_local.at[w])

    def a2a(w, k):
        to = (q + k) % 4
        return pltpu.make_async_remote_copy(
            src_ref=quarter(w, to), dst_ref=w_all.at[w, z, q],
            send_sem=a2a_send.at[w, k - 1], recv_sem=a2a_recv.at[w, k - 1],
            device_id=at(base + to, y), device_id_type=MESH,
        )

    def a2a_start(w):
        a2a_own(w).start()
        for k in (2, 1, 3):
            a2a(w, k).start()

    def a2a_wait(w):
        a2a_own(w).wait()
        for k in (1, 2, 3):
            came = w_all.at[w, z, (q + 4 - k) % 4]
            pltpu.make_async_remote_copy(
                src_ref=came, dst_ref=came,
                send_sem=a2a_send.at[w, k - 1], recv_sem=a2a_recv.at[w, k - 1],
                device_id=at(base + (q + k) % 4, y), device_id_type=MESH,
            ).wait_recv()

    def region(item, zz):
        if item < 3:
            return w_all.at[item, zz]
        return oz_ref.at[zz, item - 3]

    def z_copy(item, way, d):
        zz = z - d if way == 0 else z + d
        block = region(item, zz)
        source = wo_ref.at[pl.ds((item - 3) * half, half)] if item >= 3 and d == 0 else block
        return pltpu.make_async_remote_copy(
            src_ref=source, dst_ref=block,
            send_sem=z_send.at[item, way, d], recv_sem=z_recv.at[item, way, d],
            device_id=at(me + 4 if way == 0 else me - 4, y), device_id_type=MESH,
        )

    def z_has(way, d):
        return z >= d if way == 0 else z + d <= layers - 1

    def z_sends(way, d):
        if way == 0:
            return jnp.logical_and(z >= d, z < layers - 1)
        return jnp.logical_and(z + d <= layers - 1, z > 0)

    def z_begin(item):
        for way in range(2):

            @pl.when(z_sends(way, 0))
            def _(way=way):
                z_copy(item, way, 0).start()

    def z_relay(item, d):
        for way in range(2):

            @pl.when(z_has(way, d))
            def _(way=way):
                zz = z - d if way == 0 else z + d
                block = region(item, zz)
                pltpu.make_async_remote_copy(
                    src_ref=block, dst_ref=block,
                    send_sem=z_send.at[item, way, d - 1], recv_sem=z_recv.at[item, way, d - 1],
                    device_id=at(me + 4 if way == 0 else me - 4, y), device_id_type=MESH,
                ).wait_recv()

            if d < layers - 1:

                @pl.when(z_sends(way, d))
                def _(way=way):
                    z_copy(item, way, d).start()

    def z_drain(item):
        for way in range(2):
            for d in range(layers - 1):

                @pl.when(z_sends(way, d))
                def _(way=way, d=d):
                    z_copy(item, way, d).wait_send()

    def part(slot, side, p):
        return x_all.at[slot, side, pl.ds(p * tok, tok)]

    twin = at(base + tq, y)
    across = at(base + xq, y)
    over = at(me, 1 - y)

    def n_copy(way, p, slot=None, side=None):
        block = part(q, y, p) if slot is None else part(slot, side, p)
        return pltpu.make_async_remote_copy(
            src_ref=block, dst_ref=block,
            send_sem=n_send.at[way, p], recv_sem=n_recv.at[way, p],
            device_id=(twin, across, over)[way], device_id_type=MESH,
        )

    def d_copy(p, landing=False):
        if landing:
            block = part(xq, 1 - y, p)
        else:
            block = part(xq, y, p) if p == 0 else part(q, 1 - y, p)
        return pltpu.make_async_remote_copy(
            src_ref=block, dst_ref=block,
            send_sem=d_send.at[p], recv_sem=d_recv.at[p],
            device_id=over if p == 0 else across, device_id_type=MESH,
        )

    def f_copy(kind, p, landing=False):
        if landing:
            block = (part(dq, y, p), part(tq, 1 - y, p), part(dq, 1 - y, p))[kind]
        else:
            block = (part(xq, y, p), part(q, 1 - y, p), part(xq, 1 - y, p))[kind]
        return pltpu.make_async_remote_copy(
            src_ref=block, dst_ref=block,
            send_sem=f_send.at[kind, p], recv_sem=f_recv.at[kind, p],
            device_id=twin, device_id_type=MESH,
        )

    def s_copy():
        return pltpu.make_async_remote_copy(
            src_ref=sums, dst_ref=sums_in, send_sem=s_send, recv_sem=s_recv,
            device_id=over, device_id_type=MESH,
        )

    step = 16

    def norm_sums():
        @pl.loop(0, tok // step)
        def _(i):
            rows = pl.ds(pl.multiple_of(i * step, step), step)
            rows_t = pl.ds(pl.multiple_of(tok + i * step, step), step)
            lat = x_all[q, y, rows, :].astype(jnp.float32)
            tang = x_all[q, y, rows_t, :].astype(jnp.float32)
            squares = jnp.sum(lat * lat, -1, keepdims=True)
            crossed = jnp.sum(lat * tang, -1, keepdims=True)
            lane = lax.broadcasted_iota(jnp.int32, (step, HD), 1)
            sums[rows, :] = jnp.where(lane < HD // 2, squares, crossed)

    def norm_apply():
        @pl.loop(0, tok // step)
        def _(i):
            rows = pl.ds(pl.multiple_of(i * step, step), step)
            rows_t = pl.ds(pl.multiple_of(tok + i * step, step), step)
            both = sums[rows, :] + sums_in[rows, :]
            inverse = lax.rsqrt(both[:, 0:1] / D + 1e-06)
            along = both[:, HD // 2:HD // 2 + 1] / D
            second = inverse * inverse * inverse * along
            lat = x_all[q, y, rows, :].astype(jnp.float32)
            tang = x_all[q, y, rows_t, :].astype(jnp.float32)
            gain = gain_ref[y]
            x_all[q, y, rows, :] = (lat * inverse * gain).astype(bf)
            x_all[q, y, rows_t, :] = ((tang * inverse - lat * second) * gain).astype(bf)

    def project(w, blk):
        into, first = ((k_all, tok), (v_all, tok), (q_all, 0))[w]
        for p in range(2):
            acc = None
            for side in range(2):
                weight = w_all[w, side * (layers // 2):(side + 1) * (layers // 2)]
                term = jnp.dot(
                    x_all[blk, side, p * tok:(p + 1) * tok, :], weight.reshape(own, cols),
                    preferred_element_type=jnp.float32,
                )
                acc = term if acc is None else acc + term
            res = acc.astype(bf)
            rows = pl.ds(pl.multiple_of(blk * tok + first, tok), tok)
            for h in range(nheads):
                lanes = slice((2 * h + p) * HD, (2 * h + p + 1) * HD)
                into[rows, lanes] = res[:, h * HD:(h + 1) * HD]

    kv = (k_all, v_all)

    def halo(way, a, landing=False):
        if way == 0:
            source = pl.ds(4 * tok, tok)
            target = pl.ds(0, tok)
        else:
            source = pl.ds(tok, tok)
            target = pl.ds(5 * tok, tok)
        return pltpu.make_async_remote_copy(
            src_ref=kv[a].at[target if landing else source], dst_ref=kv[a].at[target],
            send_sem=h_send.at[way, a], recv_sem=h_recv.at[way, a],
            device_id=at(me + 4 if way == 0 else me - 4, y), device_id_type=MESH,
        )

    def halo_start(a):
        @pl.when(z < layers - 1)
        def _():
            halo(0, a).start()

        @pl.when(z > 0)
        def _():
            halo(1, a).start()

    def halo_wait(a):
        @pl.when(z > 0)
        def _():
            halo(0, a, True).wait_recv()

        @pl.when(z < layers - 1)
        def _():
            halo(1, a, True).wait_recv()

    def halo_fill():
        @pl.when(z == 0)
        def _():
            for a in range(2):
                kv[a][0:tok, :] = jnp.zeros((tok, 2 * cols), bf)

        @pl.when(z == layers - 1)
        def _():
            for a in range(2):
                kv[a][5 * tok:6 * tok, :] = jnp.zeros((tok, 2 * cols), bf)

    def halo_drain(a):
        @pl.when(z < layers - 1)
        def _():
            halo(0, a).wait_send()

        @pl.when(z > 0)
        def _():
            halo(1, a).wait_send()

    tiles = tok // TILE
    band = 2 * tiles + 1
    scale = HD ** (-0.5)
    contract = (((1,), (1,)), ((), ()))

    def attend_tile(blk, i):
        tile = blk * tiles + i
        rows = pl.ds(pl.multiple_of(tile * TILE, TILE), TILE)
        span = pl.ds(pl.multiple_of(tile * TILE, TILE), band * TILE)
        bias = [
            (mask_ref[tile, tile + j] - 1).astype(jnp.float32) * 1e30 for j in range(band)
        ]
        for h in range(nheads):
            lanes = slice(2 * h * HD, 2 * (h + 1) * HD)
            query = q_all[rows, lanes]
            keys = k_all[span, lanes]
            left = jnp.concatenate(
                [
                    jnp.concatenate([query[:, :HD], query[:, HD:]], 0),
                    jnp.concatenate([jnp.zeros((TILE, HD), bf), query[:, :HD]], 0),
                ],
                1,
            )
            scores = lax.dot_general(left, keys, contract, preferred_element_type=jnp.float32)
            masked = jnp.concatenate(
                [
                    scores[:TILE, j * TILE:(j + 1) * TILE] * scale + bias[j]
                    for j in range(band)
                ],
                1,
            )
            highest = jnp.max(masked, -1, keepdims=True)
            expos = jnp.exp(masked - highest)
            probs = expos * (1.0 / jnp.sum(expos, -1, keepdims=True))
            weighed = probs * (scores[TILE:] * scale)
            probs_t = weighed - probs * jnp.sum(weighed, -1, keepdims=True)
            stacked = jnp.concatenate([probs.astype(bf), probs_t.astype(bf)], 0)
            out = jnp.dot(stacked, v_all[span, lanes], preferred_element_type=jnp.float32)
            at_h = slice(h * HD, (h + 1) * HD)
            a_all[blk, 0, pl.ds(pl.multiple_of(i * TILE, TILE), TILE), at_h] = (
                out[:TILE, :HD].astype(bf)
            )
            a_all[blk, 1, pl.ds(pl.multiple_of(i * TILE, TILE), TILE), at_h] = (
                (out[:TILE, HD:] + out[TILE:, :HD]).astype(bf)
            )

    def attend_block(blk):
        @pl.loop(0, tiles)
        def _(i):
            attend_tile(blk, i)

    def att_slot(head, slot):
        return att_ref.at[head, :, :, pl.ds(pl.multiple_of(slot * cols, cols), cols)]

    def att_copy(k, j):
        blk = (q + k) % 4
        return pltpu.make_async_remote_copy(
            src_ref=a_all.at[blk], dst_ref=att_slot(y, q),
            send_sem=at_send.at[k, j], recv_sem=at_recv.at[k, j],
            device_id=at(base + blk, (y + j) % 2), device_id_type=MESH,
        )

    def att_own():
        return pltpu.make_async_copy(a_all.at[q], att_slot(y, q), at_local)

    def att_start(k):
        for j in (1, 0):
            if k or j:
                att_copy(k, j).start()
            else:
                att_own().start()

    def att_end():
        for k in range(4):
            for j in range(2):
                if k or j:
                    came = att_slot((y + j) % 2, (q + 4 - k) % 4)
                    pltpu.make_async_remote_copy(
                        src_ref=came, dst_ref=came,
                        send_sem=at_send.at[k, j], recv_sem=at_recv.at[k, j],
                        device_id=at(base + (q + k) % 4, (y + j) % 2), device_id_type=MESH,
                    ).wait_recv()
                    att_copy(k, j).wait_send()
        att_own().wait()

    per = layers // 2

    def o_slot(zz, xs, cs, ys, h):
        return ofull_ref.at[zz % per, xs, cs, ys, pl.ds(h * half, half)]

    def o_source(zz, own_block, h):
        return wo_ref.at[pl.ds(h * half, half)] if own_block else oz_ref.at[zz, h]

    def o_far(zz, own_block, h):
        goal = zz // per
        return pltpu.make_async_remote_copy(
            src_ref=o_source(zz, own_block, h), dst_ref=o_slot(zz, x, c, y, h),
            send_sem=o_send.at[zz, h, 0], recv_sem=o_recv.at[zz % per, h, 1, (y + goal) % 2],
            device_id=at(base + xq, goal), device_id_type=MESH,
        )

    def o_near(zz, own_block, h):
        return pltpu.make_async_remote_copy(
            src_ref=o_source(zz, own_block, h), dst_ref=o_slot(zz, x, c, y, h),
            send_sem=o_send.at[zz, h, 1], recv_sem=o_recv.at[zz % per, h, 0, 1],
            device_id=over, device_id_type=MESH,
        )

    def o_self(zz, own_block, h):
        return pltpu.make_async_copy(
            o_source(zz, own_block, h), o_slot(zz, x, c, y, h), o_local.at[zz % per, h]
        )

    def o_give(zz, own_block, h):
        o_far(zz, own_block, h).start()

        @pl.when(zz // per == y)
        def _():
            o_self(zz, own_block, h).start()

        @pl.when(zz // per != y)
        def _():
            o_near(zz, own_block, h).start()

    def o_give_dist(d):
        for h in range(2):
            for way in range(2 if d else 1):

                @pl.when(z_has(way, d))
                def _(way=way, h=h):
                    o_give(z - d if way == 0 else z + d, d == 0, h)

    def o_drain():
        for d in range(layers):
            for h in range(2):
                for way in range(2 if d else 1):

                    @pl.when(z_has(way, d))
                    def _(way=way, h=h, d=d):
                        zz = z - d if way == 0 else z + d
                        o_far(zz, d == 0, h).wait_send()

                        @pl.when(zz // per != y)
                        def _():
                            o_near(zz, d == 0, h).wait_send()

    def o_flip(zz, h, dx, dy, landing=False):
        xs = (x + dx) % 2
        ys = (y + dy) % 2
        block = o_slot(zz, xs, 1 - c if landing else c, ys, h)
        return pltpu.make_async_remote_copy(
            src_ref=block, dst_ref=block,
            send_sem=of_send.at[zz % per, h, dx, dy], recv_sem=of_recv.at[zz % per, h, dx, dy],
            device_id=twin, device_id_type=MESH,
        )

    def o_take(zz, h):
        for dx in range(2):
            for dy in range(2):
                if dx or dy:
                    came = o_slot(zz, (x + dx) % 2, c, (y + dy) % 2, h)
                    pltpu.make_async_remote_copy(
                        src_ref=came, dst_ref=came,
                        send_sem=o_send.at[zz, h, 0], recv_sem=o_recv.at[zz % per, h, dx, dy],
                        device_id=twin, device_id_type=MESH,
                    ).wait_recv()
                else:
                    o_self(zz, False, h).wait()
                o_flip(zz, h, dx, dy).start()

    def o_take_end(zz, h):
        for dx in range(2):
            for dy in range(2):
                o_flip(zz, h, dx, dy, True).wait_recv()
                o_flip(zz, h, dx, dy).wait_send()

    ends = (z == 0).astype(jnp.int32) + (z == layers - 1).astype(jnp.int32)
    pl.semaphore_wait(barrier, 9 - ends)

    a2a_start(0)
    z_begin(3)
    load_in(0).wait()
    load_in(1).wait()
    norm_sums()
    s_copy().start()
    halo_fill()
    s_copy().wait()
    norm_apply()
    for p in range(2):
        n_copy(1, p).start()
        n_copy(2, p).start()
        n_copy(0, p).start()
    a2a_start(1)
    a2a_wait(0)
    z_begin(0)
    z_begin(4)
    z_relay(0, 1)
    a2a_wait(1)
    z_begin(1)

    def x_came(p):
        n_copy(1, p, xq, y).wait_recv()
        if p == 0:
            d_copy(0).start()
        f_copy(0, p).start()
        n_copy(2, p, q, 1 - y).wait_recv()
        if p == 1:
            d_copy(1).start()
        f_copy(1, p).start()

    x_came(0)
    z_relay(0, 2)
    z_relay(0, 3)
    x_came(1)
    a2a_start(2)
    for p in range(2):
        n_copy(0, p, tq, y).wait_recv()
        f_copy(1, p, True).wait_recv()

    def project_pair(w, side):
        @pl.loop(0, 2)
        def _(j):
            project(w, 2 * side + j)

    z_relay(1, 1)
    project_pair(0, x)
    a2a_wait(2)
    z_begin(2)
    z_relay(1, 2)
    for p in range(2):
        d_copy(p, True).wait_recv()
        f_copy(2, p).start()
    o_give_dist(0)
    for p in range(2):
        f_copy(0, p, True).wait_recv()
        f_copy(2, p, True).wait_recv()
    project_pair(0, 1 - x)
    halo_start(0)
    z_relay(1, 3)
    project_pair(1, x)
    project_pair(1, 1 - x)
    halo_start(1)
    z_relay(2, 1)
    z_relay(3, 1)
    z_relay(4, 1)
    o_give_dist(1)
    z_relay(2, 2)
    halo_wait(0)
    halo_wait(1)
    z_relay(2, 3)
    for n, k in enumerate((3, 2, 1, 0)):
        blk = (q + k) % 4
        project(2, blk)
        attend_block(blk)
        att_start(k)
        if n == 1:
            z_relay(3, 2)
            z_relay(4, 2)
            o_give_dist(2)
    z_relay(3, 3)
    z_relay(4, 3)
    o_give_dist(3)
    near = jnp.where(z > per * y, per - 1, 0)
    for k in range(per):
        zz = per * y + jnp.where(z > per * y, per - 1 - k, k)
        for h in range(2):
            o_take(zz, h)
    att_end()
    for zz in range(per):
        for h in range(2):
            o_take_end(per * y + zz, h)
    s_done = None
    for w in range(3):
        for k in (1, 2, 3):
            a2a(w, k).wait_send()
    for item in range(5):
        z_drain(item)
    for p in range(2):
        for way in range(3):
            n_copy(way, p).wait_send()
        d_copy(p).wait_send()
        for kind in range(3):
            f_copy(kind, p).wait_send()
    halo_drain(0)
    halo_drain(1)
    o_drain()


def run_layers(mask_rows, latent, probe, gain, wk, wv, wq, wo):
    layers = lax.axis_size("ctx") // 4
    tok, own = latent.shape
    rows, width = wk.shape
    cols = width // 4
    half = rows // 2
    dma = pltpu.SemaphoreType.DMA
    bf = jnp.bfloat16
    vmem = pl.BlockSpec(memory_space=pltpu.VMEM)
    smem = pl.BlockSpec(memory_space=pltpu.SMEM)
    anywhere = pl.BlockSpec(memory_space=pl.ANY)
    return pl.pallas_call(
        functools.partial(layer_kernel, layers),
        out_shape=(
            jax.ShapeDtypeStruct((2, 2, tok, width), bf),
            jax.ShapeDtypeStruct((layers // 2, 2, 2, 2, rows, width), bf),
            jax.ShapeDtypeStruct((layers, 2, half, width), bf),
        ),
        in_specs=[smem, anywhere, anywhere, vmem] + [anywhere] * 4,
        out_specs=(anywhere,) * 3,
        scratch_shapes=[
            pltpu.VMEM((4, 2, 2 * tok, own), bf),
            pltpu.VMEM((3, layers, 4, rows, cols), bf),
            pltpu.VMEM((6 * tok, 2 * cols), bf),
            pltpu.VMEM((6 * tok, 2 * cols), bf),
            pltpu.VMEM((4 * tok, 2 * cols), bf),
            pltpu.VMEM((4, 2, tok, cols), bf),
            pltpu.VMEM((tok, HD), jnp.float32),
            pltpu.VMEM((tok, HD), jnp.float32),
            dma((2,)), dma((3, 3)), dma((3, 3)), dma((3,)),
            dma((5, 2, layers - 1)), dma((5, 2, layers - 1)), dma, dma,
            dma((3, 2)), dma((3, 2)), dma((2,)), dma((2,)), dma((3, 2)), dma((3, 2)),
            dma((2, 2)), dma((2, 2)),
            dma((4, 2)), dma((4, 2)), dma,
            dma((layers, 2, 2)), dma((layers // 2, 2, 2, 2)), dma((layers // 2, 2)),
            dma((layers // 2, 2, 2, 2)), dma((layers // 2, 2, 2, 2)),
        ],
        compiler_params=pltpu.CompilerParams(
            collective_id=0, has_side_effects=True, vmem_limit_bytes=60 * MIB
        ),
    )(mask_rows, latent, probe, gain, wk, wv, wq, wo)


def finish_kernel(head_ref, att_ref, o_ref, lat_ref, probe_ref, mixed_ref, tang_ref, trace_ref):
    tok, chunk = lat_ref.shape
    contract = (((1,), (1,)), ((), ()))
    branch = None
    for ys in range(2):
        weight = o_ref[:, ys].reshape(chunk, o_ref.shape[-1])
        lhs = att_ref[ys].reshape(2 * tok, att_ref.shape[-1])
        term = lax.dot_general(lhs, weight, contract, preferred_element_type=jnp.float32)
        term = term.astype(jnp.bfloat16).astype(jnp.float32)
        branch = term if branch is None else branch + term
    branch_t = branch[tok:]
    mixed_ref[...] = (lat_ref[...].astype(jnp.float32) + branch[:tok]).astype(jnp.bfloat16)
    tang_ref[...] = branch_t.astype(jnp.bfloat16)
    terms = jnp.sum(probe_ref[...].astype(jnp.float32) * branch_t, -1, keepdims=True)

    @pl.when(pl.program_id(0) == 0)
    def _():
        trace_ref[...] = jnp.zeros_like(trace_ref)

    trace_ref[...] += jnp.broadcast_to(terms, trace_ref.shape)


def finish(att, ofull, latent, probe):
    tok, own = latent.shape
    per, _, _, _, rows, width = ofull.shape
    steps = 2 * per
    chunk = own // steps
    blocks = ofull.reshape(steps, 2, 2, rows, width)
    return pl.pallas_call(
        finish_kernel,
        grid_spec=pltpu.PrefetchScalarGridSpec(
            num_scalar_prefetch=1,
            grid=(steps,),
            in_specs=[
                pl.BlockSpec((2, 2, tok, width), lambda i, h: (0, 0, 0, 0)),
                pl.BlockSpec((None, 2, 2, rows, width), lambda i, h: (i, 0, 0, 0, 0)),
                pl.BlockSpec((tok, chunk), lambda i, h: (0, i)),
                pl.BlockSpec((tok, chunk), lambda i, h: (0, h[0] * steps + i)),
            ],
            out_specs=[
                pl.BlockSpec((tok, chunk), lambda i, h: (0, i)),
                pl.BlockSpec((tok, chunk), lambda i, h: (0, i)),
                pl.BlockSpec((tok, HD), lambda i, h: (0, 0)),
            ],
        ),
        out_shape=(
            jax.ShapeDtypeStruct((tok, own), jnp.bfloat16),
            jax.ShapeDtypeStruct((tok, own), jnp.bfloat16),
            jax.ShapeDtypeStruct((tok, HD), jnp.float32),
        ),
        compiler_params=pltpu.CompilerParams(vmem_limit_bytes=48 * MIB),
    )(lax.axis_index("head").reshape(1), att, blocks, latent, probe)


def layer_shards(latent, probe, norm_gain, w_query, w_key, w_value, w_out, tile_mask):
    tok = latent.shape[0]
    tiles = tok // TILE
    layer_tiles = 4 * tiles
    layer = lax.axis_index("ctx") // 4
    mask_pad = jnp.pad(tile_mask, tiles)
    mask_rows = lax.dynamic_slice(
        mask_pad,
        (layer * layer_tiles + tiles, layer * layer_tiles),
        (layer_tiles, layer_tiles + 2 * tiles),
    )
    att, ofull, _ = run_layers(
        mask_rows, latent, probe, norm_gain.reshape(2, 1, D // 2),
        w_key, w_value, w_query, w_out.T,
    )
    mixed, tangent, trace = finish(att, ofull, latent, probe)
    return (mixed, tangent, lax.psum(trace[:, 0], "head"))


def solution(mesh):
    placed = (
        P("ctx", "head"),
        P("ctx", None),
        P(),
        P("ctx", "head"),
        P("ctx", "head"),
        P("ctx", "head"),
        P("head", "ctx"),
        P(),
    )
    by_layer = mesh.shape["ctx"] == 16 and mesh.shape["head"] == 2
    return jax.shard_map(
        layer_shards if by_layer else shards,
        mesh=mesh,
        in_specs=placed,
        out_specs=(P("ctx", "head"), P("ctx", "head"), P("ctx")),
        check_vma=False,
    )
```

```python
import functools

import jax
import jax.numpy as jnp
from jax import lax
from jax.experimental import pallas as pl
from jax.experimental.pallas import tpu as pltpu
from jax.sharding import PartitionSpec as P

D = 5120
HD = 128
TILE = 128
MESH = pl.DeviceIdType.MESH
MIB = 1 << 20


def chip_of(pos, chips):
    half = pos // (chips // 2)
    return (1 - half) * 2 * pos + half * (2 * (chips - 1 - pos) + 1)


def project_kernel(
    n, heads, lat_ref, probe_ref, gain_ref, w_ref,
    qkv_ref, wo_ref, proj_ref, halo_ref,
    lat_all, x_ref, wbuf, obuf,
    local_sem, ring_send, ring_recv, flip_send, flip_recv, own_send, own_recv,
    lat_send, lat_recv, lat_local, load_sem, store_sem, halo_send, halo_recv, halo_local,
):
    chips = n // 2
    hops = chips - 1
    tok, own = lat_ref.shape
    cols = proj_ref.shape[-1]
    width = wbuf.shape[-1]
    pieces = cols // width
    me = lax.axis_index("ctx")
    head = lax.axis_index("head")
    core = me % 2
    chip = me // 2
    cx = chip % 2
    cz = chip // 2
    pos = (1 - cx) * cz + cx * (chips - 1 - cz)
    ahead = chip_of((pos + 1) % chips, chips) * 2 + core
    behind = chip_of((pos + chips - 1) % chips, chips) * 2 + core
    twin = me + 1 - 2 * core
    right = (me + 1) % n
    left = (me + n - 1) % n

    barrier = pltpu.get_barrier_semaphore()
    for other in (ahead, behind, twin, right, left):
        pl.semaphore_signal(barrier, inc=1, device_id={"ctx": other}, device_id_type=MESH)
    for k in range(1, heads):
        pl.semaphore_signal(
            barrier, inc=1, device_id={"head": (head + k) % heads}, device_id_type=MESH
        )

    def full(w):
        return wo_ref if w == 3 else qkv_ref.at[w]

    def local_copy(w):
        return pltpu.make_async_copy(w_ref.at[w], full(w).at[me], local_sem.at[w])

    for w in range(4):
        local_copy(w).start()
    mine = pltpu.make_async_copy(lat_ref, lat_all.at[head], lat_local)
    mine.start()
    pl.semaphore_wait(barrier, 5 + heads - 1)

    def ring(w, hop, way, first=False):
        source = (pos + chips - hop) % chips if way == 0 else (pos + hop) % chips
        owner = chip_of(source, chips) * 2 + core
        block = full(w).at[owner, way]
        return pltpu.make_async_remote_copy(
            src_ref=w_ref.at[w, way] if first else block, dst_ref=block,
            send_sem=ring_send.at[w, hop, way], recv_sem=ring_recv.at[w, hop, way],
            device_id={"ctx": ahead if way == 0 else behind}, device_id_type=MESH,
        )

    def arrived(w, hop, way):
        source = (pos + chips - hop - 1) % chips if way == 0 else (pos + hop + 1) % chips
        return full(w).at[chip_of(source, chips) * 2 + core, way]

    def ring_wait(w, hop, way):
        block = arrived(w, hop, way)
        pltpu.make_async_remote_copy(
            src_ref=block, dst_ref=block,
            send_sem=ring_send.at[w, hop, way], recv_sem=ring_recv.at[w, hop, way],
            device_id={"ctx": ahead if way == 0 else behind}, device_id_type=MESH,
        ).wait_recv()

    def flip(w, hop, way):
        block = arrived(w, hop, way)
        return pltpu.make_async_remote_copy(
            src_ref=block, dst_ref=block,
            send_sem=flip_send.at[w, hop, way], recv_sem=flip_recv.at[w, hop, way],
            device_id={"ctx": twin}, device_id_type=MESH,
        )

    def flip_wait(w, hop, way):
        source = (pos + chips - hop - 1) % chips if way == 0 else (pos + hop + 1) % chips
        block = full(w).at[chip_of(source, chips) * 2 + 1 - core, way]
        pltpu.make_async_remote_copy(
            src_ref=block, dst_ref=block,
            send_sem=flip_send.at[w, hop, way], recv_sem=flip_recv.at[w, hop, way],
            device_id={"ctx": twin}, device_id_type=MESH,
        ).wait_recv()

    def own_flip(w, who):
        return pltpu.make_async_remote_copy(
            src_ref=w_ref.at[w], dst_ref=full(w).at[who],
            send_sem=own_send.at[w], recv_sem=own_recv.at[w],
            device_id={"ctx": twin}, device_id_type=MESH,
        )

    def begin(w):
        ring(w, 0, 0, True).start()
        ring(w, 0, 1, True).start()
        own_flip(w, me).start()

    def advance(w, hop):
        for way in range(2):
            ring_wait(w, hop - 1, way)
            ring(w, hop, way).start()
            flip(w, hop - 1, way).start()

    def finish(w):
        for way in range(2):
            ring_wait(w, hops - 1, way)
            flip(w, hops - 1, way).start()

    def settle(w):
        local_copy(w).wait()
        own_flip(w, twin).wait_recv()

        @pl.loop(0, hops)
        def _(hop):
            for way in range(2):
                flip_wait(w, hop, way)

    def drain(w):
        own_flip(w, me).wait_send()

        @pl.loop(0, hops)
        def _(hop):
            for way in range(2):
                ring(w, hop, way).wait_send()
                flip(w, hop, way).wait_send()

    def lat_copy(k):
        return pltpu.make_async_remote_copy(
            src_ref=lat_ref, dst_ref=lat_all.at[head],
            send_sem=lat_send.at[k - 1], recv_sem=lat_recv.at[k - 1],
            device_id={"head": (head + k) % heads}, device_id_type=MESH,
        )

    def norm():
        mine.wait()
        for k in range(1, heads):
            came = lat_all.at[(head + heads - k) % heads]
            pltpu.make_async_remote_copy(
                src_ref=lat_ref, dst_ref=came,
                send_sem=lat_send.at[k - 1], recv_sem=lat_recv.at[k - 1],
                device_id={"head": (head + k) % heads}, device_id_type=MESH,
            ).wait_recv()
        step = 16

        @pl.loop(0, tok // step)
        def _(i):
            rows = pl.ds(pl.multiple_of(i * step, step), step)
            squares = jnp.zeros((step, 1), jnp.float32)
            crossed = jnp.zeros((step, 1), jnp.float32)
            for h in range(heads):
                part = lat_all[h, rows, :].astype(jnp.float32)
                tang = probe_ref[rows, h * own:(h + 1) * own].astype(jnp.float32)
                squares = squares + jnp.sum(part * part, -1, keepdims=True)
                crossed = crossed + jnp.sum(part * tang, -1, keepdims=True)
            inverse = lax.rsqrt(squares / D + 1e-06)
            along = crossed / D
            second = inverse * inverse * inverse * along
            rows_t = pl.ds(pl.multiple_of(tok + i * step, step), step)
            for h in range(heads):
                part = lat_all[h, rows, :].astype(jnp.float32)
                tang = probe_ref[rows, h * own:(h + 1) * own].astype(jnp.float32)
                gain = gain_ref[:, h * own:(h + 1) * own]
                x_ref[rows, h * own:(h + 1) * own] = (part * inverse * gain).astype(jnp.bfloat16)
                x_ref[rows_t, h * own:(h + 1) * own] = (
                    (tang * inverse - part * second) * gain
                ).astype(jnp.bfloat16)

    def load(w, piece, slot):
        at = pl.ds(pl.multiple_of(piece * width, width), width)
        return pltpu.make_async_copy(
            qkv_ref.at[w, :, :, :, at], wbuf.at[slot], load_sem.at[slot]
        )

    def multiply(w, piece, slot):
        load(w, piece, slot).wait()
        weight = wbuf[slot].reshape(D, width)
        rows = 128

        @pl.loop(0, 2 * tok // rows)
        def _(i):
            at = pl.ds(pl.multiple_of(i * rows, rows), rows)
            obuf[slot, at, :] = jnp.dot(
                x_ref[at, :], weight, preferred_element_type=jnp.float32
            ).astype(jnp.bfloat16)

        at = pl.ds(pl.multiple_of(piece * width, width), width)
        store = pltpu.make_async_copy(
            obuf.at[slot], proj_ref.at[w, :, at], store_sem.at[slot]
        )
        store.start()
        store.wait()

    def fetch(q, slot):
        @pl.when(q < 2 * pieces)
        def _():
            load(q // pieces, q % pieces, slot).start()

    def work(q, slot):
        @pl.when(q < 2 * pieces)
        def _():
            multiply(q // pieces, q % pieces, slot)

    def halo(side, a):
        return pltpu.make_async_remote_copy(
            src_ref=proj_ref.at[a], dst_ref=halo_ref.at[side, a],
            send_sem=halo_send.at[side, a], recv_sem=halo_recv.at[side, a],
            device_id={"ctx": right if side == 0 else left}, device_id_type=MESH,
        )

    def halo_fill(side, a):
        return pltpu.make_async_copy(proj_ref.at[a], halo_ref.at[side, a], halo_local.at[a])

    def halo_start(a):
        @pl.when(me < n - 1)
        def _():
            halo(0, a).start()

        @pl.when(me > 0)
        def _():
            halo(1, a).start()

        @pl.when(me == 0)
        def _():
            halo_fill(0, a).start()

        @pl.when(me == n - 1)
        def _():
            halo_fill(1, a).start()

    def halo_end(a):
        @pl.when(me < n - 1)
        def _():
            halo(0, a).wait_send()
            halo(1, a).wait_recv()

        @pl.when(me > 0)
        def _():
            halo(1, a).wait_send()
            halo(0, a).wait_recv()

        @pl.when(me == 0)
        def _():
            halo_fill(0, a).wait()

        @pl.when(me == n - 1)
        def _():
            halo_fill(1, a).wait()

    begin(0)
    begin(1)
    for k in range(1, heads):
        lat_copy(k).start()

    @pl.loop(1, hops)
    def _(hop):
        advance(0, hop)
        advance(1, hop)

        @pl.when(hop == hops - 1)
        def _():
            norm()

    begin(2)
    begin(3)
    finish(0)
    finish(1)
    settle(0)
    settle(1)

    @pl.loop(1, hops)
    def _(hop):
        q = (hop - 1) * 4
        fetch(q, 0)
        fetch(q + 1, 1)
        advance(2, hop)
        work(q, 0)
        fetch(q + 2, 0)
        work(q + 1, 1)
        fetch(q + 3, 1)
        advance(3, hop)
        work(q + 2, 0)
        work(q + 3, 1)
        for a in range(2):

            @pl.when(hop == -(-(a + 1) * pieces // 4))
            def _(a=a):
                halo_start(a)

    finish(2)
    finish(3)
    settle(2)

    load(2, 0, 0).start()
    for piece in range(pieces):
        if piece + 1 < pieces:
            load(2, piece + 1, (piece + 1) % 2).start()
        multiply(2, piece, piece % 2)

    settle(3)
    halo_end(0)
    halo_end(1)
    for w in range(4):
        drain(w)
    for k in range(1, heads):
        lat_copy(k).wait_send()


def gather_and_project(latent, probe, gain, weights):
    n = lax.axis_size("ctx")
    heads = lax.axis_size("head")
    hops = n // 2 - 1
    tok, own = latent.shape
    rows, cols = weights.shape[1:]
    weights = weights.reshape(4, 2, rows // 2, cols)
    width = 256 if cols % 256 == 0 else 128
    dma = pltpu.SemaphoreType.DMA
    bf = jnp.bfloat16
    vmem = pl.BlockSpec(memory_space=pltpu.VMEM)
    anywhere = pl.BlockSpec(memory_space=pl.ANY)
    return pl.pallas_call(
        functools.partial(project_kernel, n, heads),
        out_shape=(
            jax.ShapeDtypeStruct((3, n, 2, rows // 2, cols), bf),
            jax.ShapeDtypeStruct((n, 2, rows // 2, cols), bf),
            jax.ShapeDtypeStruct((3, 2 * tok, cols), bf),
            jax.ShapeDtypeStruct((2, 2, 2 * tok, cols), bf),
        ),
        in_specs=[vmem, vmem, vmem, anywhere],
        out_specs=(anywhere,) * 4,
        scratch_shapes=[
            pltpu.VMEM((heads, tok, own), bf),
            pltpu.VMEM((2 * tok, D), bf),
            pltpu.VMEM((2, n, 2, rows // 2, width), bf),
            pltpu.VMEM((2, 2 * tok, width), bf),
            dma((4,)), dma((4, hops, 2)), dma((4, hops, 2)), dma((4, hops, 2)), dma((4, hops, 2)),
            dma((4,)), dma((4,)),
            dma((heads - 1,)), dma((heads - 1,)), dma, dma((2,)), dma((2,)),
            dma((2, 2)), dma((2, 2)), dma((2,)),
        ],
        compiler_params=pltpu.CompilerParams(
            collective_id=0, has_side_effects=True, vmem_limit_bytes=48 * MIB
        ),
    )(latent, probe, gain, weights)


def attend_kernel(tiles, mask_ref, q_ref, own_ref, low_ref, high_ref, out_ref, k_all, v_all):
    tok = tiles * TILE
    scale = HD ** (-0.5)
    for place, ref in enumerate((low_ref, own_ref, high_ref)):
        at = slice(place * tok, (place + 1) * tok)
        k_all[at, :HD] = ref[0, :tok, :]
        k_all[at, HD:] = ref[0, tok:, :]
        v_all[at, :HD] = ref[1, :tok, :]
        v_all[at, HD:] = ref[1, tok:, :]
    contract = (((1,), (1,)), ((), ()))
    band = 2 * tiles + 1
    for i in range(tiles):
        rows = slice(i * TILE, (i + 1) * TILE)
        rows_t = slice(tok + i * TILE, tok + (i + 1) * TILE)
        query = q_ref[0, rows, :]
        query_t = q_ref[0, rows_t, :]
        keys = k_all[i * TILE:(i + band) * TILE, :]
        scores = lax.dot_general(
            query, keys[:, :HD], contract, preferred_element_type=jnp.float32
        ) * scale
        scores_t = lax.dot_general(
            jnp.concatenate([query_t, query], 1), keys, contract,
            preferred_element_type=jnp.float32,
        ) * scale
        masked = jnp.concatenate(
            [
                jnp.where(
                    mask_ref[i, i + j] == 1, scores[:, j * TILE:(j + 1) * TILE], -1e30
                )
                for j in range(band)
            ],
            1,
        )
        highest = jnp.max(masked, -1, keepdims=True)
        expos = jnp.exp(masked - highest)
        probs = expos * (1.0 / jnp.sum(expos, -1, keepdims=True))
        weighed = probs * scores_t
        probs_t = weighed - probs * jnp.sum(weighed, -1, keepdims=True)
        probs_b = probs.astype(jnp.bfloat16)
        values = v_all[i * TILE:(i + band) * TILE, :]
        first = jnp.dot(probs_b, values, preferred_element_type=jnp.float32)
        second = first[:, HD:] + jnp.dot(
            probs_t.astype(jnp.bfloat16), values[:, :HD], preferred_element_type=jnp.float32
        )
        out_ref[rows, :] = first[:, :HD].astype(jnp.bfloat16)
        out_ref[rows_t, :] = second.astype(jnp.bfloat16)


def attend(tile_rows, proj, halo):
    rows, cols = proj.shape[1:]
    tok = rows // 2
    tiles = tok // TILE
    return pl.pallas_call(
        functools.partial(attend_kernel, tiles),
        grid=(cols // HD,),
        out_shape=jax.ShapeDtypeStruct((rows, cols), jnp.bfloat16),
        in_specs=[
            pl.BlockSpec(memory_space=pltpu.SMEM),
            pl.BlockSpec((1, rows, HD), lambda h: (2, 0, h)),
            pl.BlockSpec((2, rows, HD), lambda h: (0, 0, h)),
            pl.BlockSpec((None, 2, rows, HD), lambda h: (0, 0, 0, h)),
            pl.BlockSpec((None, 2, rows, HD), lambda h: (1, 0, 0, h)),
        ],
        out_specs=pl.BlockSpec((rows, HD), lambda h: (0, h)),
        scratch_shapes=[pltpu.VMEM((3 * tok, 2 * HD), jnp.bfloat16)] * 2,
        compiler_params=pltpu.CompilerParams(vmem_limit_bytes=32 * MIB),
    )(tile_rows, proj, proj, halo, halo)


def shards(latent, probe, norm_gain, w_query, w_key, w_value, w_out, tile_mask):
    tok_rows, own_cols = latent.shape
    weights = jnp.stack([w_key, w_value, w_query, w_out.T])
    _, wo_full, proj, halo = gather_and_project(latent, probe, norm_gain.reshape(1, D), weights)
    tiles_dev = tok_rows // TILE
    ctx_slot = lax.axis_index("ctx")
    mask_pad = jnp.pad(tile_mask, tiles_dev)
    tile_rows = lax.dynamic_slice(
        mask_pad,
        (ctx_slot * tiles_dev + tiles_dev, ctx_slot * tiles_dev),
        (tiles_dev, 3 * tiles_dev),
    )
    both_rows = attend(tile_rows, proj, halo)
    w_out_t = wo_full.reshape(D, w_out.shape[0])
    terms = lax.dot_general(
        both_rows, w_out_t, (((1,), (1,)), ((), ())), preferred_element_type=jnp.float32
    ).astype(jnp.bfloat16)
    summed = lax.psum_scatter(terms, "head", scatter_dimension=1, tiled=True).astype(jnp.float32)
    branch = summed[:tok_rows]
    branch_t = summed[tok_rows:]
    latent_f = latent.astype(jnp.float32)
    col_start = lax.axis_index("head") * own_cols
    tangent_own = lax.dynamic_slice_in_dim(probe, col_start, own_cols, 1).astype(jnp.float32)
    mixed = (latent_f + branch).astype(jnp.bfloat16)
    trace_terms = lax.psum(jnp.sum(tangent_own * branch_t, -1), "head")
    return (mixed, branch_t.astype(jnp.bfloat16), trace_terms)


def layer_kernel(
    layers, mask_ref, lat_ref, probe_ref, gain_ref, wk_ref, wv_ref, wq_ref, wo_ref,
    att_ref, ofull_ref, oz_ref,
    x_all, w_all, wq_all, k_all, v_all, q_all, a_all, sums, sums_in,
    in_sem, a2a_send, a2a_recv, a2a_local, z_send, z_recv, s_send, s_recv,
    n_send, n_recv, d_send, d_recv, f_send, f_recv, h_send, h_recv,
    at_send, at_recv, at_local, o_send, o_recv, o_local, of_send, of_recv,
):
    tok, own = lat_ref.shape
    cols = w_all.shape[-1]
    nheads = cols // HD
    half = wo_ref.shape[0] // 2
    me = lax.axis_index("ctx")
    y = lax.axis_index("head")
    z = me // 4
    x = (me // 2) % 2
    c = me % 2
    base = z * 4
    q = 2 * x + c
    tq = 2 * x + 1 - c
    xq = 2 * (1 - x) + c
    dq = 2 * (1 - x) + 1 - c
    heads_at = 2
    outs_at = 2 + nheads
    items = outs_at + 2
    bf = jnp.bfloat16

    def at(ctx, head):
        return {"ctx": ctx, "head": head}

    barrier = pltpu.get_barrier_semaphore()
    for k in range(4):
        for j in range(2):
            if k or j:
                pl.semaphore_signal(
                    barrier, inc=1, device_id=at(base + (q + k) % 4, (y + j) % 2),
                    device_id_type=MESH,
                )

    @pl.when(z < layers - 1)
    def _():
        pl.semaphore_signal(barrier, inc=1, device_id=at(me + 4, y), device_id_type=MESH)

    @pl.when(z > 0)
    def _():
        pl.semaphore_signal(barrier, inc=1, device_id=at(me - 4, y), device_id_type=MESH)

    def load_in(p):
        if p == 0:
            source = lat_ref
        else:
            source = probe_ref.at[:, pl.ds(pl.multiple_of(y * own, own), own)]
        return pltpu.make_async_copy(
            source, x_all.at[q, y, pl.ds(p * tok, tok)], in_sem.at[p]
        )

    load_in(0).start()
    load_in(1).start()

    def quarter(w, k):
        if w < heads_at:
            return (wk_ref, wv_ref)[w].at[:, pl.ds(pl.multiple_of(k * cols, cols), cols)]
        first = pl.multiple_of(k * cols + (w - heads_at) * HD, HD)
        return wq_ref.at[:, pl.ds(first, HD)]

    def weight_at(w, zz):
        return w_all.at[w, zz] if w < heads_at else wq_all.at[w - heads_at, zz]

    def a2a_own(w):
        return pltpu.make_async_copy(quarter(w, q), weight_at(w, z).at[q], a2a_local.at[w])

    def a2a(w, k):
        to = (q + k) % 4
        return pltpu.make_async_remote_copy(
            src_ref=quarter(w, to), dst_ref=weight_at(w, z).at[q],
            send_sem=a2a_send.at[w, k - 1], recv_sem=a2a_recv.at[w, k - 1],
            device_id=at(base + to, y), device_id_type=MESH,
        )

    def a2a_start(w):
        a2a_own(w).start()
        for k in (2, 1, 3):
            a2a(w, k).start()

    def a2a_wait(w):
        a2a_own(w).wait()
        for k in (1, 2, 3):
            came = weight_at(w, z).at[(q + 4 - k) % 4]
            pltpu.make_async_remote_copy(
                src_ref=came, dst_ref=came,
                send_sem=a2a_send.at[w, k - 1], recv_sem=a2a_recv.at[w, k - 1],
                device_id=at(base + (q + k) % 4, y), device_id_type=MESH,
            ).wait_recv()

    def region(item, zz):
        return weight_at(item, zz) if item < outs_at else oz_ref.at[zz, item - outs_at]

    def z_copy(item, way, d):
        zz = z - d if way == 0 else z + d
        block = region(item, zz)
        mine = item >= outs_at and d == 0
        return pltpu.make_async_remote_copy(
            src_ref=wo_ref.at[pl.ds((item - outs_at) * half, half)] if mine else block,
            dst_ref=block,
            send_sem=z_send.at[item, way, d], recv_sem=z_recv.at[item, way, d],
            device_id=at(me + 4 if way == 0 else me - 4, y), device_id_type=MESH,
        )

    def z_has(way, d):
        return z >= d if way == 0 else z + d <= layers - 1

    def z_sends(way, d):
        if way == 0:
            return jnp.logical_and(z >= d, z < layers - 1)
        return jnp.logical_and(z + d <= layers - 1, z > 0)

    def z_edge(way):
        return z == layers - 2 if way == 0 else z == 1

    def z_begin(item, edge=None):
        for way in range(2):
            here = z_sends(way, 0)
            if edge is not None:
                here = jnp.logical_and(here, z_edge(way) == edge)

            @pl.when(here)
            def _(way=way):
                z_copy(item, way, 0).start()

    def z_pace(item):
        for way in range(2):
            for d in range(2):

                @pl.when(jnp.logical_and(z_sends(way, d), z_edge(way)))
                def _(way=way, d=d):
                    z_copy(item, way, d).wait_send()

    def z_came(item, way, d):
        block = region(item, z - d if way == 0 else z + d)
        pltpu.make_async_remote_copy(
            src_ref=block, dst_ref=block,
            send_sem=z_send.at[item, way, d - 1], recv_sem=z_recv.at[item, way, d - 1],
            device_id=at(me + 4 if way == 0 else me - 4, y), device_id_type=MESH,
        ).wait_recv()

    def z_relay(item, d):
        for way in range(2):

            @pl.when(z_sends(way, d))
            def _(way=way):
                z_came(item, way, d)
                z_copy(item, way, d).start()

    def z_ends(way, d):
        if way == 0:
            return jnp.logical_and(z >= d, z == layers - 1)
        return jnp.logical_and(z + d <= layers - 1, z == 0)

    def z_wait(item, *dists):
        for d in dists:
            for way in range(2):

                @pl.when(z_ends(way, d))
                def _(way=way, d=d):
                    z_came(item, way, d)

    def z_drain(item, paced):
        for way in range(2):
            for d in range(layers - 1):
                here = z_sends(way, d)
                if paced and d < 2:
                    here = jnp.logical_and(here, jnp.logical_not(z_edge(way)))

                @pl.when(here)
                def _(way=way, d=d):
                    z_copy(item, way, d).wait_send()

    def part(slot, side, p):
        return x_all.at[slot, side, pl.ds(p * tok, tok)]

    twin = at(base + tq, y)
    across = at(base + xq, y)
    over = at(me, 1 - y)

    def n_copy(way, p, slot=None, side=None):
        block = part(q, y, p) if slot is None else part(slot, side, p)
        return pltpu.make_async_remote_copy(
            src_ref=block, dst_ref=block,
            send_sem=n_send.at[way, p], recv_sem=n_recv.at[way, p],
            device_id=(twin, across, over)[way], device_id_type=MESH,
        )

    def d_copy(p, landing=False):
        if landing:
            block = part(xq, 1 - y, p)
        else:
            block = part(xq, y, p) if p == 0 else part(q, 1 - y, p)
        return pltpu.make_async_remote_copy(
            src_ref=block, dst_ref=block,
            send_sem=d_send.at[p], recv_sem=d_recv.at[p],
            device_id=over if p == 0 else across, device_id_type=MESH,
        )

    def f_copy(kind, p, landing=False):
        if landing:
            block = (part(dq, y, p), part(tq, 1 - y, p), part(dq, 1 - y, p))[kind]
        else:
            block = (part(xq, y, p), part(q, 1 - y, p), part(xq, 1 - y, p))[kind]
        return pltpu.make_async_remote_copy(
            src_ref=block, dst_ref=block,
            send_sem=f_send.at[kind, p], recv_sem=f_recv.at[kind, p],
            device_id=twin, device_id_type=MESH,
        )

    def s_copy():
        return pltpu.make_async_remote_copy(
            src_ref=sums, dst_ref=sums_in, send_sem=s_send, recv_sem=s_recv,
            device_id=over, device_id_type=MESH,
        )

    step = 16

    def norm_sums():
        @pl.loop(0, tok // step)
        def _(i):
            rows = pl.ds(pl.multiple_of(i * step, step), step)
            rows_t = pl.ds(pl.multiple_of(tok + i * step, step), step)
            lat = x_all[q, y, rows, :].astype(jnp.float32)
            tang = x_all[q, y, rows_t, :].astype(jnp.float32)
            squares = jnp.sum(lat * lat, -1, keepdims=True)
            crossed = jnp.sum(lat * tang, -1, keepdims=True)
            lane = lax.broadcasted_iota(jnp.int32, (step, HD), 1)
            sums[rows, :] = jnp.where(lane < HD // 2, squares, crossed)

    def norm_apply():
        @pl.loop(0, tok // step)
        def _(i):
            rows = pl.ds(pl.multiple_of(i * step, step), step)
            rows_t = pl.ds(pl.multiple_of(tok + i * step, step), step)
            both = sums[rows, :] + sums_in[rows, :]
            inverse = lax.rsqrt(both[:, 0:1] / D + 1e-06)
            along = both[:, HD // 2:HD // 2 + 1] / D
            second = inverse * inverse * inverse * along
            lat = x_all[q, y, rows, :].astype(jnp.float32)
            tang = x_all[q, y, rows_t, :].astype(jnp.float32)
            gain = gain_ref[y]
            x_all[q, y, rows, :] = (lat * inverse * gain).astype(bf)
            x_all[q, y, rows_t, :] = ((tang * inverse - lat * second) * gain).astype(bf)

    def multiply(weight, blk, p):
        acc = None
        for side in range(2):
            rows_in = weight[pl.ds(side * (layers // 2), layers // 2)]
            term = jnp.dot(
                x_all[blk, side, p * tok:(p + 1) * tok, :], rows_in.reshape(own, -1),
                preferred_element_type=jnp.float32,
            )
            acc = term if acc is None else acc + term
        return acc.astype(bf)

    def project(w, blk):
        for p in range(2):
            res = multiply(w_all.at[w], blk, p)
            rows = pl.ds(pl.multiple_of(blk * tok + tok, tok), tok)
            for h in range(nheads):
                lanes = slice((2 * h + p) * HD, (2 * h + p + 1) * HD)
                (k_all, v_all)[w][rows, lanes] = res[:, h * HD:(h + 1) * HD]

    def project_query(h):
        @pl.loop(0, 4)
        def _(blk):
            for p in range(2):
                rows = pl.ds(pl.multiple_of(blk * tok, tok), tok)
                q_all[rows, (2 * h + p) * HD:(2 * h + p + 1) * HD] = multiply(
                    wq_all.at[h], blk, p
                )

    kv = (k_all, v_all)

    def halo(way, a, landing=False):
        if way == 0:
            source = pl.ds(4 * tok, tok)
            target = pl.ds(0, tok)
        else:
            source = pl.ds(tok, tok)
            target = pl.ds(5 * tok, tok)
        return pltpu.make_async_remote_copy(
            src_ref=kv[a].at[target if landing else source], dst_ref=kv[a].at[target],
            send_sem=h_send.at[way, a], recv_sem=h_recv.at[way, a],
            device_id=at(me + 4 if way == 0 else me - 4, y), device_id_type=MESH,
        )

    def halo_start(a):
        @pl.when(z < layers - 1)
        def _():
            halo(0, a).start()

        @pl.when(z > 0)
        def _():
            halo(1, a).start()

    def halo_wait(a):
        @pl.when(z > 0)
        def _():
            halo(0, a, True).wait_recv()

        @pl.when(z < layers - 1)
        def _():
            halo(1, a, True).wait_recv()

    def halo_fill():
        @pl.when(z == 0)
        def _():
            for a in range(2):
                kv[a][0:tok, :] = jnp.zeros((tok, 2 * cols), bf)

        @pl.when(z == layers - 1)
        def _():
            for a in range(2):
                kv[a][5 * tok:6 * tok, :] = jnp.zeros((tok, 2 * cols), bf)

    def halo_drain(a):
        @pl.when(z < layers - 1)
        def _():
            halo(0, a).wait_send()

        @pl.when(z > 0)
        def _():
            halo(1, a).wait_send()

    tiles = tok // TILE
    band = 2 * tiles + 1
    scale = HD ** (-0.5)
    contract = (((1,), (1,)), ((), ()))

    def attend_block(h, blk):
        lanes = slice(2 * h * HD, 2 * (h + 1) * HD)

        @pl.loop(0, tiles)
        def _(i):
            tile = blk * tiles + i
            rows = pl.ds(pl.multiple_of(tile * TILE, TILE), TILE)
            span = pl.ds(pl.multiple_of(tile * TILE, TILE), band * TILE)
            query = q_all[rows, lanes]
            keys = k_all[span, lanes]
            left = jnp.concatenate(
                [
                    jnp.concatenate([query[:, :HD], query[:, HD:]], 0),
                    jnp.concatenate([jnp.zeros((TILE, HD), bf), query[:, :HD]], 0),
                ],
                1,
            )
            scores = lax.dot_general(left, keys, contract, preferred_element_type=jnp.float32)
            masked = jnp.concatenate(
                [
                    scores[:TILE, j * TILE:(j + 1) * TILE] * scale
                    + (mask_ref[tile, tile + j] - 1).astype(jnp.float32) * 1e30
                    for j in range(band)
                ],
                1,
            )
            highest = jnp.max(masked, -1, keepdims=True)
            expos = jnp.exp(masked - highest)
            probs = expos * (1.0 / jnp.sum(expos, -1, keepdims=True))
            weighed = probs * (scores[TILE:] * scale)
            probs_t = weighed - probs * jnp.sum(weighed, -1, keepdims=True)
            stacked = jnp.concatenate([probs.astype(bf), probs_t.astype(bf)], 0)
            out = jnp.dot(stacked, v_all[span, lanes], preferred_element_type=jnp.float32)
            into = pl.ds(pl.multiple_of(i * TILE, TILE), TILE)
            a_all[h, blk, 0, into, :] = out[:TILE, :HD].astype(bf)
            a_all[h, blk, 1, into, :] = (out[:TILE, HD:] + out[TILE:, :HD]).astype(bf)

    def att_slot(h, head, slot):
        return att_ref.at[head, :, :, pl.ds(pl.multiple_of((slot * nheads + h) * HD, HD), HD)]

    def att_copy(h, k, j):
        blk = (q + k) % 4
        return pltpu.make_async_remote_copy(
            src_ref=a_all.at[h, blk], dst_ref=att_slot(h, y, q),
            send_sem=at_send.at[h, k, j], recv_sem=at_recv.at[h, k, j],
            device_id=at(base + blk, (y + j) % 2), device_id_type=MESH,
        )

    def att_own(h):
        return pltpu.make_async_copy(a_all.at[h, q], att_slot(h, y, q), at_local.at[h])

    def att_start(h, k):
        for j in (1, 0):
            if k or j:
                att_copy(h, k, j).start()
            else:
                att_own(h).start()

    def att_end(h):
        for k in range(4):
            for j in range(2):
                if k or j:
                    came = att_slot(h, (y + j) % 2, (q + 4 - k) % 4)
                    pltpu.make_async_remote_copy(
                        src_ref=came, dst_ref=came,
                        send_sem=at_send.at[h, k, j], recv_sem=at_recv.at[h, k, j],
                        device_id=at(base + (q + k) % 4, (y + j) % 2), device_id_type=MESH,
                    ).wait_recv()
                    att_copy(h, k, j).wait_send()
        att_own(h).wait()

    per = layers // 2

    def o_slot(zz, xs, cs, ys, h):
        return ofull_ref.at[zz % per, xs, cs, ys, pl.ds(h * half, half)]

    def o_source(zz, own_block, h):
        return wo_ref.at[pl.ds(h * half, half)] if own_block else oz_ref.at[zz, h]

    def o_far(zz, own_block, h):
        goal = zz // per
        return pltpu.make_async_remote_copy(
            src_ref=o_source(zz, own_block, h), dst_ref=o_slot(zz, x, c, y, h),
            send_sem=o_send.at[zz, h, 0], recv_sem=o_recv.at[zz % per, h, 1, (y + goal) % 2],
            device_id=at(base + xq, goal), device_id_type=MESH,
        )

    def o_near(zz, own_block, h):
        return pltpu.make_async_remote_copy(
            src_ref=o_source(zz, own_block, h), dst_ref=o_slot(zz, x, c, y, h),
            send_sem=o_send.at[zz, h, 1], recv_sem=o_recv.at[zz % per, h, 0, 1],
            device_id=over, device_id_type=MESH,
        )

    def o_self(zz, own_block, h):
        return pltpu.make_async_copy(
            o_source(zz, own_block, h), o_slot(zz, x, c, y, h), o_local.at[zz % per, h]
        )

    def o_give(zz, own_block, h):
        o_far(zz, own_block, h).start()

        @pl.when(zz // per == y)
        def _():
            o_self(zz, own_block, h).start()

        @pl.when(zz // per != y)
        def _():
            o_near(zz, own_block, h).start()

    def o_give_dist(d, among):
        for h in range(2):
            for way in range(2 if d else 1):

                @pl.when(among(way, d))
                def _(way=way, h=h):
                    o_give(z - d if way == 0 else z + d, d == 0, h)

    def o_drain():
        for d in range(layers):
            for h in range(2):
                for way in range(2 if d else 1):

                    @pl.when(z_has(way, d))
                    def _(way=way, h=h, d=d):
                        zz = z - d if way == 0 else z + d
                        o_far(zz, d == 0, h).wait_send()

                        @pl.when(zz // per != y)
                        def _():
                            o_near(zz, d == 0, h).wait_send()

    def o_flip(zz, h, dx, dy, landing=False):
        xs = (x + dx) % 2
        ys = (y + dy) % 2
        block = o_slot(zz, xs, 1 - c if landing else c, ys, h)
        return pltpu.make_async_remote_copy(
            src_ref=block, dst_ref=block,
            send_sem=of_send.at[zz % per, h, dx, dy], recv_sem=of_recv.at[zz % per, h, dx, dy],
            device_id=twin, device_id_type=MESH,
        )

    def o_take(zz, h):
        for dx in range(2):
            for dy in range(2):
                if dx or dy:
                    came = o_slot(zz, (x + dx) % 2, c, (y + dy) % 2, h)
                    pltpu.make_async_remote_copy(
                        src_ref=came, dst_ref=came,
                        send_sem=o_send.at[zz, h, 0], recv_sem=o_recv.at[zz % per, h, dx, dy],
                        device_id=twin, device_id_type=MESH,
                    ).wait_recv()
                else:
                    o_self(zz, False, h).wait()
                o_flip(zz, h, dx, dy).start()

    def o_take_end(zz, h):
        for dx in range(2):
            for dy in range(2):
                o_flip(zz, h, dx, dy, True).wait_recv()
                o_flip(zz, h, dx, dy).wait_send()

    ends = (z == 0).astype(jnp.int32) + (z == layers - 1).astype(jnp.int32)
    pl.semaphore_wait(barrier, 9 - ends)

    queries = [heads_at + h for h in range(nheads)]
    outs = [outs_at, outs_at + 1]
    every = range(1, layers)
    a2a_start(0)
    for w in outs:
        z_begin(w)
    load_in(0).wait()
    load_in(1).wait()
    norm_sums()
    s_copy().start()
    halo_fill()
    s_copy().wait()
    norm_apply()
    n_copy(1, 0).start()
    n_copy(2, 1).start()
    n_copy(0, 0).start()
    n_copy(0, 1).start()
    a2a_wait(0)
    z_begin(0)
    a2a_start(1)
    for w in outs:
        z_relay(w, 1)

    n_copy(1, 0, xq, y).wait_recv()
    n_copy(1, 1).start()
    f_copy(0, 0).start()
    n_copy(2, 1, q, 1 - y).wait_recv()
    n_copy(2, 0).start()
    f_copy(1, 1).start()

    z_relay(0, 1)
    for w in outs:
        z_relay(w, 2)
    a2a_wait(1)
    z_begin(1)

    n_copy(1, 1, xq, y).wait_recv()
    n_copy(2, 0, q, 1 - y).wait_recv()
    d_copy(0).start()
    d_copy(1).start()
    f_copy(0, 1).start()
    f_copy(1, 0).start()
    for w in queries:
        a2a_start(w)

    z_relay(0, 2)
    z_relay(1, 1)
    z_wait(0, *every)
    for p in range(2):
        n_copy(0, p, tq, y).wait_recv()
        f_copy(1, p, True).wait_recv()

    def project_pair(w, side):
        @pl.loop(0, 2)
        def _(j):
            project(w, 2 * side + j)

    project_pair(0, x)
    z_relay(1, 2)
    for p in range(2):
        d_copy(p, True).wait_recv()
        f_copy(2, p).start()
    for w in outs:
        z_wait(w, *every)
    for d in range(layers):
        o_give_dist(d, z_has)
    for w in queries:
        a2a_wait(w)
        z_begin(w, False)
    for p in range(2):
        f_copy(0, p, True).wait_recv()
        f_copy(2, p, True).wait_recv()
    project_pair(0, 1 - x)
    halo_start(0)
    z_wait(1, *every)
    project_pair(1, x)
    project_pair(1, 1 - x)
    halo_start(1)

    def o_take_all(early):
        for n in range(per):
            zz = per * y + n
            close = jnp.logical_and(zz - z <= 1, z - zz <= 1)

            @pl.when(close if early else jnp.logical_not(close))
            def _(zz=zz):
                for h in range(2):
                    o_take(zz, h)

    for h in range(nheads):
        if h:
            z_pace(queries[h - 1])
        z_begin(queries[h], True)
        for d in every[:-1]:
            z_relay(queries[h], d)
        if h == 0:
            halo_wait(0)
            halo_wait(1)
        z_wait(queries[h], *every)
        project_query(h)
        for k in (3, 2, 1, 0):
            attend_block(h, (q + k) % 4)
            att_start(h, k)
        if h < 2:
            o_take_all(h == 0)
    for h in range(nheads):
        att_end(h)
    for zz in range(per):
        for h in range(2):
            o_take_end(per * y + zz, h)
    for w in range(outs_at):
        for k in (1, 2, 3):
            a2a(w, k).wait_send()
    for item in range(items):
        z_drain(item, item in queries[:-1])
    for p in range(2):
        for way in range(3):
            n_copy(way, p).wait_send()
        d_copy(p).wait_send()
        for kind in range(3):
            f_copy(kind, p).wait_send()
    halo_drain(0)
    halo_drain(1)
    o_drain()


def run_layers(mask_rows, latent, probe, gain, wk, wv, wq, wo):
    layers = lax.axis_size("ctx") // 4
    tok, own = latent.shape
    rows, width = wk.shape
    cols = width // 4
    nheads = cols // HD
    half = rows // 2
    dma = pltpu.SemaphoreType.DMA
    bf = jnp.bfloat16
    vmem = pl.BlockSpec(memory_space=pltpu.VMEM)
    smem = pl.BlockSpec(memory_space=pltpu.SMEM)
    anywhere = pl.BlockSpec(memory_space=pl.ANY)
    return pl.pallas_call(
        functools.partial(layer_kernel, layers),
        out_shape=(
            jax.ShapeDtypeStruct((2, 2, tok, width), bf),
            jax.ShapeDtypeStruct((layers // 2, 2, 2, 2, rows, width), bf),
            jax.ShapeDtypeStruct((layers, 2, half, width), bf),
        ),
        in_specs=[smem, anywhere, anywhere, vmem] + [anywhere] * 4,
        out_specs=(anywhere,) * 3,
        scratch_shapes=[
            pltpu.VMEM((4, 2, 2 * tok, own), bf),
            pltpu.VMEM((2, layers, 4, rows, cols), bf),
            pltpu.VMEM((nheads, layers, 4, rows, HD), bf),
            pltpu.VMEM((6 * tok, 2 * cols), bf),
            pltpu.VMEM((6 * tok, 2 * cols), bf),
            pltpu.VMEM((4 * tok, 2 * cols), bf),
            pltpu.VMEM((nheads, 4, 2, tok, HD), bf),
            pltpu.VMEM((tok, HD), jnp.float32),
            pltpu.VMEM((tok, HD), jnp.float32),
            dma((2,)), dma((2 + nheads, 3)), dma((2 + nheads, 3)), dma((2 + nheads,)),
            dma((4 + nheads, 2, layers - 1)), dma((4 + nheads, 2, layers - 1)), dma, dma,
            dma((3, 2)), dma((3, 2)), dma((2,)), dma((2,)), dma((3, 2)), dma((3, 2)),
            dma((2, 2)), dma((2, 2)),
            dma((nheads, 4, 2)), dma((nheads, 4, 2)), dma((nheads,)),
            dma((layers, 2, 2)), dma((layers // 2, 2, 2, 2)), dma((layers // 2, 2)),
            dma((layers // 2, 2, 2, 2)), dma((layers // 2, 2, 2, 2)),
        ],
        compiler_params=pltpu.CompilerParams(
            collective_id=0, has_side_effects=True, vmem_limit_bytes=60 * MIB
        ),
    )(mask_rows, latent, probe, gain, wk, wv, wq, wo)


def finish_kernel(head_ref, att_ref, o_ref, lat_ref, probe_ref, mixed_ref, tang_ref, trace_ref):
    tok, chunk = lat_ref.shape
    contract = (((1,), (1,)), ((), ()))
    branch = None
    for ys in range(2):
        weight = o_ref[:, ys].reshape(chunk, o_ref.shape[-1])
        lhs = att_ref[ys].reshape(2 * tok, att_ref.shape[-1])
        term = lax.dot_general(lhs, weight, contract, preferred_element_type=jnp.float32)
        term = term.astype(jnp.bfloat16).astype(jnp.float32)
        branch = term if branch is None else branch + term
    branch_t = branch[tok:]
    mixed_ref[...] = (lat_ref[...].astype(jnp.float32) + branch[:tok]).astype(jnp.bfloat16)
    tang_ref[...] = branch_t.astype(jnp.bfloat16)
    terms = jnp.sum(probe_ref[...].astype(jnp.float32) * branch_t, -1, keepdims=True)

    @pl.when(pl.program_id(0) == 0)
    def _():
        trace_ref[...] = jnp.zeros_like(trace_ref)

    trace_ref[...] += jnp.broadcast_to(terms, trace_ref.shape)


def finish(att, ofull, latent, probe):
    tok, own = latent.shape
    per, _, _, _, rows, width = ofull.shape
    steps = 2 * per
    chunk = own // steps
    blocks = ofull.reshape(steps, 2, 2, rows, width)
    return pl.pallas_call(
        finish_kernel,
        grid_spec=pltpu.PrefetchScalarGridSpec(
            num_scalar_prefetch=1,
            grid=(steps,),
            in_specs=[
                pl.BlockSpec((2, 2, tok, width), lambda i, h: (0, 0, 0, 0)),
                pl.BlockSpec((None, 2, 2, rows, width), lambda i, h: (i, 0, 0, 0, 0)),
                pl.BlockSpec((tok, chunk), lambda i, h: (0, i)),
                pl.BlockSpec((tok, chunk), lambda i, h: (0, h[0] * steps + i)),
            ],
            out_specs=[
                pl.BlockSpec((tok, chunk), lambda i, h: (0, i)),
                pl.BlockSpec((tok, chunk), lambda i, h: (0, i)),
                pl.BlockSpec((tok, HD), lambda i, h: (0, 0)),
            ],
        ),
        out_shape=(
            jax.ShapeDtypeStruct((tok, own), jnp.bfloat16),
            jax.ShapeDtypeStruct((tok, own), jnp.bfloat16),
            jax.ShapeDtypeStruct((tok, HD), jnp.float32),
        ),
        compiler_params=pltpu.CompilerParams(vmem_limit_bytes=48 * MIB),
    )(lax.axis_index("head").reshape(1), att, blocks, latent, probe)


def layer_shards(latent, probe, norm_gain, w_query, w_key, w_value, w_out, tile_mask):
    tok = latent.shape[0]
    tiles = tok // TILE
    layer_tiles = 4 * tiles
    layer = lax.axis_index("ctx") // 4
    mask_pad = jnp.pad(tile_mask, tiles)
    mask_rows = lax.dynamic_slice(
        mask_pad,
        (layer * layer_tiles + tiles, layer * layer_tiles),
        (layer_tiles, layer_tiles + 2 * tiles),
    )
    att, ofull, _ = run_layers(
        mask_rows, latent, probe, norm_gain.reshape(2, 1, D // 2),
        w_key, w_value, w_query, w_out.T,
    )
    mixed, tangent, trace = finish(att, ofull, latent, probe)
    return (mixed, tangent, lax.psum(trace[:, 0], "head"))


def solution(mesh):
    placed = (
        P("ctx", "head"),
        P("ctx", None),
        P(),
        P("ctx", "head"),
        P("ctx", "head"),
        P("ctx", "head"),
        P("head", "ctx"),
        P(),
    )
    by_layer = mesh.shape["ctx"] == 16 and mesh.shape["head"] == 2
    return jax.shard_map(
        layer_shards if by_layer else shards,
        mesh=mesh,
        in_specs=placed,
        out_specs=(P("ctx", "head"), P("ctx", "head"), P("ctx")),
        check_vma=False,
    )
```

```python
import functools

import jax
import jax.numpy as jnp
from jax import lax
from jax.experimental import pallas as pl
from jax.experimental.pallas import tpu as pltpu
from jax.sharding import PartitionSpec as P

D = 5120
HD = 128
TILE = 128
MESH = pl.DeviceIdType.MESH
MIB = 1 << 20


def chip_of(pos, chips):
    half = pos // (chips // 2)
    return (1 - half) * 2 * pos + half * (2 * (chips - 1 - pos) + 1)


def project_kernel(
    n, heads, lat_ref, probe_ref, gain_ref, w_ref,
    qkv_ref, wo_ref, proj_ref, halo_ref,
    lat_all, x_ref, wbuf, obuf,
    local_sem, ring_send, ring_recv, flip_send, flip_recv, own_send, own_recv,
    lat_send, lat_recv, lat_local, load_sem, store_sem, halo_send, halo_recv, halo_local,
):
    chips = n // 2
    hops = chips - 1
    tok, own = lat_ref.shape
    cols = proj_ref.shape[-1]
    width = wbuf.shape[-1]
    pieces = cols // width
    me = lax.axis_index("ctx")
    head = lax.axis_index("head")
    core = me % 2
    chip = me // 2
    cx = chip % 2
    cz = chip // 2
    pos = (1 - cx) * cz + cx * (chips - 1 - cz)
    ahead = chip_of((pos + 1) % chips, chips) * 2 + core
    behind = chip_of((pos + chips - 1) % chips, chips) * 2 + core
    twin = me + 1 - 2 * core
    right = (me + 1) % n
    left = (me + n - 1) % n

    barrier = pltpu.get_barrier_semaphore()
    for other in (ahead, behind, twin, right, left):
        pl.semaphore_signal(barrier, inc=1, device_id={"ctx": other}, device_id_type=MESH)
    for k in range(1, heads):
        pl.semaphore_signal(
            barrier, inc=1, device_id={"head": (head + k) % heads}, device_id_type=MESH
        )

    def full(w):
        return wo_ref if w == 3 else qkv_ref.at[w]

    def local_copy(w):
        return pltpu.make_async_copy(w_ref.at[w], full(w).at[me], local_sem.at[w])

    for w in range(4):
        local_copy(w).start()
    mine = pltpu.make_async_copy(lat_ref, lat_all.at[head], lat_local)
    mine.start()
    pl.semaphore_wait(barrier, 5 + heads - 1)

    def ring(w, hop, way, first=False):
        source = (pos + chips - hop) % chips if way == 0 else (pos + hop) % chips
        owner = chip_of(source, chips) * 2 + core
        block = full(w).at[owner, way]
        return pltpu.make_async_remote_copy(
            src_ref=w_ref.at[w, way] if first else block, dst_ref=block,
            send_sem=ring_send.at[w, hop, way], recv_sem=ring_recv.at[w, hop, way],
            device_id={"ctx": ahead if way == 0 else behind}, device_id_type=MESH,
        )

    def arrived(w, hop, way):
        source = (pos + chips - hop - 1) % chips if way == 0 else (pos + hop + 1) % chips
        return full(w).at[chip_of(source, chips) * 2 + core, way]

    def ring_wait(w, hop, way):
        block = arrived(w, hop, way)
        pltpu.make_async_remote_copy(
            src_ref=block, dst_ref=block,
            send_sem=ring_send.at[w, hop, way], recv_sem=ring_recv.at[w, hop, way],
            device_id={"ctx": ahead if way == 0 else behind}, device_id_type=MESH,
        ).wait_recv()

    def flip(w, hop, way):
        block = arrived(w, hop, way)
        return pltpu.make_async_remote_copy(
            src_ref=block, dst_ref=block,
            send_sem=flip_send.at[w, hop, way], recv_sem=flip_recv.at[w, hop, way],
            device_id={"ctx": twin}, device_id_type=MESH,
        )

    def flip_wait(w, hop, way):
        source = (pos + chips - hop - 1) % chips if way == 0 else (pos + hop + 1) % chips
        block = full(w).at[chip_of(source, chips) * 2 + 1 - core, way]
        pltpu.make_async_remote_copy(
            src_ref=block, dst_ref=block,
            send_sem=flip_send.at[w, hop, way], recv_sem=flip_recv.at[w, hop, way],
            device_id={"ctx": twin}, device_id_type=MESH,
        ).wait_recv()

    def own_flip(w, who):
        return pltpu.make_async_remote_copy(
            src_ref=w_ref.at[w], dst_ref=full(w).at[who],
            send_sem=own_send.at[w], recv_sem=own_recv.at[w],
            device_id={"ctx": twin}, device_id_type=MESH,
        )

    def begin(w):
        ring(w, 0, 0, True).start()
        ring(w, 0, 1, True).start()
        own_flip(w, me).start()

    def advance(w, hop):
        for way in range(2):
            ring_wait(w, hop - 1, way)
            ring(w, hop, way).start()
            flip(w, hop - 1, way).start()

    def finish(w):
        for way in range(2):
            ring_wait(w, hops - 1, way)
            flip(w, hops - 1, way).start()

    def settle(w):
        local_copy(w).wait()
        own_flip(w, twin).wait_recv()

        @pl.loop(0, hops)
        def _(hop):
            for way in range(2):
                flip_wait(w, hop, way)

    def drain(w):
        own_flip(w, me).wait_send()

        @pl.loop(0, hops)
        def _(hop):
            for way in range(2):
                ring(w, hop, way).wait_send()
                flip(w, hop, way).wait_send()

    def lat_copy(k):
        return pltpu.make_async_remote_copy(
            src_ref=lat_ref, dst_ref=lat_all.at[head],
            send_sem=lat_send.at[k - 1], recv_sem=lat_recv.at[k - 1],
            device_id={"head": (head + k) % heads}, device_id_type=MESH,
        )

    def norm():
        mine.wait()
        for k in range(1, heads):
            came = lat_all.at[(head + heads - k) % heads]
            pltpu.make_async_remote_copy(
                src_ref=lat_ref, dst_ref=came,
                send_sem=lat_send.at[k - 1], recv_sem=lat_recv.at[k - 1],
                device_id={"head": (head + k) % heads}, device_id_type=MESH,
            ).wait_recv()
        step = 16

        @pl.loop(0, tok // step)
        def _(i):
            rows = pl.ds(pl.multiple_of(i * step, step), step)
            squares = jnp.zeros((step, 1), jnp.float32)
            crossed = jnp.zeros((step, 1), jnp.float32)
            for h in range(heads):
                part = lat_all[h, rows, :].astype(jnp.float32)
                tang = probe_ref[rows, h * own:(h + 1) * own].astype(jnp.float32)
                squares = squares + jnp.sum(part * part, -1, keepdims=True)
                crossed = crossed + jnp.sum(part * tang, -1, keepdims=True)
            inverse = lax.rsqrt(squares / D + 1e-06)
            along = crossed / D
            second = inverse * inverse * inverse * along
            rows_t = pl.ds(pl.multiple_of(tok + i * step, step), step)
            for h in range(heads):
                part = lat_all[h, rows, :].astype(jnp.float32)
                tang = probe_ref[rows, h * own:(h + 1) * own].astype(jnp.float32)
                gain = gain_ref[:, h * own:(h + 1) * own]
                x_ref[rows, h * own:(h + 1) * own] = (part * inverse * gain).astype(jnp.bfloat16)
                x_ref[rows_t, h * own:(h + 1) * own] = (
                    (tang * inverse - part * second) * gain
                ).astype(jnp.bfloat16)

    def load(w, piece, slot):
        at = pl.ds(pl.multiple_of(piece * width, width), width)
        return pltpu.make_async_copy(
            qkv_ref.at[w, :, :, :, at], wbuf.at[slot], load_sem.at[slot]
        )

    def multiply(w, piece, slot):
        load(w, piece, slot).wait()
        weight = wbuf[slot].reshape(D, width)
        rows = 128

        @pl.loop(0, 2 * tok // rows)
        def _(i):
            at = pl.ds(pl.multiple_of(i * rows, rows), rows)
            obuf[slot, at, :] = jnp.dot(
                x_ref[at, :], weight, preferred_element_type=jnp.float32
            ).astype(jnp.bfloat16)

        at = pl.ds(pl.multiple_of(piece * width, width), width)
        store = pltpu.make_async_copy(
            obuf.at[slot], proj_ref.at[w, :, at], store_sem.at[slot]
        )
        store.start()
        store.wait()

    def fetch(q, slot):
        @pl.when(q < 2 * pieces)
        def _():
            load(q // pieces, q % pieces, slot).start()

    def work(q, slot):
        @pl.when(q < 2 * pieces)
        def _():
            multiply(q // pieces, q % pieces, slot)

    def halo(side, a):
        return pltpu.make_async_remote_copy(
            src_ref=proj_ref.at[a], dst_ref=halo_ref.at[side, a],
            send_sem=halo_send.at[side, a], recv_sem=halo_recv.at[side, a],
            device_id={"ctx": right if side == 0 else left}, device_id_type=MESH,
        )

    def halo_fill(side, a):
        return pltpu.make_async_copy(proj_ref.at[a], halo_ref.at[side, a], halo_local.at[a])

    def halo_start(a):
        @pl.when(me < n - 1)
        def _():
            halo(0, a).start()

        @pl.when(me > 0)
        def _():
            halo(1, a).start()

        @pl.when(me == 0)
        def _():
            halo_fill(0, a).start()

        @pl.when(me == n - 1)
        def _():
            halo_fill(1, a).start()

    def halo_end(a):
        @pl.when(me < n - 1)
        def _():
            halo(0, a).wait_send()
            halo(1, a).wait_recv()

        @pl.when(me > 0)
        def _():
            halo(1, a).wait_send()
            halo(0, a).wait_recv()

        @pl.when(me == 0)
        def _():
            halo_fill(0, a).wait()

        @pl.when(me == n - 1)
        def _():
            halo_fill(1, a).wait()

    begin(0)
    begin(1)
    for k in range(1, heads):
        lat_copy(k).start()

    @pl.loop(1, hops)
    def _(hop):
        advance(0, hop)
        advance(1, hop)

        @pl.when(hop == hops - 1)
        def _():
            norm()

    begin(2)
    begin(3)
    finish(0)
    finish(1)
    settle(0)
    settle(1)

    @pl.loop(1, hops)
    def _(hop):
        q = (hop - 1) * 4
        fetch(q, 0)
        fetch(q + 1, 1)
        advance(2, hop)
        work(q, 0)
        fetch(q + 2, 0)
        work(q + 1, 1)
        fetch(q + 3, 1)
        advance(3, hop)
        work(q + 2, 0)
        work(q + 3, 1)
        for a in range(2):

            @pl.when(hop == -(-(a + 1) * pieces // 4))
            def _(a=a):
                halo_start(a)

    finish(2)
    finish(3)
    settle(2)

    load(2, 0, 0).start()
    for piece in range(pieces):
        if piece + 1 < pieces:
            load(2, piece + 1, (piece + 1) % 2).start()
        multiply(2, piece, piece % 2)

    settle(3)
    halo_end(0)
    halo_end(1)
    for w in range(4):
        drain(w)
    for k in range(1, heads):
        lat_copy(k).wait_send()


def gather_and_project(latent, probe, gain, weights):
    n = lax.axis_size("ctx")
    heads = lax.axis_size("head")
    hops = n // 2 - 1
    tok, own = latent.shape
    rows, cols = weights.shape[1:]
    weights = weights.reshape(4, 2, rows // 2, cols)
    width = 256 if cols % 256 == 0 else 128
    dma = pltpu.SemaphoreType.DMA
    bf = jnp.bfloat16
    vmem = pl.BlockSpec(memory_space=pltpu.VMEM)
    anywhere = pl.BlockSpec(memory_space=pl.ANY)
    return pl.pallas_call(
        functools.partial(project_kernel, n, heads),
        out_shape=(
            jax.ShapeDtypeStruct((3, n, 2, rows // 2, cols), bf),
            jax.ShapeDtypeStruct((n, 2, rows // 2, cols), bf),
            jax.ShapeDtypeStruct((3, 2 * tok, cols), bf),
            jax.ShapeDtypeStruct((2, 2, 2 * tok, cols), bf),
        ),
        in_specs=[vmem, vmem, vmem, anywhere],
        out_specs=(anywhere,) * 4,
        scratch_shapes=[
            pltpu.VMEM((heads, tok, own), bf),
            pltpu.VMEM((2 * tok, D), bf),
            pltpu.VMEM((2, n, 2, rows // 2, width), bf),
            pltpu.VMEM((2, 2 * tok, width), bf),
            dma((4,)), dma((4, hops, 2)), dma((4, hops, 2)), dma((4, hops, 2)), dma((4, hops, 2)),
            dma((4,)), dma((4,)),
            dma((heads - 1,)), dma((heads - 1,)), dma, dma((2,)), dma((2,)),
            dma((2, 2)), dma((2, 2)), dma((2,)),
        ],
        compiler_params=pltpu.CompilerParams(
            collective_id=0, has_side_effects=True, vmem_limit_bytes=48 * MIB
        ),
    )(latent, probe, gain, weights)


def attend_kernel(tiles, mask_ref, q_ref, own_ref, low_ref, high_ref, out_ref, k_all, v_all):
    tok = tiles * TILE
    scale = HD ** (-0.5)
    for place, ref in enumerate((low_ref, own_ref, high_ref)):
        at = slice(place * tok, (place + 1) * tok)
        k_all[at, :HD] = ref[0, :tok, :]
        k_all[at, HD:] = ref[0, tok:, :]
        v_all[at, :HD] = ref[1, :tok, :]
        v_all[at, HD:] = ref[1, tok:, :]
    contract = (((1,), (1,)), ((), ()))
    band = 2 * tiles + 1
    for i in range(tiles):
        rows = slice(i * TILE, (i + 1) * TILE)
        rows_t = slice(tok + i * TILE, tok + (i + 1) * TILE)
        query = q_ref[0, rows, :]
        query_t = q_ref[0, rows_t, :]
        keys = k_all[i * TILE:(i + band) * TILE, :]
        scores = lax.dot_general(
            query, keys[:, :HD], contract, preferred_element_type=jnp.float32
        ) * scale
        scores_t = lax.dot_general(
            jnp.concatenate([query_t, query], 1), keys, contract,
            preferred_element_type=jnp.float32,
        ) * scale
        masked = jnp.concatenate(
            [
                jnp.where(
                    mask_ref[i, i + j] == 1, scores[:, j * TILE:(j + 1) * TILE], -1e30
                )
                for j in range(band)
            ],
            1,
        )
        highest = jnp.max(masked, -1, keepdims=True)
        expos = jnp.exp(masked - highest)
        probs = expos * (1.0 / jnp.sum(expos, -1, keepdims=True))
        weighed = probs * scores_t
        probs_t = weighed - probs * jnp.sum(weighed, -1, keepdims=True)
        probs_b = probs.astype(jnp.bfloat16)
        values = v_all[i * TILE:(i + band) * TILE, :]
        first = jnp.dot(probs_b, values, preferred_element_type=jnp.float32)
        second = first[:, HD:] + jnp.dot(
            probs_t.astype(jnp.bfloat16), values[:, :HD], preferred_element_type=jnp.float32
        )
        out_ref[rows, :] = first[:, :HD].astype(jnp.bfloat16)
        out_ref[rows_t, :] = second.astype(jnp.bfloat16)


def attend(tile_rows, proj, halo):
    rows, cols = proj.shape[1:]
    tok = rows // 2
    tiles = tok // TILE
    return pl.pallas_call(
        functools.partial(attend_kernel, tiles),
        grid=(cols // HD,),
        out_shape=jax.ShapeDtypeStruct((rows, cols), jnp.bfloat16),
        in_specs=[
            pl.BlockSpec(memory_space=pltpu.SMEM),
            pl.BlockSpec((1, rows, HD), lambda h: (2, 0, h)),
            pl.BlockSpec((2, rows, HD), lambda h: (0, 0, h)),
            pl.BlockSpec((None, 2, rows, HD), lambda h: (0, 0, 0, h)),
            pl.BlockSpec((None, 2, rows, HD), lambda h: (1, 0, 0, h)),
        ],
        out_specs=pl.BlockSpec((rows, HD), lambda h: (0, h)),
        scratch_shapes=[pltpu.VMEM((3 * tok, 2 * HD), jnp.bfloat16)] * 2,
        compiler_params=pltpu.CompilerParams(vmem_limit_bytes=32 * MIB),
    )(tile_rows, proj, proj, halo, halo)


def shards(latent, probe, norm_gain, w_query, w_key, w_value, w_out, tile_mask):
    tok_rows, own_cols = latent.shape
    weights = jnp.stack([w_key, w_value, w_query, w_out.T])
    _, wo_full, proj, halo = gather_and_project(latent, probe, norm_gain.reshape(1, D), weights)
    tiles_dev = tok_rows // TILE
    ctx_slot = lax.axis_index("ctx")
    mask_pad = jnp.pad(tile_mask, tiles_dev)
    tile_rows = lax.dynamic_slice(
        mask_pad,
        (ctx_slot * tiles_dev + tiles_dev, ctx_slot * tiles_dev),
        (tiles_dev, 3 * tiles_dev),
    )
    both_rows = attend(tile_rows, proj, halo)
    w_out_t = wo_full.reshape(D, w_out.shape[0])
    terms = lax.dot_general(
        both_rows, w_out_t, (((1,), (1,)), ((), ())), preferred_element_type=jnp.float32
    ).astype(jnp.bfloat16)
    summed = lax.psum_scatter(terms, "head", scatter_dimension=1, tiled=True).astype(jnp.float32)
    branch = summed[:tok_rows]
    branch_t = summed[tok_rows:]
    latent_f = latent.astype(jnp.float32)
    col_start = lax.axis_index("head") * own_cols
    tangent_own = lax.dynamic_slice_in_dim(probe, col_start, own_cols, 1).astype(jnp.float32)
    mixed = (latent_f + branch).astype(jnp.bfloat16)
    trace_terms = lax.psum(jnp.sum(tangent_own * branch_t, -1), "head")
    return (mixed, branch_t.astype(jnp.bfloat16), trace_terms)


def layer_kernel(
    layers, mask_ref, lat_ref, probe_ref, gain_ref, wk_ref, wv_ref, wq_ref, wo_ref,
    att_ref, ofull_ref, oz_ref,
    x_all, w_all, wq_all, k_all, v_all, q_all, a_all, sums, sums_in,
    in_sem, a2a_send, a2a_recv, a2a_local, z_send, z_recv, s_send, s_recv,
    n_send, n_recv, d_send, d_recv, f_send, f_recv, h_send, h_recv,
    at_send, at_recv, at_local, o_send, o_recv, o_local, of_send, of_recv,
):
    tok, own = lat_ref.shape
    cols = w_all.shape[-1]
    nheads = cols // HD
    half = wo_ref.shape[0] // 2
    me = lax.axis_index("ctx")
    y = lax.axis_index("head")
    z = me // 4
    x = (me // 2) % 2
    c = me % 2
    base = z * 4
    q = 2 * x + c
    tq = 2 * x + 1 - c
    xq = 2 * (1 - x) + c
    dq = 2 * (1 - x) + 1 - c
    heads_at = 2
    outs_at = 2 + nheads
    items = outs_at + 2
    bf = jnp.bfloat16

    def at(ctx, head):
        return {"ctx": ctx, "head": head}

    barrier = pltpu.get_barrier_semaphore()
    for k in range(4):
        for j in range(2):
            if k or j:
                pl.semaphore_signal(
                    barrier, inc=1, device_id=at(base + (q + k) % 4, (y + j) % 2),
                    device_id_type=MESH,
                )

    @pl.when(z < layers - 1)
    def _():
        pl.semaphore_signal(barrier, inc=1, device_id=at(me + 4, y), device_id_type=MESH)

    @pl.when(z > 0)
    def _():
        pl.semaphore_signal(barrier, inc=1, device_id=at(me - 4, y), device_id_type=MESH)

    def load_in(p):
        if p == 0:
            source = lat_ref
        else:
            source = probe_ref.at[:, pl.ds(pl.multiple_of(y * own, own), own)]
        return pltpu.make_async_copy(
            source, x_all.at[q, y, pl.ds(p * tok, tok)], in_sem.at[p]
        )

    load_in(0).start()
    load_in(1).start()

    def quarter(w, k):
        if w < heads_at:
            return (wk_ref, wv_ref)[w].at[:, pl.ds(pl.multiple_of(k * cols, cols), cols)]
        first = pl.multiple_of(k * cols + (w - heads_at) * HD, HD)
        return wq_ref.at[:, pl.ds(first, HD)]

    def weight_at(w, zz):
        return w_all.at[w, zz] if w < heads_at else wq_all.at[w - heads_at, zz]

    def a2a_own(w):
        return pltpu.make_async_copy(quarter(w, q), weight_at(w, z).at[q], a2a_local.at[w])

    def a2a(w, k):
        to = (q + k) % 4
        return pltpu.make_async_remote_copy(
            src_ref=quarter(w, to), dst_ref=weight_at(w, z).at[q],
            send_sem=a2a_send.at[w, k - 1], recv_sem=a2a_recv.at[w, k - 1],
            device_id=at(base + to, y), device_id_type=MESH,
        )

    def a2a_start(w):
        a2a_own(w).start()
        for k in (2, 1, 3):
            a2a(w, k).start()

    def a2a_wait(w):
        a2a_own(w).wait()
        for k in (1, 2, 3):
            came = weight_at(w, z).at[(q + 4 - k) % 4]
            pltpu.make_async_remote_copy(
                src_ref=came, dst_ref=came,
                send_sem=a2a_send.at[w, k - 1], recv_sem=a2a_recv.at[w, k - 1],
                device_id=at(base + (q + k) % 4, y), device_id_type=MESH,
            ).wait_recv()

    def region(item, zz):
        return weight_at(item, zz) if item < outs_at else oz_ref.at[zz, item - outs_at]

    def z_copy(item, way, d):
        zz = z - d if way == 0 else z + d
        block = region(item, zz)
        mine = item >= outs_at and d == 0
        return pltpu.make_async_remote_copy(
            src_ref=wo_ref.at[pl.ds((item - outs_at) * half, half)] if mine else block,
            dst_ref=block,
            send_sem=z_send.at[item, way, d], recv_sem=z_recv.at[item, way, d],
            device_id=at(me + 4 if way == 0 else me - 4, y), device_id_type=MESH,
        )

    def z_has(way, d):
        return z >= d if way == 0 else z + d <= layers - 1

    def z_sends(way, d):
        if way == 0:
            return jnp.logical_and(z >= d, z < layers - 1)
        return jnp.logical_and(z + d <= layers - 1, z > 0)

    def z_edge(way):
        return z == layers - 2 if way == 0 else z == 1

    def z_begin(item, edge=None):
        for way in range(2):
            here = z_sends(way, 0)
            if edge is not None:
                here = jnp.logical_and(here, z_edge(way) == edge)

            @pl.when(here)
            def _(way=way):
                z_copy(item, way, 0).start()

    def z_pace(item):
        for way in range(2):
            for d in range(2):

                @pl.when(jnp.logical_and(z_sends(way, d), z_edge(way)))
                def _(way=way, d=d):
                    z_copy(item, way, d).wait_send()

    def z_came(item, way, d):
        block = region(item, z - d if way == 0 else z + d)
        pltpu.make_async_remote_copy(
            src_ref=block, dst_ref=block,
            send_sem=z_send.at[item, way, d - 1], recv_sem=z_recv.at[item, way, d - 1],
            device_id=at(me + 4 if way == 0 else me - 4, y), device_id_type=MESH,
        ).wait_recv()

    def z_relay(item, d):
        for way in range(2):

            @pl.when(z_sends(way, d))
            def _(way=way):
                z_came(item, way, d)
                z_copy(item, way, d).start()

    def z_ends(way, d):
        if way == 0:
            return jnp.logical_and(z >= d, z == layers - 1)
        return jnp.logical_and(z + d <= layers - 1, z == 0)

    def z_wait(item, *dists):
        for d in dists:
            for way in range(2):

                @pl.when(z_ends(way, d))
                def _(way=way, d=d):
                    z_came(item, way, d)

    def z_drain(item, paced):
        for way in range(2):
            for d in range(layers - 1):
                here = z_sends(way, d)
                if paced and d < 2:
                    here = jnp.logical_and(here, jnp.logical_not(z_edge(way)))

                @pl.when(here)
                def _(way=way, d=d):
                    z_copy(item, way, d).wait_send()

    def part(slot, side, p):
        return x_all.at[slot, side, pl.ds(p * tok, tok)]

    twin = at(base + tq, y)
    across = at(base + xq, y)
    over = at(me, 1 - y)

    def n_copy(way, p, slot=None, side=None):
        block = part(q, y, p) if slot is None else part(slot, side, p)
        return pltpu.make_async_remote_copy(
            src_ref=block, dst_ref=block,
            send_sem=n_send.at[way, p], recv_sem=n_recv.at[way, p],
            device_id=(twin, across, over)[way], device_id_type=MESH,
        )

    def d_copy(p, landing=False):
        if landing:
            block = part(xq, 1 - y, p)
        else:
            block = part(xq, y, p) if p == 0 else part(q, 1 - y, p)
        return pltpu.make_async_remote_copy(
            src_ref=block, dst_ref=block,
            send_sem=d_send.at[p], recv_sem=d_recv.at[p],
            device_id=over if p == 0 else across, device_id_type=MESH,
        )

    def f_copy(kind, p, landing=False):
        if landing:
            block = (part(dq, y, p), part(tq, 1 - y, p), part(dq, 1 - y, p))[kind]
        else:
            block = (part(xq, y, p), part(q, 1 - y, p), part(xq, 1 - y, p))[kind]
        return pltpu.make_async_remote_copy(
            src_ref=block, dst_ref=block,
            send_sem=f_send.at[kind, p], recv_sem=f_recv.at[kind, p],
            device_id=twin, device_id_type=MESH,
        )

    def s_copy():
        return pltpu.make_async_remote_copy(
            src_ref=sums, dst_ref=sums_in, send_sem=s_send, recv_sem=s_recv,
            device_id=over, device_id_type=MESH,
        )

    step = 16

    def norm_sums():
        @pl.loop(0, tok // step)
        def _(i):
            rows = pl.ds(pl.multiple_of(i * step, step), step)
            rows_t = pl.ds(pl.multiple_of(tok + i * step, step), step)
            lat = x_all[q, y, rows, :].astype(jnp.float32)
            tang = x_all[q, y, rows_t, :].astype(jnp.float32)
            squares = jnp.sum(lat * lat, -1, keepdims=True)
            crossed = jnp.sum(lat * tang, -1, keepdims=True)
            lane = lax.broadcasted_iota(jnp.int32, (step, HD), 1)
            sums[rows, :] = jnp.where(lane < HD // 2, squares, crossed)

    def norm_apply():
        @pl.loop(0, tok // step)
        def _(i):
            rows = pl.ds(pl.multiple_of(i * step, step), step)
            rows_t = pl.ds(pl.multiple_of(tok + i * step, step), step)
            both = sums[rows, :] + sums_in[rows, :]
            inverse = lax.rsqrt(both[:, 0:1] / D + 1e-06)
            along = both[:, HD // 2:HD // 2 + 1] / D
            second = inverse * inverse * inverse * along
            lat = x_all[q, y, rows, :].astype(jnp.float32)
            tang = x_all[q, y, rows_t, :].astype(jnp.float32)
            gain = gain_ref[y]
            x_all[q, y, rows, :] = (lat * inverse * gain).astype(bf)
            x_all[q, y, rows_t, :] = ((tang * inverse - lat * second) * gain).astype(bf)

    def multiply(weight, blk, p):
        acc = None
        for side in range(2):
            rows_in = weight[pl.ds(side * (layers // 2), layers // 2)]
            term = jnp.dot(
                x_all[blk, side, pl.ds(p * tok, tok), :], rows_in.reshape(own, -1),
                preferred_element_type=jnp.float32,
            )
            acc = term if acc is None else acc + term
        return acc.astype(bf)

    def project(w, blk):
        for p in range(2):
            res = multiply(w_all.at[w], blk, p)
            rows = pl.ds(pl.multiple_of(blk * tok + tok, tok), tok)
            for h in range(nheads):
                lanes = slice((2 * h + p) * HD, (2 * h + p + 1) * HD)
                (k_all, v_all)[w][rows, lanes] = res[:, h * HD:(h + 1) * HD]

    def project_query(h, blk):
        rows = pl.ds(pl.multiple_of(blk * tok, tok), tok)

        @pl.loop(0, 2)
        def _(p):
            lanes = pl.ds(pl.multiple_of((2 * h + p) * HD, HD), HD)
            q_all[rows, lanes] = multiply(wq_all.at[h], blk, p)

    kv = (k_all, v_all)

    def halo(way, a, landing=False):
        if way == 0:
            source = pl.ds(4 * tok, tok)
            target = pl.ds(0, tok)
        else:
            source = pl.ds(tok, tok)
            target = pl.ds(5 * tok, tok)
        return pltpu.make_async_remote_copy(
            src_ref=kv[a].at[target if landing else source], dst_ref=kv[a].at[target],
            send_sem=h_send.at[way, a], recv_sem=h_recv.at[way, a],
            device_id=at(me + 4 if way == 0 else me - 4, y), device_id_type=MESH,
        )

    def halo_start(a):
        @pl.when(z < layers - 1)
        def _():
            halo(0, a).start()

        @pl.when(z > 0)
        def _():
            halo(1, a).start()

    def halo_wait(a):
        @pl.when(z > 0)
        def _():
            halo(0, a, True).wait_recv()

        @pl.when(z < layers - 1)
        def _():
            halo(1, a, True).wait_recv()

    def halo_fill():
        @pl.when(z == 0)
        def _():
            for a in range(2):
                kv[a][0:tok, :] = jnp.zeros((tok, 2 * cols), bf)

        @pl.when(z == layers - 1)
        def _():
            for a in range(2):
                kv[a][5 * tok:6 * tok, :] = jnp.zeros((tok, 2 * cols), bf)

    def halo_drain(a):
        @pl.when(z < layers - 1)
        def _():
            halo(0, a).wait_send()

        @pl.when(z > 0)
        def _():
            halo(1, a).wait_send()

    tiles = tok // TILE
    band = 2 * tiles + 1
    scale = HD ** (-0.5)
    contract = (((1,), (1,)), ((), ()))

    def hidden(tile, j):
        row = z * 4 * tiles + tile
        col = row - tiles + j
        total = layers * 4 * tiles
        inside = jnp.logical_and(col >= 0, col < total).astype(jnp.int32)
        seen = mask_ref[row, jnp.clip(col, 0, total - 1)] * inside
        return (seen - 1).astype(jnp.float32) * 1e30

    def attend_block(h, blk):
        lanes = slice(2 * h * HD, 2 * (h + 1) * HD)

        for i in range(tiles):
            tile = blk * tiles + i
            rows = pl.ds(pl.multiple_of(tile * TILE, TILE), TILE)
            span = pl.ds(pl.multiple_of(tile * TILE, TILE), band * TILE)
            query = q_all[rows, lanes]
            keys = k_all[span, lanes]
            left = jnp.concatenate(
                [
                    jnp.concatenate([query[:, :HD], query[:, HD:]], 0),
                    jnp.concatenate([jnp.zeros((TILE, HD), bf), query[:, :HD]], 0),
                ],
                1,
            )
            scores = lax.dot_general(left, keys, contract, preferred_element_type=jnp.float32)
            masked = jnp.concatenate(
                [
                    scores[:TILE, j * TILE:(j + 1) * TILE] * scale + hidden(tile, j)
                    for j in range(band)
                ],
                1,
            )
            highest = jnp.max(masked, -1, keepdims=True)
            expos = jnp.exp(masked - highest)
            probs = expos * (1.0 / jnp.sum(expos, -1, keepdims=True))
            weighed = probs * (scores[TILE:] * scale)
            probs_t = weighed - probs * jnp.sum(weighed, -1, keepdims=True)
            stacked = jnp.concatenate([probs.astype(bf), probs_t.astype(bf)], 0)
            out = jnp.dot(stacked, v_all[span, lanes], preferred_element_type=jnp.float32)
            into = slice(i * TILE, (i + 1) * TILE)
            a_all[h, blk, 0, into, :] = out[:TILE, :HD].astype(bf)
            a_all[h, blk, 1, into, :] = (out[:TILE, HD:] + out[TILE:, :HD]).astype(bf)

    def att_slot(h, head, slot):
        return att_ref.at[head, :, :, pl.ds(pl.multiple_of((slot * nheads + h) * HD, HD), HD)]

    def att_copy(h, k, j):
        blk = (q + k) % 4
        return pltpu.make_async_remote_copy(
            src_ref=a_all.at[h, blk], dst_ref=att_slot(h, y, q),
            send_sem=at_send.at[h, k, j], recv_sem=at_recv.at[h, k, j],
            device_id=at(base + blk, (y + j) % 2), device_id_type=MESH,
        )

    def att_own(h):
        return pltpu.make_async_copy(a_all.at[h, q], att_slot(h, y, q), at_local.at[h])

    def att_start(h, k, blk):
        att_copy(h, k, 1).start()

        @pl.when(k > 0)
        def _():
            att_copy(h, k, 0).start()

        @pl.when(k == 0)
        def _():
            att_own(h).start()

    def att_end(h):
        for k in range(4):
            for j in range(2):
                if k or j:
                    came = att_slot(h, (y + j) % 2, (q + 4 - k) % 4)
                    pltpu.make_async_remote_copy(
                        src_ref=came, dst_ref=came,
                        send_sem=at_send.at[h, k, j], recv_sem=at_recv.at[h, k, j],
                        device_id=at(base + (q + k) % 4, (y + j) % 2), device_id_type=MESH,
                    ).wait_recv()
                    att_copy(h, k, j).wait_send()
        att_own(h).wait()

    per = layers // 2

    def o_slot(zz, xs, cs, ys, h):
        return ofull_ref.at[zz % per, xs, cs, ys, pl.ds(h * half, half)]

    def o_source(zz, own_block, h):
        return wo_ref.at[pl.ds(h * half, half)] if own_block else oz_ref.at[zz, h]

    def o_far(zz, own_block, h):
        goal = zz // per
        return pltpu.make_async_remote_copy(
            src_ref=o_source(zz, own_block, h), dst_ref=o_slot(zz, x, c, y, h),
            send_sem=o_send.at[zz, h, 0], recv_sem=o_recv.at[zz % per, h, 1, (y + goal) % 2],
            device_id=at(base + xq, goal), device_id_type=MESH,
        )

    def o_near(zz, own_block, h):
        return pltpu.make_async_remote_copy(
            src_ref=o_source(zz, own_block, h), dst_ref=o_slot(zz, x, c, y, h),
            send_sem=o_send.at[zz, h, 1], recv_sem=o_recv.at[zz % per, h, 0, 1],
            device_id=over, device_id_type=MESH,
        )

    def o_self(zz, own_block, h):
        return pltpu.make_async_copy(
            o_source(zz, own_block, h), o_slot(zz, x, c, y, h), o_local.at[zz % per, h]
        )

    def o_give(zz, own_block, h):
        o_far(zz, own_block, h).start()

        @pl.when(zz // per == y)
        def _():
            o_self(zz, own_block, h).start()

        @pl.when(zz // per != y)
        def _():
            o_near(zz, own_block, h).start()

    def o_give_dist(d, among):
        for h in range(2):
            for way in range(2 if d else 1):

                @pl.when(among(way, d))
                def _(way=way, h=h):
                    o_give(z - d if way == 0 else z + d, d == 0, h)

    def o_drain():
        for d in range(layers):
            for h in range(2):
                for way in range(2 if d else 1):

                    @pl.when(z_has(way, d))
                    def _(way=way, h=h, d=d):
                        zz = z - d if way == 0 else z + d
                        o_far(zz, d == 0, h).wait_send()

                        @pl.when(zz // per != y)
                        def _():
                            o_near(zz, d == 0, h).wait_send()

    def o_flip(zz, h, dx, dy, landing=False):
        xs = (x + dx) % 2
        ys = (y + dy) % 2
        block = o_slot(zz, xs, 1 - c if landing else c, ys, h)
        return pltpu.make_async_remote_copy(
            src_ref=block, dst_ref=block,
            send_sem=of_send.at[zz % per, h, dx, dy], recv_sem=of_recv.at[zz % per, h, dx, dy],
            device_id=twin, device_id_type=MESH,
        )

    def o_take(zz, h):
        for dx in range(2):
            for dy in range(2):
                if dx or dy:
                    came = o_slot(zz, (x + dx) % 2, c, (y + dy) % 2, h)
                    pltpu.make_async_remote_copy(
                        src_ref=came, dst_ref=came,
                        send_sem=o_send.at[zz, h, 0], recv_sem=o_recv.at[zz % per, h, dx, dy],
                        device_id=twin, device_id_type=MESH,
                    ).wait_recv()
                else:
                    o_self(zz, False, h).wait()
                o_flip(zz, h, dx, dy).start()

    def o_take_end(zz, h):
        for dx in range(2):
            for dy in range(2):
                o_flip(zz, h, dx, dy, True).wait_recv()
                o_flip(zz, h, dx, dy).wait_send()

    ends = (z == 0).astype(jnp.int32) + (z == layers - 1).astype(jnp.int32)
    pl.semaphore_wait(barrier, 9 - ends)

    queries = [heads_at + h for h in range(nheads)]
    outs = [outs_at, outs_at + 1]
    every = range(1, layers)
    a2a_start(0)
    for w in outs:
        z_begin(w)
    load_in(0).wait()
    load_in(1).wait()
    norm_sums()
    s_copy().start()
    halo_fill()
    s_copy().wait()
    norm_apply()
    n_copy(1, 0).start()
    n_copy(2, 1).start()
    n_copy(0, 0).start()
    n_copy(0, 1).start()
    a2a_wait(0)
    z_begin(0)
    a2a_start(1)
    for w in outs:
        z_relay(w, 1)

    n_copy(1, 0, xq, y).wait_recv()
    n_copy(1, 1).start()
    f_copy(0, 0).start()
    n_copy(2, 1, q, 1 - y).wait_recv()
    n_copy(2, 0).start()
    f_copy(1, 1).start()

    z_relay(0, 1)
    for w in outs:
        z_relay(w, 2)
    a2a_wait(1)
    z_begin(1)

    n_copy(1, 1, xq, y).wait_recv()
    n_copy(2, 0, q, 1 - y).wait_recv()
    d_copy(0).start()
    d_copy(1).start()
    f_copy(0, 1).start()
    f_copy(1, 0).start()
    for w in queries:
        a2a_start(w)

    z_relay(0, 2)
    z_relay(1, 1)
    z_wait(0, *every)
    for p in range(2):
        n_copy(0, p, tq, y).wait_recv()
        f_copy(1, p, True).wait_recv()

    def project_pair(w, side):
        @pl.loop(0, 2)
        def _(j):
            project(w, 2 * side + j)

    project_pair(0, x)
    z_relay(1, 2)
    for p in range(2):
        d_copy(p, True).wait_recv()
        f_copy(2, p).start()
    for w in outs:
        z_wait(w, *every)
    for d in range(layers):
        o_give_dist(d, z_has)
    for w in queries:
        a2a_wait(w)
        z_begin(w, False)
    for p in range(2):
        f_copy(0, p, True).wait_recv()
        f_copy(2, p, True).wait_recv()
    project_pair(0, 1 - x)
    halo_start(0)
    z_wait(1, *every)
    project_pair(1, x)
    project_pair(1, 1 - x)
    halo_start(1)

    def o_take_all(early):
        for n in range(per):
            zz = per * y + n
            close = jnp.logical_and(zz - z <= 1, z - zz <= 1)

            @pl.when(close if early else jnp.logical_not(close))
            def _(zz=zz):
                for h in range(2):
                    o_take(zz, h)

    for h in range(nheads):
        if h:
            z_pace(queries[h - 1])
        z_begin(queries[h], True)
        for d in every[:-1]:
            z_relay(queries[h], d)
        if h == 0:
            halo_wait(0)
            halo_wait(1)
        z_wait(queries[h], *every)
        @pl.loop(0, 4)
        def _(n, h=h):
            k = 3 - n
            blk = (q + k) % 4
            project_query(h, blk)
            attend_block(h, blk)
            att_start(h, k, blk)

        if h < 2:
            o_take_all(h == 0)
    for h in range(nheads):
        att_end(h)
    for zz in range(per):
        for h in range(2):
            o_take_end(per * y + zz, h)
    for w in range(outs_at):
        for k in (1, 2, 3):
            a2a(w, k).wait_send()
    for item in range(items):
        z_drain(item, item in queries[:-1])
    for p in range(2):
        for way in range(3):
            n_copy(way, p).wait_send()
        d_copy(p).wait_send()
        for kind in range(3):
            f_copy(kind, p).wait_send()
    halo_drain(0)
    halo_drain(1)
    o_drain()


def run_layers(tile_mask, latent, probe, gain, wk, wv, wq, wo):
    layers = lax.axis_size("ctx") // 4
    tok, own = latent.shape
    rows, width = wk.shape
    cols = width // 4
    nheads = cols // HD
    half = rows // 2
    dma = pltpu.SemaphoreType.DMA
    bf = jnp.bfloat16
    vmem = pl.BlockSpec(memory_space=pltpu.VMEM)
    smem = pl.BlockSpec(memory_space=pltpu.SMEM)
    anywhere = pl.BlockSpec(memory_space=pl.ANY)
    return pl.pallas_call(
        functools.partial(layer_kernel, layers),
        out_shape=(
            jax.ShapeDtypeStruct((2, 2, tok, width), bf),
            jax.ShapeDtypeStruct((layers // 2, 2, 2, 2, rows, width), bf),
            jax.ShapeDtypeStruct((layers, 2, half, width), bf),
        ),
        in_specs=[smem, anywhere, anywhere, vmem] + [anywhere] * 4,
        out_specs=(anywhere,) * 3,
        scratch_shapes=[
            pltpu.VMEM((4, 2, 2 * tok, own), bf),
            pltpu.VMEM((2, layers, 4, rows, cols), bf),
            pltpu.VMEM((nheads, layers, 4, rows, HD), bf),
            pltpu.VMEM((6 * tok, 2 * cols), bf),
            pltpu.VMEM((6 * tok, 2 * cols), bf),
            pltpu.VMEM((4 * tok, 2 * cols), bf),
            pltpu.VMEM((nheads, 4, 2, tok, HD), bf),
            pltpu.VMEM((tok, HD), jnp.float32),
            pltpu.VMEM((tok, HD), jnp.float32),
            dma((2,)), dma((2 + nheads, 3)), dma((2 + nheads, 3)), dma((2 + nheads,)),
            dma((4 + nheads, 2, layers - 1)), dma((4 + nheads, 2, layers - 1)), dma, dma,
            dma((3, 2)), dma((3, 2)), dma((2,)), dma((2,)), dma((3, 2)), dma((3, 2)),
            dma((2, 2)), dma((2, 2)),
            dma((nheads, 4, 2)), dma((nheads, 4, 2)), dma((nheads,)),
            dma((layers, 2, 2)), dma((layers // 2, 2, 2, 2)), dma((layers // 2, 2)),
            dma((layers // 2, 2, 2, 2)), dma((layers // 2, 2, 2, 2)),
        ],
        compiler_params=pltpu.CompilerParams(
            collective_id=0, has_side_effects=True, vmem_limit_bytes=60 * MIB
        ),
    )(tile_mask, latent, probe, gain, wk, wv, wq, wo)


def finish_kernel(head_ref, att_ref, o_ref, lat_ref, probe_ref, mixed_ref, tang_ref, trace_ref):
    tok, chunk = lat_ref.shape
    contract = (((1,), (1,)), ((), ()))
    branch = None
    for ys in range(2):
        weight = o_ref[:, ys].reshape(chunk, o_ref.shape[-1])
        lhs = att_ref[ys].reshape(2 * tok, att_ref.shape[-1])
        term = lax.dot_general(lhs, weight, contract, preferred_element_type=jnp.float32)
        term = term.astype(jnp.bfloat16).astype(jnp.float32)
        branch = term if branch is None else branch + term
    branch_t = branch[tok:]
    mixed_ref[...] = (lat_ref[...].astype(jnp.float32) + branch[:tok]).astype(jnp.bfloat16)
    tang_ref[...] = branch_t.astype(jnp.bfloat16)
    terms = jnp.sum(probe_ref[...].astype(jnp.float32) * branch_t, -1, keepdims=True)

    @pl.when(pl.program_id(0) == 0)
    def _():
        trace_ref[...] = jnp.zeros_like(trace_ref)

    trace_ref[...] += jnp.broadcast_to(terms, trace_ref.shape)


def finish(att, ofull, latent, probe):
    tok, own = latent.shape
    per, _, _, _, rows, width = ofull.shape
    steps = 2 * per
    chunk = own // steps
    blocks = ofull.reshape(steps, 2, 2, rows, width)
    return pl.pallas_call(
        finish_kernel,
        grid_spec=pltpu.PrefetchScalarGridSpec(
            num_scalar_prefetch=1,
            grid=(steps,),
            in_specs=[
                pl.BlockSpec((2, 2, tok, width), lambda i, h: (0, 0, 0, 0)),
                pl.BlockSpec((None, 2, 2, rows, width), lambda i, h: (i, 0, 0, 0, 0)),
                pl.BlockSpec((tok, chunk), lambda i, h: (0, i)),
                pl.BlockSpec((tok, chunk), lambda i, h: (0, h[0] * steps + i)),
            ],
            out_specs=[
                pl.BlockSpec((tok, chunk), lambda i, h: (0, i)),
                pl.BlockSpec((tok, chunk), lambda i, h: (0, i)),
                pl.BlockSpec((tok, HD), lambda i, h: (0, 0)),
            ],
        ),
        out_shape=(
            jax.ShapeDtypeStruct((tok, own), jnp.bfloat16),
            jax.ShapeDtypeStruct((tok, own), jnp.bfloat16),
            jax.ShapeDtypeStruct((tok, HD), jnp.float32),
        ),
        compiler_params=pltpu.CompilerParams(vmem_limit_bytes=48 * MIB),
    )(lax.axis_index("head").reshape(1), att, blocks, latent, probe)


def layer_shards(latent, probe, norm_gain, w_query, w_key, w_value, w_out, tile_mask):
    att, ofull, _ = run_layers(
        tile_mask, latent, probe, norm_gain.reshape(2, 1, D // 2),
        w_key, w_value, w_query, w_out.T,
    )
    mixed, tangent, trace = finish(att, ofull, latent, probe)
    return (mixed, tangent, lax.psum(trace[:, 0], "head"))


def solution(mesh):
    placed = (
        P("ctx", "head"),
        P("ctx", None),
        P(),
        P("ctx", "head"),
        P("ctx", "head"),
        P("ctx", "head"),
        P("head", "ctx"),
        P(),
    )
    by_layer = mesh.shape["ctx"] == 16 and mesh.shape["head"] == 2
    return jax.shard_map(
        layer_shards if by_layer else shards,
        mesh=mesh,
        in_specs=placed,
        out_specs=(P("ctx", "head"), P("ctx", "head"), P("ctx")),
        check_vma=False,
    )
```

```python
import functools

import jax
import jax.numpy as jnp
from jax import lax
from jax.experimental import pallas as pl
from jax.experimental.pallas import tpu as pltpu
from jax.sharding import PartitionSpec as P

D = 5120
HD = 128
TILE = 128
MESH = pl.DeviceIdType.MESH
MIB = 1 << 20


def chip_of(pos, chips):
    half = pos // (chips // 2)
    return (1 - half) * 2 * pos + half * (2 * (chips - 1 - pos) + 1)


def project_kernel(
    n, heads, lat_ref, probe_ref, gain_ref, w_ref,
    qkv_ref, wo_ref, proj_ref, halo_ref,
    lat_all, x_ref, wbuf, obuf,
    local_sem, ring_send, ring_recv, flip_send, flip_recv, own_send, own_recv,
    lat_send, lat_recv, lat_local, load_sem, store_sem, halo_send, halo_recv, halo_local,
):
    chips = n // 2
    hops = chips - 1
    tok, own = lat_ref.shape
    cols = proj_ref.shape[-1]
    width = wbuf.shape[-1]
    pieces = cols // width
    me = lax.axis_index("ctx")
    head = lax.axis_index("head")
    core = me % 2
    chip = me // 2
    cx = chip % 2
    cz = chip // 2
    pos = (1 - cx) * cz + cx * (chips - 1 - cz)
    ahead = chip_of((pos + 1) % chips, chips) * 2 + core
    behind = chip_of((pos + chips - 1) % chips, chips) * 2 + core
    twin = me + 1 - 2 * core
    right = (me + 1) % n
    left = (me + n - 1) % n

    barrier = pltpu.get_barrier_semaphore()
    for other in (ahead, behind, twin, right, left):
        pl.semaphore_signal(barrier, inc=1, device_id={"ctx": other}, device_id_type=MESH)
    for k in range(1, heads):
        pl.semaphore_signal(
            barrier, inc=1, device_id={"head": (head + k) % heads}, device_id_type=MESH
        )

    def full(w):
        return wo_ref if w == 3 else qkv_ref.at[w]

    def local_copy(w):
        return pltpu.make_async_copy(w_ref.at[w], full(w).at[me], local_sem.at[w])

    for w in range(4):
        local_copy(w).start()
    mine = pltpu.make_async_copy(lat_ref, lat_all.at[head], lat_local)
    mine.start()
    pl.semaphore_wait(barrier, 5 + heads - 1)

    def ring(w, hop, way, first=False):
        source = (pos + chips - hop) % chips if way == 0 else (pos + hop) % chips
        owner = chip_of(source, chips) * 2 + core
        block = full(w).at[owner, way]
        return pltpu.make_async_remote_copy(
            src_ref=w_ref.at[w, way] if first else block, dst_ref=block,
            send_sem=ring_send.at[w, hop, way], recv_sem=ring_recv.at[w, hop, way],
            device_id={"ctx": ahead if way == 0 else behind}, device_id_type=MESH,
        )

    def arrived(w, hop, way):
        source = (pos + chips - hop - 1) % chips if way == 0 else (pos + hop + 1) % chips
        return full(w).at[chip_of(source, chips) * 2 + core, way]

    def ring_wait(w, hop, way):
        block = arrived(w, hop, way)
        pltpu.make_async_remote_copy(
            src_ref=block, dst_ref=block,
            send_sem=ring_send.at[w, hop, way], recv_sem=ring_recv.at[w, hop, way],
            device_id={"ctx": ahead if way == 0 else behind}, device_id_type=MESH,
        ).wait_recv()

    def flip(w, hop, way):
        block = arrived(w, hop, way)
        return pltpu.make_async_remote_copy(
            src_ref=block, dst_ref=block,
            send_sem=flip_send.at[w, hop, way], recv_sem=flip_recv.at[w, hop, way],
            device_id={"ctx": twin}, device_id_type=MESH,
        )

    def flip_wait(w, hop, way):
        source = (pos + chips - hop - 1) % chips if way == 0 else (pos + hop + 1) % chips
        block = full(w).at[chip_of(source, chips) * 2 + 1 - core, way]
        pltpu.make_async_remote_copy(
            src_ref=block, dst_ref=block,
            send_sem=flip_send.at[w, hop, way], recv_sem=flip_recv.at[w, hop, way],
            device_id={"ctx": twin}, device_id_type=MESH,
        ).wait_recv()

    def own_flip(w, who):
        return pltpu.make_async_remote_copy(
            src_ref=w_ref.at[w], dst_ref=full(w).at[who],
            send_sem=own_send.at[w], recv_sem=own_recv.at[w],
            device_id={"ctx": twin}, device_id_type=MESH,
        )

    def begin(w):
        ring(w, 0, 0, True).start()
        ring(w, 0, 1, True).start()
        own_flip(w, me).start()

    def advance(w, hop):
        for way in range(2):
            ring_wait(w, hop - 1, way)
            ring(w, hop, way).start()
            flip(w, hop - 1, way).start()

    def finish(w):
        for way in range(2):
            ring_wait(w, hops - 1, way)
            flip(w, hops - 1, way).start()

    def settle(w):
        local_copy(w).wait()
        own_flip(w, twin).wait_recv()

        @pl.loop(0, hops)
        def _(hop):
            for way in range(2):
                flip_wait(w, hop, way)

    def drain(w):
        own_flip(w, me).wait_send()

        @pl.loop(0, hops)
        def _(hop):
            for way in range(2):
                ring(w, hop, way).wait_send()
                flip(w, hop, way).wait_send()

    def lat_copy(k):
        return pltpu.make_async_remote_copy(
            src_ref=lat_ref, dst_ref=lat_all.at[head],
            send_sem=lat_send.at[k - 1], recv_sem=lat_recv.at[k - 1],
            device_id={"head": (head + k) % heads}, device_id_type=MESH,
        )

    def norm():
        mine.wait()
        for k in range(1, heads):
            came = lat_all.at[(head + heads - k) % heads]
            pltpu.make_async_remote_copy(
                src_ref=lat_ref, dst_ref=came,
                send_sem=lat_send.at[k - 1], recv_sem=lat_recv.at[k - 1],
                device_id={"head": (head + k) % heads}, device_id_type=MESH,
            ).wait_recv()
        step = 16

        @pl.loop(0, tok // step)
        def _(i):
            rows = pl.ds(pl.multiple_of(i * step, step), step)
            squares = jnp.zeros((step, 1), jnp.float32)
            crossed = jnp.zeros((step, 1), jnp.float32)
            for h in range(heads):
                part = lat_all[h, rows, :].astype(jnp.float32)
                tang = probe_ref[rows, h * own:(h + 1) * own].astype(jnp.float32)
                squares = squares + jnp.sum(part * part, -1, keepdims=True)
                crossed = crossed + jnp.sum(part * tang, -1, keepdims=True)
            inverse = lax.rsqrt(squares / D + 1e-06)
            along = crossed / D
            second = inverse * inverse * inverse * along
            rows_t = pl.ds(pl.multiple_of(tok + i * step, step), step)
            for h in range(heads):
                part = lat_all[h, rows, :].astype(jnp.float32)
                tang = probe_ref[rows, h * own:(h + 1) * own].astype(jnp.float32)
                gain = gain_ref[:, h * own:(h + 1) * own]
                x_ref[rows, h * own:(h + 1) * own] = (part * inverse * gain).astype(jnp.bfloat16)
                x_ref[rows_t, h * own:(h + 1) * own] = (
                    (tang * inverse - part * second) * gain
                ).astype(jnp.bfloat16)

    def load(w, piece, slot):
        at = pl.ds(pl.multiple_of(piece * width, width), width)
        return pltpu.make_async_copy(
            qkv_ref.at[w, :, :, :, at], wbuf.at[slot], load_sem.at[slot]
        )

    def multiply(w, piece, slot):
        load(w, piece, slot).wait()
        weight = wbuf[slot].reshape(D, width)
        rows = 128

        @pl.loop(0, 2 * tok // rows)
        def _(i):
            at = pl.ds(pl.multiple_of(i * rows, rows), rows)
            obuf[slot, at, :] = jnp.dot(
                x_ref[at, :], weight, preferred_element_type=jnp.float32
            ).astype(jnp.bfloat16)

        at = pl.ds(pl.multiple_of(piece * width, width), width)
        store = pltpu.make_async_copy(
            obuf.at[slot], proj_ref.at[w, :, at], store_sem.at[slot]
        )
        store.start()
        store.wait()

    def fetch(q, slot):
        @pl.when(q < 2 * pieces)
        def _():
            load(q // pieces, q % pieces, slot).start()

    def work(q, slot):
        @pl.when(q < 2 * pieces)
        def _():
            multiply(q // pieces, q % pieces, slot)

    def halo(side, a):
        return pltpu.make_async_remote_copy(
            src_ref=proj_ref.at[a], dst_ref=halo_ref.at[side, a],
            send_sem=halo_send.at[side, a], recv_sem=halo_recv.at[side, a],
            device_id={"ctx": right if side == 0 else left}, device_id_type=MESH,
        )

    def halo_fill(side, a):
        return pltpu.make_async_copy(proj_ref.at[a], halo_ref.at[side, a], halo_local.at[a])

    def halo_start(a):
        @pl.when(me < n - 1)
        def _():
            halo(0, a).start()

        @pl.when(me > 0)
        def _():
            halo(1, a).start()

        @pl.when(me == 0)
        def _():
            halo_fill(0, a).start()

        @pl.when(me == n - 1)
        def _():
            halo_fill(1, a).start()

    def halo_end(a):
        @pl.when(me < n - 1)
        def _():
            halo(0, a).wait_send()
            halo(1, a).wait_recv()

        @pl.when(me > 0)
        def _():
            halo(1, a).wait_send()
            halo(0, a).wait_recv()

        @pl.when(me == 0)
        def _():
            halo_fill(0, a).wait()

        @pl.when(me == n - 1)
        def _():
            halo_fill(1, a).wait()

    begin(0)
    begin(1)
    for k in range(1, heads):
        lat_copy(k).start()

    @pl.loop(1, hops)
    def _(hop):
        advance(0, hop)
        advance(1, hop)

        @pl.when(hop == hops - 1)
        def _():
            norm()

    begin(2)
    begin(3)
    finish(0)
    finish(1)
    settle(0)
    settle(1)

    @pl.loop(1, hops)
    def _(hop):
        q = (hop - 1) * 4
        fetch(q, 0)
        fetch(q + 1, 1)
        advance(2, hop)
        work(q, 0)
        fetch(q + 2, 0)
        work(q + 1, 1)
        fetch(q + 3, 1)
        advance(3, hop)
        work(q + 2, 0)
        work(q + 3, 1)
        for a in range(2):

            @pl.when(hop == -(-(a + 1) * pieces // 4))
            def _(a=a):
                halo_start(a)

    finish(2)
    finish(3)
    settle(2)

    load(2, 0, 0).start()
    for piece in range(pieces):
        if piece + 1 < pieces:
            load(2, piece + 1, (piece + 1) % 2).start()
        multiply(2, piece, piece % 2)

    settle(3)
    halo_end(0)
    halo_end(1)
    for w in range(4):
        drain(w)
    for k in range(1, heads):
        lat_copy(k).wait_send()


def gather_and_project(latent, probe, gain, weights):
    n = lax.axis_size("ctx")
    heads = lax.axis_size("head")
    hops = n // 2 - 1
    tok, own = latent.shape
    rows, cols = weights.shape[1:]
    weights = weights.reshape(4, 2, rows // 2, cols)
    width = 256 if cols % 256 == 0 else 128
    dma = pltpu.SemaphoreType.DMA
    bf = jnp.bfloat16
    vmem = pl.BlockSpec(memory_space=pltpu.VMEM)
    anywhere = pl.BlockSpec(memory_space=pl.ANY)
    return pl.pallas_call(
        functools.partial(project_kernel, n, heads),
        out_shape=(
            jax.ShapeDtypeStruct((3, n, 2, rows // 2, cols), bf),
            jax.ShapeDtypeStruct((n, 2, rows // 2, cols), bf),
            jax.ShapeDtypeStruct((3, 2 * tok, cols), bf),
            jax.ShapeDtypeStruct((2, 2, 2 * tok, cols), bf),
        ),
        in_specs=[vmem, vmem, vmem, anywhere],
        out_specs=(anywhere,) * 4,
        scratch_shapes=[
            pltpu.VMEM((heads, tok, own), bf),
            pltpu.VMEM((2 * tok, D), bf),
            pltpu.VMEM((2, n, 2, rows // 2, width), bf),
            pltpu.VMEM((2, 2 * tok, width), bf),
            dma((4,)), dma((4, hops, 2)), dma((4, hops, 2)), dma((4, hops, 2)), dma((4, hops, 2)),
            dma((4,)), dma((4,)),
            dma((heads - 1,)), dma((heads - 1,)), dma, dma((2,)), dma((2,)),
            dma((2, 2)), dma((2, 2)), dma((2,)),
        ],
        compiler_params=pltpu.CompilerParams(
            collective_id=0, has_side_effects=True, vmem_limit_bytes=48 * MIB
        ),
    )(latent, probe, gain, weights)


def attend_kernel(tiles, mask_ref, q_ref, own_ref, low_ref, high_ref, out_ref, k_all, v_all):
    tok = tiles * TILE
    scale = HD ** (-0.5)
    for place, ref in enumerate((low_ref, own_ref, high_ref)):
        at = slice(place * tok, (place + 1) * tok)
        k_all[at, :HD] = ref[0, :tok, :]
        k_all[at, HD:] = ref[0, tok:, :]
        v_all[at, :HD] = ref[1, :tok, :]
        v_all[at, HD:] = ref[1, tok:, :]
    contract = (((1,), (1,)), ((), ()))
    band = 2 * tiles + 1
    for i in range(tiles):
        rows = slice(i * TILE, (i + 1) * TILE)
        rows_t = slice(tok + i * TILE, tok + (i + 1) * TILE)
        query = q_ref[0, rows, :]
        query_t = q_ref[0, rows_t, :]
        keys = k_all[i * TILE:(i + band) * TILE, :]
        scores = lax.dot_general(
            query, keys[:, :HD], contract, preferred_element_type=jnp.float32
        ) * scale
        scores_t = lax.dot_general(
            jnp.concatenate([query_t, query], 1), keys, contract,
            preferred_element_type=jnp.float32,
        ) * scale
        masked = jnp.concatenate(
            [
                jnp.where(
                    mask_ref[i, i + j] == 1, scores[:, j * TILE:(j + 1) * TILE], -1e30
                )
                for j in range(band)
            ],
            1,
        )
        highest = jnp.max(masked, -1, keepdims=True)
        expos = jnp.exp(masked - highest)
        probs = expos * (1.0 / jnp.sum(expos, -1, keepdims=True))
        weighed = probs * scores_t
        probs_t = weighed - probs * jnp.sum(weighed, -1, keepdims=True)
        probs_b = probs.astype(jnp.bfloat16)
        values = v_all[i * TILE:(i + band) * TILE, :]
        first = jnp.dot(probs_b, values, preferred_element_type=jnp.float32)
        second = first[:, HD:] + jnp.dot(
            probs_t.astype(jnp.bfloat16), values[:, :HD], preferred_element_type=jnp.float32
        )
        out_ref[rows, :] = first[:, :HD].astype(jnp.bfloat16)
        out_ref[rows_t, :] = second.astype(jnp.bfloat16)


def attend(tile_rows, proj, halo):
    rows, cols = proj.shape[1:]
    tok = rows // 2
    tiles = tok // TILE
    return pl.pallas_call(
        functools.partial(attend_kernel, tiles),
        grid=(cols // HD,),
        out_shape=jax.ShapeDtypeStruct((rows, cols), jnp.bfloat16),
        in_specs=[
            pl.BlockSpec(memory_space=pltpu.SMEM),
            pl.BlockSpec((1, rows, HD), lambda h: (2, 0, h)),
            pl.BlockSpec((2, rows, HD), lambda h: (0, 0, h)),
            pl.BlockSpec((None, 2, rows, HD), lambda h: (0, 0, 0, h)),
            pl.BlockSpec((None, 2, rows, HD), lambda h: (1, 0, 0, h)),
        ],
        out_specs=pl.BlockSpec((rows, HD), lambda h: (0, h)),
        scratch_shapes=[pltpu.VMEM((3 * tok, 2 * HD), jnp.bfloat16)] * 2,
        compiler_params=pltpu.CompilerParams(vmem_limit_bytes=32 * MIB),
    )(tile_rows, proj, proj, halo, halo)


def shards(latent, probe, norm_gain, w_query, w_key, w_value, w_out, tile_mask):
    tok_rows, own_cols = latent.shape
    weights = jnp.stack([w_key, w_value, w_query, w_out.T])
    _, wo_full, proj, halo = gather_and_project(latent, probe, norm_gain.reshape(1, D), weights)
    tiles_dev = tok_rows // TILE
    ctx_slot = lax.axis_index("ctx")
    mask_pad = jnp.pad(tile_mask, tiles_dev)
    tile_rows = lax.dynamic_slice(
        mask_pad,
        (ctx_slot * tiles_dev + tiles_dev, ctx_slot * tiles_dev),
        (tiles_dev, 3 * tiles_dev),
    )
    both_rows = attend(tile_rows, proj, halo)
    w_out_t = wo_full.reshape(D, w_out.shape[0])
    terms = lax.dot_general(
        both_rows, w_out_t, (((1,), (1,)), ((), ())), preferred_element_type=jnp.float32
    ).astype(jnp.bfloat16)
    summed = lax.psum_scatter(terms, "head", scatter_dimension=1, tiled=True).astype(jnp.float32)
    branch = summed[:tok_rows]
    branch_t = summed[tok_rows:]
    latent_f = latent.astype(jnp.float32)
    col_start = lax.axis_index("head") * own_cols
    tangent_own = lax.dynamic_slice_in_dim(probe, col_start, own_cols, 1).astype(jnp.float32)
    mixed = (latent_f + branch).astype(jnp.bfloat16)
    trace_terms = lax.psum(jnp.sum(tangent_own * branch_t, -1), "head")
    return (mixed, branch_t.astype(jnp.bfloat16), trace_terms)


def layer_kernel(
    layers, mask_ref, lat_ref, probe_ref, gain_ref, wk_ref, wv_ref, wq_ref, wo_ref,
    att_ref, ofull_ref, oz_ref,
    x_all, w_all, wq_all, k_all, v_all, q_blk, q_part, a_all, sums, sums_in,
    in_sem, a2a_send, a2a_recv, a2a_local, z_send, z_recv, s_send, s_recv,
    n_send, n_recv, d_send, d_recv, f_send, f_recv, h_send, h_recv,
    at_send, at_recv, at_local, o_send, o_recv, o_local, of_send, of_recv,
):
    tok, own = lat_ref.shape
    cols = w_all.shape[-1]
    nheads = cols // HD
    half = wo_ref.shape[0] // 2
    me = lax.axis_index("ctx")
    y = lax.axis_index("head")
    z = me // 4
    x = (me // 2) % 2
    c = me % 2
    base = z * 4
    q = 2 * x + c
    tq = 2 * x + 1 - c
    xq = 2 * (1 - x) + c
    dq = 2 * (1 - x) + 1 - c
    heads_at = 2
    outs_at = 2 + nheads
    items = outs_at + 2
    bf = jnp.bfloat16

    def at(ctx, head):
        return {"ctx": ctx, "head": head}

    barrier = pltpu.get_barrier_semaphore()
    for k in range(4):
        for j in range(2):
            if k or j:
                pl.semaphore_signal(
                    barrier, inc=1, device_id=at(base + (q + k) % 4, (y + j) % 2),
                    device_id_type=MESH,
                )

    @pl.when(z < layers - 1)
    def _():
        pl.semaphore_signal(barrier, inc=1, device_id=at(me + 4, y), device_id_type=MESH)

    @pl.when(z > 0)
    def _():
        pl.semaphore_signal(barrier, inc=1, device_id=at(me - 4, y), device_id_type=MESH)

    def load_in(p):
        if p == 0:
            source = lat_ref
        else:
            source = probe_ref.at[:, pl.ds(pl.multiple_of(y * own, own), own)]
        return pltpu.make_async_copy(
            source, x_all.at[q, y, pl.ds(p * tok, tok)], in_sem.at[p]
        )

    load_in(0).start()
    load_in(1).start()

    def quarter(w, k):
        if w < heads_at:
            return (wk_ref, wv_ref)[w].at[:, pl.ds(pl.multiple_of(k * cols, cols), cols)]
        first = pl.multiple_of(k * cols + (w - heads_at) * HD, HD)
        return wq_ref.at[:, pl.ds(first, HD)]

    def weight_at(w, zz):
        return w_all.at[w, zz] if w < heads_at else wq_all.at[w - heads_at, zz]

    def a2a_own(w):
        return pltpu.make_async_copy(quarter(w, q), weight_at(w, z).at[q], a2a_local.at[w])

    def a2a(w, k):
        to = (q + k) % 4
        return pltpu.make_async_remote_copy(
            src_ref=quarter(w, to), dst_ref=weight_at(w, z).at[q],
            send_sem=a2a_send.at[w, k - 1], recv_sem=a2a_recv.at[w, k - 1],
            device_id=at(base + to, y), device_id_type=MESH,
        )

    def a2a_start(w):
        a2a_own(w).start()
        for k in (2, 1, 3):
            a2a(w, k).start()

    def a2a_wait(w):
        a2a_own(w).wait()
        for k in (1, 2, 3):
            came = weight_at(w, z).at[(q + 4 - k) % 4]
            pltpu.make_async_remote_copy(
                src_ref=came, dst_ref=came,
                send_sem=a2a_send.at[w, k - 1], recv_sem=a2a_recv.at[w, k - 1],
                device_id=at(base + (q + k) % 4, y), device_id_type=MESH,
            ).wait_recv()

    def region(item, zz):
        return weight_at(item, zz) if item < outs_at else oz_ref.at[zz, item - outs_at]

    def z_copy(item, way, d):
        zz = z - d if way == 0 else z + d
        block = region(item, zz)
        mine = item >= outs_at and d == 0
        return pltpu.make_async_remote_copy(
            src_ref=wo_ref.at[pl.ds((item - outs_at) * half, half)] if mine else block,
            dst_ref=block,
            send_sem=z_send.at[item, way, d], recv_sem=z_recv.at[item, way, d],
            device_id=at(me + 4 if way == 0 else me - 4, y), device_id_type=MESH,
        )

    def z_has(way, d):
        return z >= d if way == 0 else z + d <= layers - 1

    def z_sends(way, d):
        if way == 0:
            return jnp.logical_and(z >= d, z < layers - 1)
        return jnp.logical_and(z + d <= layers - 1, z > 0)

    def z_edge(way):
        return z == layers - 2 if way == 0 else z == 1

    def z_begin(item, edge=None):
        for way in range(2):
            here = z_sends(way, 0)
            if edge is not None:
                here = jnp.logical_and(here, z_edge(way) == edge)

            @pl.when(here)
            def _(way=way):
                z_copy(item, way, 0).start()

    def z_pace(item):
        for way in range(2):
            for d in range(2):

                @pl.when(jnp.logical_and(z_sends(way, d), z_edge(way)))
                def _(way=way, d=d):
                    z_copy(item, way, d).wait_send()

    def z_came(item, way, d):
        block = region(item, z - d if way == 0 else z + d)
        pltpu.make_async_remote_copy(
            src_ref=block, dst_ref=block,
            send_sem=z_send.at[item, way, d - 1], recv_sem=z_recv.at[item, way, d - 1],
            device_id=at(me + 4 if way == 0 else me - 4, y), device_id_type=MESH,
        ).wait_recv()

    def z_relay(item, d):
        for way in range(2):

            @pl.when(z_sends(way, d))
            def _(way=way):
                z_came(item, way, d)
                z_copy(item, way, d).start()

    def z_ends(way, d):
        if way == 0:
            return jnp.logical_and(z >= d, z == layers - 1)
        return jnp.logical_and(z + d <= layers - 1, z == 0)

    def z_wait(item, *dists):
        for d in dists:
            for way in range(2):

                @pl.when(z_ends(way, d))
                def _(way=way, d=d):
                    z_came(item, way, d)

    def z_drain(item, paced):
        for way in range(2):
            for d in range(layers - 1):
                here = z_sends(way, d)
                if paced and d < 2:
                    here = jnp.logical_and(here, jnp.logical_not(z_edge(way)))

                @pl.when(here)
                def _(way=way, d=d):
                    z_copy(item, way, d).wait_send()

    def part(slot, side, p):
        return x_all.at[slot, side, pl.ds(p * tok, tok)]

    twin = at(base + tq, y)
    across = at(base + xq, y)
    over = at(me, 1 - y)

    def n_copy(way, p, slot=None, side=None):
        block = part(q, y, p) if slot is None else part(slot, side, p)
        return pltpu.make_async_remote_copy(
            src_ref=block, dst_ref=block,
            send_sem=n_send.at[way, p], recv_sem=n_recv.at[way, p],
            device_id=(twin, across, over)[way], device_id_type=MESH,
        )

    def d_copy(p, landing=False):
        if landing:
            block = part(xq, 1 - y, p)
        else:
            block = part(xq, y, p) if p == 0 else part(q, 1 - y, p)
        return pltpu.make_async_remote_copy(
            src_ref=block, dst_ref=block,
            send_sem=d_send.at[p], recv_sem=d_recv.at[p],
            device_id=over if p == 0 else across, device_id_type=MESH,
        )

    def f_copy(kind, p, landing=False):
        if landing:
            block = (part(dq, y, p), part(tq, 1 - y, p), part(dq, 1 - y, p))[kind]
        else:
            block = (part(xq, y, p), part(q, 1 - y, p), part(xq, 1 - y, p))[kind]
        return pltpu.make_async_remote_copy(
            src_ref=block, dst_ref=block,
            send_sem=f_send.at[kind, p], recv_sem=f_recv.at[kind, p],
            device_id=twin, device_id_type=MESH,
        )

    def s_copy():
        return pltpu.make_async_remote_copy(
            src_ref=sums, dst_ref=sums_in, send_sem=s_send, recv_sem=s_recv,
            device_id=over, device_id_type=MESH,
        )

    step = 16

    def norm_sums():
        @pl.loop(0, tok // step)
        def _(i):
            rows = pl.ds(pl.multiple_of(i * step, step), step)
            rows_t = pl.ds(pl.multiple_of(tok + i * step, step), step)
            lat = x_all[q, y, rows, :].astype(jnp.float32)
            tang = x_all[q, y, rows_t, :].astype(jnp.float32)
            squares = jnp.sum(lat * lat, -1, keepdims=True)
            crossed = jnp.sum(lat * tang, -1, keepdims=True)
            lane = lax.broadcasted_iota(jnp.int32, (step, HD), 1)
            sums[rows, :] = jnp.where(lane < HD // 2, squares, crossed)

    def norm_apply():
        @pl.loop(0, tok // step)
        def _(i):
            rows = pl.ds(pl.multiple_of(i * step, step), step)
            rows_t = pl.ds(pl.multiple_of(tok + i * step, step), step)
            both = sums[rows, :] + sums_in[rows, :]
            inverse = lax.rsqrt(both[:, 0:1] / D + 1e-06)
            along = both[:, HD // 2:HD // 2 + 1] / D
            second = inverse * inverse * inverse * along
            lat = x_all[q, y, rows, :].astype(jnp.float32)
            tang = x_all[q, y, rows_t, :].astype(jnp.float32)
            gain = gain_ref[y]
            x_all[q, y, rows, :] = (lat * inverse * gain).astype(bf)
            x_all[q, y, rows_t, :] = ((tang * inverse - lat * second) * gain).astype(bf)

    def multiply(weight, blk, p):
        acc = None
        for side in range(2):
            rows_in = weight[pl.ds(side * (layers // 2), layers // 2)]
            term = jnp.dot(
                x_all[blk, side, pl.ds(p * tok, tok), :], rows_in.reshape(own, -1),
                preferred_element_type=jnp.float32,
            )
            acc = term if acc is None else acc + term
        return acc.astype(bf)

    def project(w, blk):
        for p in range(2):
            res = multiply(w_all.at[w], blk, p)
            rows = pl.ds(pl.multiple_of(blk * tok + tok, tok), tok)
            for h in range(nheads):
                lanes = slice((2 * h + p) * HD, (2 * h + p + 1) * HD)
                (k_all, v_all)[w][rows, lanes] = res[:, h * HD:(h + 1) * HD]

    early = z // (layers // 2)

    def query_term(h, blk, side, p):
        rows_in = wq_all[h, pl.ds(side * (layers // 2), layers // 2)]
        return jnp.dot(
            x_all[blk, side, pl.ds(p * tok, tok), :], rows_in.reshape(own, HD),
            preferred_element_type=jnp.float32,
        )

    def query_begin(h):
        @pl.loop(0, 4)
        def _(blk):
            @pl.loop(0, 2)
            def _(p):
                q_part[blk, p] = query_term(h, blk, early, p)

    def project_query(h, blk):
        @pl.loop(0, 2)
        def _(p):
            lanes = pl.ds(pl.multiple_of(p * HD, HD), HD)
            if h == nheads - 1:
                q_blk[:, lanes] = (q_part[blk, p] + query_term(h, blk, 1 - early, p)).astype(bf)
            else:
                q_blk[:, lanes] = multiply(wq_all.at[h], blk, p)

    kv = (k_all, v_all)

    def halo(way, a, landing=False):
        if way == 0:
            source = pl.ds(4 * tok, tok)
            target = pl.ds(0, tok)
        else:
            source = pl.ds(tok, tok)
            target = pl.ds(5 * tok, tok)
        return pltpu.make_async_remote_copy(
            src_ref=kv[a].at[target if landing else source], dst_ref=kv[a].at[target],
            send_sem=h_send.at[way, a], recv_sem=h_recv.at[way, a],
            device_id=at(me + 4 if way == 0 else me - 4, y), device_id_type=MESH,
        )

    def halo_start(a):
        @pl.when(z < layers - 1)
        def _():
            halo(0, a).start()

        @pl.when(z > 0)
        def _():
            halo(1, a).start()

    def halo_wait(a):
        @pl.when(z > 0)
        def _():
            halo(0, a, True).wait_recv()

        @pl.when(z < layers - 1)
        def _():
            halo(1, a, True).wait_recv()

    def halo_fill():
        @pl.when(z == 0)
        def _():
            for a in range(2):
                kv[a][0:tok, :] = jnp.zeros((tok, 2 * cols), bf)

        @pl.when(z == layers - 1)
        def _():
            for a in range(2):
                kv[a][5 * tok:6 * tok, :] = jnp.zeros((tok, 2 * cols), bf)

    def halo_drain(a):
        @pl.when(z < layers - 1)
        def _():
            halo(0, a).wait_send()

        @pl.when(z > 0)
        def _():
            halo(1, a).wait_send()

    tiles = tok // TILE
    band = 2 * tiles + 1
    scale = HD ** (-0.5)
    contract = (((1,), (1,)), ((), ()))

    def hidden(tile, j):
        row = z * 4 * tiles + tile
        col = row - tiles + j
        total = layers * 4 * tiles
        inside = jnp.logical_and(col >= 0, col < total).astype(jnp.int32)
        seen = mask_ref[row, jnp.clip(col, 0, total - 1)] * inside
        return (seen - 1).astype(jnp.float32) * 1e30

    def attend_block(h, blk):
        lanes = slice(2 * h * HD, 2 * (h + 1) * HD)

        for i in range(tiles):
            tile = blk * tiles + i
            span = pl.ds(pl.multiple_of(tile * TILE, TILE), band * TILE)
            query = q_blk[i * TILE:(i + 1) * TILE, :]
            keys = k_all[span, lanes]
            left = jnp.concatenate(
                [
                    jnp.concatenate([query[:, :HD], query[:, HD:]], 0),
                    jnp.concatenate([jnp.zeros((TILE, HD), bf), query[:, :HD]], 0),
                ],
                1,
            )
            scores = lax.dot_general(left, keys, contract, preferred_element_type=jnp.float32)
            masked = jnp.concatenate(
                [
                    scores[:TILE, j * TILE:(j + 1) * TILE] * scale + hidden(tile, j)
                    for j in range(band)
                ],
                1,
            )
            highest = jnp.max(masked, -1, keepdims=True)
            expos = jnp.exp(masked - highest)
            probs = expos * (1.0 / jnp.sum(expos, -1, keepdims=True))
            weighed = probs * (scores[TILE:] * scale)
            probs_t = weighed - probs * jnp.sum(weighed, -1, keepdims=True)
            stacked = jnp.concatenate([probs.astype(bf), probs_t.astype(bf)], 0)
            out = jnp.dot(stacked, v_all[span, lanes], preferred_element_type=jnp.float32)
            into = slice(i * TILE, (i + 1) * TILE)
            a_all[h, blk, 0, into, :] = out[:TILE, :HD].astype(bf)
            a_all[h, blk, 1, into, :] = (out[:TILE, HD:] + out[TILE:, :HD]).astype(bf)

    def att_slot(h, head, slot):
        return att_ref.at[head, :, :, pl.ds(pl.multiple_of((slot * nheads + h) * HD, HD), HD)]

    def att_copy(h, k, j):
        blk = (q + k) % 4
        return pltpu.make_async_remote_copy(
            src_ref=a_all.at[h, blk], dst_ref=att_slot(h, y, q),
            send_sem=at_send.at[h, k, j], recv_sem=at_recv.at[h, k, j],
            device_id=at(base + blk, (y + j) % 2), device_id_type=MESH,
        )

    def att_own(h):
        return pltpu.make_async_copy(a_all.at[h, q], att_slot(h, y, q), at_local.at[h])

    def att_start(h, k, blk):
        att_copy(h, k, 1).start()

        @pl.when(k > 0)
        def _():
            att_copy(h, k, 0).start()

        @pl.when(k == 0)
        def _():
            att_own(h).start()

    def att_end(h):
        for k in range(4):
            for j in range(2):
                if k or j:
                    came = att_slot(h, (y + j) % 2, (q + 4 - k) % 4)
                    pltpu.make_async_remote_copy(
                        src_ref=came, dst_ref=came,
                        send_sem=at_send.at[h, k, j], recv_sem=at_recv.at[h, k, j],
                        device_id=at(base + (q + k) % 4, (y + j) % 2), device_id_type=MESH,
                    ).wait_recv()
                    att_copy(h, k, j).wait_send()
        att_own(h).wait()

    per = layers // 2

    def o_slot(zz, xs, cs, ys, h):
        return ofull_ref.at[ys, zz % per, xs, cs, pl.ds(h * half, half)]

    def o_source(zz, own_block, h):
        return wo_ref.at[pl.ds(h * half, half)] if own_block else oz_ref.at[zz, h]

    def o_far(zz, own_block, h):
        goal = zz // per
        return pltpu.make_async_remote_copy(
            src_ref=o_source(zz, own_block, h), dst_ref=o_slot(zz, x, c, y, h),
            send_sem=o_send.at[zz, h, 0], recv_sem=o_recv.at[zz % per, h, 1, (y + goal) % 2],
            device_id=at(base + xq, goal), device_id_type=MESH,
        )

    def o_near(zz, own_block, h):
        return pltpu.make_async_remote_copy(
            src_ref=o_source(zz, own_block, h), dst_ref=o_slot(zz, x, c, y, h),
            send_sem=o_send.at[zz, h, 1], recv_sem=o_recv.at[zz % per, h, 0, 1],
            device_id=over, device_id_type=MESH,
        )

    def o_self(zz, own_block, h):
        return pltpu.make_async_copy(
            o_source(zz, own_block, h), o_slot(zz, x, c, y, h), o_local.at[zz % per, h]
        )

    def o_give(zz, own_block, h):
        o_far(zz, own_block, h).start()

        @pl.when(zz // per == y)
        def _():
            o_self(zz, own_block, h).start()

        @pl.when(zz // per != y)
        def _():
            o_near(zz, own_block, h).start()

    def o_give_dist(d, among):
        for h in range(2):
            for way in range(2 if d else 1):

                @pl.when(among(way, d))
                def _(way=way, h=h):
                    o_give(z - d if way == 0 else z + d, d == 0, h)

    def o_drain():
        for d in range(layers):
            for h in range(2):
                for way in range(2 if d else 1):

                    @pl.when(z_has(way, d))
                    def _(way=way, h=h, d=d):
                        zz = z - d if way == 0 else z + d
                        o_far(zz, d == 0, h).wait_send()

                        @pl.when(zz // per != y)
                        def _():
                            o_near(zz, d == 0, h).wait_send()

    def o_flip(zz, h, dx, dy, landing=False):
        xs = (x + dx) % 2
        ys = (y + dy) % 2
        block = o_slot(zz, xs, 1 - c if landing else c, ys, h)
        return pltpu.make_async_remote_copy(
            src_ref=block, dst_ref=block,
            send_sem=of_send.at[zz % per, h, dx, dy], recv_sem=of_recv.at[zz % per, h, dx, dy],
            device_id=twin, device_id_type=MESH,
        )

    def o_take(zz, h):
        for dx in range(2):
            for dy in range(2):
                if dx or dy:
                    came = o_slot(zz, (x + dx) % 2, c, (y + dy) % 2, h)
                    pltpu.make_async_remote_copy(
                        src_ref=came, dst_ref=came,
                        send_sem=o_send.at[zz, h, 0], recv_sem=o_recv.at[zz % per, h, dx, dy],
                        device_id=twin, device_id_type=MESH,
                    ).wait_recv()
                else:
                    o_self(zz, False, h).wait()
                o_flip(zz, h, dx, dy).start()

    def o_take_end(zz, h):
        for dx in range(2):
            for dy in range(2):
                o_flip(zz, h, dx, dy, True).wait_recv()
                o_flip(zz, h, dx, dy).wait_send()

    ends = (z == 0).astype(jnp.int32) + (z == layers - 1).astype(jnp.int32)
    pl.semaphore_wait(barrier, 9 - ends)

    queries = [heads_at + h for h in range(nheads)]
    outs = [outs_at, outs_at + 1]
    every = range(1, layers)
    a2a_start(0)
    for w in outs:
        z_begin(w)
    load_in(0).wait()
    load_in(1).wait()
    norm_sums()
    s_copy().start()
    halo_fill()
    s_copy().wait()
    norm_apply()
    n_copy(1, 0).start()
    n_copy(2, 1).start()
    n_copy(0, 0).start()
    n_copy(0, 1).start()
    a2a_wait(0)
    z_begin(0)
    a2a_start(1)
    for w in outs:
        z_relay(w, 1)

    n_copy(1, 0, xq, y).wait_recv()
    n_copy(1, 1).start()
    f_copy(0, 0).start()
    n_copy(2, 1, q, 1 - y).wait_recv()
    n_copy(2, 0).start()
    f_copy(1, 1).start()

    z_relay(0, 1)
    for w in outs:
        z_relay(w, 2)
    a2a_wait(1)
    z_begin(1)

    n_copy(1, 1, xq, y).wait_recv()
    n_copy(2, 0, q, 1 - y).wait_recv()
    d_copy(0).start()
    d_copy(1).start()
    f_copy(0, 1).start()
    f_copy(1, 0).start()
    for w in queries:
        a2a_start(w)

    z_relay(0, 2)
    z_relay(1, 1)
    z_wait(0, *every)
    for p in range(2):
        n_copy(0, p, tq, y).wait_recv()
        f_copy(1, p, True).wait_recv()

    def project_pair(w, side):
        @pl.loop(0, 2)
        def _(j):
            project(w, 2 * side + j)

    project_pair(0, x)
    z_relay(1, 2)
    for p in range(2):
        d_copy(p, True).wait_recv()
        f_copy(2, p).start()
    for w in outs:
        z_wait(w, *every)
    for d in range(layers):
        o_give_dist(d, z_has)
    for w in queries:
        a2a_wait(w)
        z_begin(w, False)
    for p in range(2):
        f_copy(0, p, True).wait_recv()
        f_copy(2, p, True).wait_recv()
    project_pair(0, 1 - x)
    halo_start(0)
    z_wait(1, *every)
    project_pair(1, x)
    project_pair(1, 1 - x)
    halo_start(1)

    def o_take_all(early):
        for n in range(per):
            zz = per * y + n
            close = jnp.logical_and(zz - z <= 1, z - zz <= 1)

            @pl.when(close if early else jnp.logical_not(close))
            def _(zz=zz):
                for h in range(2):
                    o_take(zz, h)

    for h in range(nheads):
        last = h == nheads - 1
        if last:
            z_begin(queries[h], True)
        if h:
            z_pace(queries[h - 1])
        if not last:
            z_begin(queries[h], True)
        for d in every[:-1]:
            z_relay(queries[h], d)
        if h == 0:
            halo_wait(0)
            halo_wait(1)
        z_wait(queries[h], 1)
        if last:
            query_begin(h)
        z_wait(queries[h], *every[1:])
        @pl.loop(0, 4)
        def _(n, h=h):
            k = 3 - n
            blk = (q + k) % 4
            project_query(h, blk)
            attend_block(h, blk)
            att_start(h, k, blk)

        if h < 2:
            o_take_all(h == 0)
    for h in range(nheads):
        att_end(h)
    for zz in range(per):
        for h in range(2):
            o_take_end(per * y + zz, h)
    for w in range(outs_at):
        for k in (1, 2, 3):
            a2a(w, k).wait_send()
    for item in range(items):
        z_drain(item, item in queries[:-1])
    for p in range(2):
        for way in range(3):
            n_copy(way, p).wait_send()
        d_copy(p).wait_send()
        for kind in range(3):
            f_copy(kind, p).wait_send()
    halo_drain(0)
    halo_drain(1)
    o_drain()


def run_layers(tile_mask, latent, probe, gain, wk, wv, wq, wo):
    layers = lax.axis_size("ctx") // 4
    tok, own = latent.shape
    rows, width = wk.shape
    cols = width // 4
    nheads = cols // HD
    half = rows // 2
    dma = pltpu.SemaphoreType.DMA
    bf = jnp.bfloat16
    vmem = pl.BlockSpec(memory_space=pltpu.VMEM)
    smem = pl.BlockSpec(memory_space=pltpu.SMEM)
    anywhere = pl.BlockSpec(memory_space=pl.ANY)
    return pl.pallas_call(
        functools.partial(layer_kernel, layers),
        out_shape=(
            jax.ShapeDtypeStruct((2, 2, tok, width), bf),
            jax.ShapeDtypeStruct((layers // 2, 2, 2, 2, rows, width), bf),
            jax.ShapeDtypeStruct((layers, 2, half, width), bf),
        ),
        in_specs=[smem, anywhere, anywhere, vmem] + [anywhere] * 4,
        out_specs=(anywhere,) * 3,
        scratch_shapes=[
            pltpu.VMEM((4, 2, 2 * tok, own), bf),
            pltpu.VMEM((2, layers, 4, rows, cols), bf),
            pltpu.VMEM((nheads, layers, 4, rows, HD), bf),
            pltpu.VMEM((6 * tok, 2 * cols), bf),
            pltpu.VMEM((6 * tok, 2 * cols), bf),
            pltpu.VMEM((tok, 2 * HD), bf),
            pltpu.VMEM((4, 2, tok, HD), jnp.float32),
            pltpu.VMEM((nheads, 4, 2, tok, HD), bf),
            pltpu.VMEM((tok, HD), jnp.float32),
            pltpu.VMEM((tok, HD), jnp.float32),
            dma((2,)), dma((2 + nheads, 3)), dma((2 + nheads, 3)), dma((2 + nheads,)),
            dma((4 + nheads, 2, layers - 1)), dma((4 + nheads, 2, layers - 1)), dma, dma,
            dma((3, 2)), dma((3, 2)), dma((2,)), dma((2,)), dma((3, 2)), dma((3, 2)),
            dma((2, 2)), dma((2, 2)),
            dma((nheads, 4, 2)), dma((nheads, 4, 2)), dma((nheads,)),
            dma((layers, 2, 2)), dma((layers // 2, 2, 2, 2)), dma((layers // 2, 2)),
            dma((layers // 2, 2, 2, 2)), dma((layers // 2, 2, 2, 2)),
        ],
        compiler_params=pltpu.CompilerParams(
            collective_id=0, has_side_effects=True, vmem_limit_bytes=60 * MIB
        ),
    )(tile_mask, latent, probe, gain, wk, wv, wq, wo)


def finish_kernel(head_ref, att_ref, o_ref, lat_ref, probe_ref, mixed_ref, tang_ref, trace_ref):
    tok, chunk = lat_ref.shape
    contract = (((1,), (1,)), ((), ()))
    branch = None
    for ys in range(2):
        lhs = att_ref[ys].reshape(2 * tok, att_ref.shape[-1])
        term = lax.dot_general(lhs, o_ref[ys], contract, preferred_element_type=jnp.float32)
        term = term.astype(jnp.bfloat16).astype(jnp.float32)
        branch = term if branch is None else branch + term
    branch_t = branch[tok:]
    mixed_ref[...] = (lat_ref[...].astype(jnp.float32) + branch[:tok]).astype(jnp.bfloat16)
    tang_ref[...] = branch_t.astype(jnp.bfloat16)
    terms = jnp.sum(probe_ref[...].astype(jnp.float32) * branch_t, -1, keepdims=True)

    @pl.when(pl.program_id(0) == 0)
    def _():
        trace_ref[...] = jnp.zeros_like(trace_ref)

    trace_ref[...] += jnp.broadcast_to(terms, trace_ref.shape)


def finish(att, ofull, latent, probe):
    tok, own = latent.shape
    width = ofull.shape[-1]
    chunk = 512
    steps = own // chunk
    blocks = ofull.reshape(2, own, width)
    return pl.pallas_call(
        finish_kernel,
        grid_spec=pltpu.PrefetchScalarGridSpec(
            num_scalar_prefetch=1,
            grid=(steps,),
            in_specs=[
                pl.BlockSpec((2, 2, tok, width), lambda i, h: (0, 0, 0, 0)),
                pl.BlockSpec((2, chunk, width), lambda i, h: (0, i, 0)),
                pl.BlockSpec((tok, chunk), lambda i, h: (0, i)),
                pl.BlockSpec((tok, chunk), lambda i, h: (0, h[0] * steps + i)),
            ],
            out_specs=[
                pl.BlockSpec((tok, chunk), lambda i, h: (0, i)),
                pl.BlockSpec((tok, chunk), lambda i, h: (0, i)),
                pl.BlockSpec((tok, HD), lambda i, h: (0, 0)),
            ],
        ),
        out_shape=(
            jax.ShapeDtypeStruct((tok, own), jnp.bfloat16),
            jax.ShapeDtypeStruct((tok, own), jnp.bfloat16),
            jax.ShapeDtypeStruct((tok, HD), jnp.float32),
        ),
        compiler_params=pltpu.CompilerParams(vmem_limit_bytes=48 * MIB),
    )(lax.axis_index("head").reshape(1), att, blocks, latent, probe)


def layer_shards(latent, probe, norm_gain, w_query, w_key, w_value, w_out, tile_mask):
    att, ofull, _ = run_layers(
        tile_mask, latent, probe, norm_gain.reshape(2, 1, D // 2),
        w_key, w_value, w_query, w_out.T,
    )
    mixed, tangent, trace = finish(att, ofull, latent, probe)
    return (mixed, tangent, lax.psum(trace[:, 0], "head"))


def solution(mesh):
    placed = (
        P("ctx", "head"),
        P("ctx", None),
        P(),
        P("ctx", "head"),
        P("ctx", "head"),
        P("ctx", "head"),
        P("head", "ctx"),
        P(),
    )
    by_layer = mesh.shape["ctx"] == 16 and mesh.shape["head"] == 2
    return jax.shard_map(
        layer_shards if by_layer else shards,
        mesh=mesh,
        in_specs=placed,
        out_specs=(P("ctx", "head"), P("ctx", "head"), P("ctx")),
        check_vma=False,
    )
```

```python
import functools

import jax
import jax.numpy as jnp
from jax import lax
from jax.experimental import pallas as pl
from jax.experimental.pallas import tpu as pltpu
from jax.sharding import PartitionSpec as P

D = 5120
HD = 128
TILE = 128
MESH = pl.DeviceIdType.MESH
MIB = 1 << 20


def chip_of(pos, chips):
    half = pos // (chips // 2)
    return (1 - half) * 2 * pos + half * (2 * (chips - 1 - pos) + 1)


def project_kernel(
    n, heads, lat_ref, probe_ref, gain_ref, w_ref,
    qkv_ref, wo_ref, proj_ref, halo_ref,
    lat_all, x_ref, wbuf, obuf,
    local_sem, ring_send, ring_recv, flip_send, flip_recv, own_send, own_recv,
    lat_send, lat_recv, lat_local, load_sem, store_sem, halo_send, halo_recv, halo_local,
):
    chips = n // 2
    hops = chips - 1
    tok, own = lat_ref.shape
    cols = proj_ref.shape[-1]
    width = wbuf.shape[-1]
    pieces = cols // width
    me = lax.axis_index("ctx")
    head = lax.axis_index("head")
    core = me % 2
    chip = me // 2
    cx = chip % 2
    cz = chip // 2
    pos = (1 - cx) * cz + cx * (chips - 1 - cz)
    ahead = chip_of((pos + 1) % chips, chips) * 2 + core
    behind = chip_of((pos + chips - 1) % chips, chips) * 2 + core
    twin = me + 1 - 2 * core
    right = (me + 1) % n
    left = (me + n - 1) % n

    barrier = pltpu.get_barrier_semaphore()
    for other in (ahead, behind, twin, right, left):
        pl.semaphore_signal(barrier, inc=1, device_id={"ctx": other}, device_id_type=MESH)
    for k in range(1, heads):
        pl.semaphore_signal(
            barrier, inc=1, device_id={"head": (head + k) % heads}, device_id_type=MESH
        )

    def full(w):
        return wo_ref if w == 3 else qkv_ref.at[w]

    def local_copy(w):
        return pltpu.make_async_copy(w_ref.at[w], full(w).at[me], local_sem.at[w])

    for w in range(4):
        local_copy(w).start()
    mine = pltpu.make_async_copy(lat_ref, lat_all.at[head], lat_local)
    mine.start()
    pl.semaphore_wait(barrier, 5 + heads - 1)

    def ring(w, hop, way, first=False):
        source = (pos + chips - hop) % chips if way == 0 else (pos + hop) % chips
        owner = chip_of(source, chips) * 2 + core
        block = full(w).at[owner, way]
        return pltpu.make_async_remote_copy(
            src_ref=w_ref.at[w, way] if first else block, dst_ref=block,
            send_sem=ring_send.at[w, hop, way], recv_sem=ring_recv.at[w, hop, way],
            device_id={"ctx": ahead if way == 0 else behind}, device_id_type=MESH,
        )

    def arrived(w, hop, way):
        source = (pos + chips - hop - 1) % chips if way == 0 else (pos + hop + 1) % chips
        return full(w).at[chip_of(source, chips) * 2 + core, way]

    def ring_wait(w, hop, way):
        block = arrived(w, hop, way)
        pltpu.make_async_remote_copy(
            src_ref=block, dst_ref=block,
            send_sem=ring_send.at[w, hop, way], recv_sem=ring_recv.at[w, hop, way],
            device_id={"ctx": ahead if way == 0 else behind}, device_id_type=MESH,
        ).wait_recv()

    def flip(w, hop, way):
        block = arrived(w, hop, way)
        return pltpu.make_async_remote_copy(
            src_ref=block, dst_ref=block,
            send_sem=flip_send.at[w, hop, way], recv_sem=flip_recv.at[w, hop, way],
            device_id={"ctx": twin}, device_id_type=MESH,
        )

    def flip_wait(w, hop, way):
        source = (pos + chips - hop - 1) % chips if way == 0 else (pos + hop + 1) % chips
        block = full(w).at[chip_of(source, chips) * 2 + 1 - core, way]
        pltpu.make_async_remote_copy(
            src_ref=block, dst_ref=block,
            send_sem=flip_send.at[w, hop, way], recv_sem=flip_recv.at[w, hop, way],
            device_id={"ctx": twin}, device_id_type=MESH,
        ).wait_recv()

    def own_flip(w, who):
        return pltpu.make_async_remote_copy(
            src_ref=w_ref.at[w], dst_ref=full(w).at[who],
            send_sem=own_send.at[w], recv_sem=own_recv.at[w],
            device_id={"ctx": twin}, device_id_type=MESH,
        )

    def begin(w):
        ring(w, 0, 0, True).start()
        ring(w, 0, 1, True).start()
        own_flip(w, me).start()

    def advance(w, hop):
        for way in range(2):
            ring_wait(w, hop - 1, way)
            ring(w, hop, way).start()
            flip(w, hop - 1, way).start()

    def finish(w):
        for way in range(2):
            ring_wait(w, hops - 1, way)
            flip(w, hops - 1, way).start()

    def settle(w):
        local_copy(w).wait()
        own_flip(w, twin).wait_recv()

        @pl.loop(0, hops)
        def _(hop):
            for way in range(2):
                flip_wait(w, hop, way)

    def drain(w):
        own_flip(w, me).wait_send()

        @pl.loop(0, hops)
        def _(hop):
            for way in range(2):
                ring(w, hop, way).wait_send()
                flip(w, hop, way).wait_send()

    def lat_copy(k):
        return pltpu.make_async_remote_copy(
            src_ref=lat_ref, dst_ref=lat_all.at[head],
            send_sem=lat_send.at[k - 1], recv_sem=lat_recv.at[k - 1],
            device_id={"head": (head + k) % heads}, device_id_type=MESH,
        )

    def norm():
        mine.wait()
        for k in range(1, heads):
            came = lat_all.at[(head + heads - k) % heads]
            pltpu.make_async_remote_copy(
                src_ref=lat_ref, dst_ref=came,
                send_sem=lat_send.at[k - 1], recv_sem=lat_recv.at[k - 1],
                device_id={"head": (head + k) % heads}, device_id_type=MESH,
            ).wait_recv()
        step = 16

        @pl.loop(0, tok // step)
        def _(i):
            rows = pl.ds(pl.multiple_of(i * step, step), step)
            squares = jnp.zeros((step, 1), jnp.float32)
            crossed = jnp.zeros((step, 1), jnp.float32)
            for h in range(heads):
                part = lat_all[h, rows, :].astype(jnp.float32)
                tang = probe_ref[rows, h * own:(h + 1) * own].astype(jnp.float32)
                squares = squares + jnp.sum(part * part, -1, keepdims=True)
                crossed = crossed + jnp.sum(part * tang, -1, keepdims=True)
            inverse = lax.rsqrt(squares / D + 1e-06)
            along = crossed / D
            second = inverse * inverse * inverse * along
            rows_t = pl.ds(pl.multiple_of(tok + i * step, step), step)
            for h in range(heads):
                part = lat_all[h, rows, :].astype(jnp.float32)
                tang = probe_ref[rows, h * own:(h + 1) * own].astype(jnp.float32)
                gain = gain_ref[:, h * own:(h + 1) * own]
                x_ref[rows, h * own:(h + 1) * own] = (part * inverse * gain).astype(jnp.bfloat16)
                x_ref[rows_t, h * own:(h + 1) * own] = (
                    (tang * inverse - part * second) * gain
                ).astype(jnp.bfloat16)

    def load(w, piece, slot):
        at = pl.ds(pl.multiple_of(piece * width, width), width)
        return pltpu.make_async_copy(
            qkv_ref.at[w, :, :, :, at], wbuf.at[slot], load_sem.at[slot]
        )

    def multiply(w, piece, slot):
        load(w, piece, slot).wait()
        weight = wbuf[slot].reshape(D, width)
        rows = 128

        @pl.loop(0, 2 * tok // rows)
        def _(i):
            at = pl.ds(pl.multiple_of(i * rows, rows), rows)
            obuf[slot, at, :] = jnp.dot(
                x_ref[at, :], weight, preferred_element_type=jnp.float32
            ).astype(jnp.bfloat16)

        at = pl.ds(pl.multiple_of(piece * width, width), width)
        store = pltpu.make_async_copy(
            obuf.at[slot], proj_ref.at[w, :, at], store_sem.at[slot]
        )
        store.start()
        store.wait()

    def fetch(q, slot):
        @pl.when(q < 2 * pieces)
        def _():
            load(q // pieces, q % pieces, slot).start()

    def work(q, slot):
        @pl.when(q < 2 * pieces)
        def _():
            multiply(q // pieces, q % pieces, slot)

    def halo(side, a):
        return pltpu.make_async_remote_copy(
            src_ref=proj_ref.at[a], dst_ref=halo_ref.at[side, a],
            send_sem=halo_send.at[side, a], recv_sem=halo_recv.at[side, a],
            device_id={"ctx": right if side == 0 else left}, device_id_type=MESH,
        )

    def halo_fill(side, a):
        return pltpu.make_async_copy(proj_ref.at[a], halo_ref.at[side, a], halo_local.at[a])

    def halo_start(a):
        @pl.when(me < n - 1)
        def _():
            halo(0, a).start()

        @pl.when(me > 0)
        def _():
            halo(1, a).start()

        @pl.when(me == 0)
        def _():
            halo_fill(0, a).start()

        @pl.when(me == n - 1)
        def _():
            halo_fill(1, a).start()

    def halo_end(a):
        @pl.when(me < n - 1)
        def _():
            halo(0, a).wait_send()
            halo(1, a).wait_recv()

        @pl.when(me > 0)
        def _():
            halo(1, a).wait_send()
            halo(0, a).wait_recv()

        @pl.when(me == 0)
        def _():
            halo_fill(0, a).wait()

        @pl.when(me == n - 1)
        def _():
            halo_fill(1, a).wait()

    begin(0)
    begin(1)
    for k in range(1, heads):
        lat_copy(k).start()

    @pl.loop(1, hops)
    def _(hop):
        advance(0, hop)
        advance(1, hop)

        @pl.when(hop == hops - 1)
        def _():
            norm()

    begin(2)
    begin(3)
    finish(0)
    finish(1)
    settle(0)
    settle(1)

    @pl.loop(1, hops)
    def _(hop):
        q = (hop - 1) * 4
        fetch(q, 0)
        fetch(q + 1, 1)
        advance(2, hop)
        work(q, 0)
        fetch(q + 2, 0)
        work(q + 1, 1)
        fetch(q + 3, 1)
        advance(3, hop)
        work(q + 2, 0)
        work(q + 3, 1)
        for a in range(2):

            @pl.when(hop == -(-(a + 1) * pieces // 4))
            def _(a=a):
                halo_start(a)

    finish(2)
    finish(3)
    settle(2)

    load(2, 0, 0).start()
    for piece in range(pieces):
        if piece + 1 < pieces:
            load(2, piece + 1, (piece + 1) % 2).start()
        multiply(2, piece, piece % 2)

    settle(3)
    halo_end(0)
    halo_end(1)
    for w in range(4):
        drain(w)
    for k in range(1, heads):
        lat_copy(k).wait_send()


def gather_and_project(latent, probe, gain, weights):
    n = lax.axis_size("ctx")
    heads = lax.axis_size("head")
    hops = n // 2 - 1
    tok, own = latent.shape
    rows, cols = weights.shape[1:]
    weights = weights.reshape(4, 2, rows // 2, cols)
    width = 256 if cols % 256 == 0 else 128
    dma = pltpu.SemaphoreType.DMA
    bf = jnp.bfloat16
    vmem = pl.BlockSpec(memory_space=pltpu.VMEM)
    anywhere = pl.BlockSpec(memory_space=pl.ANY)
    return pl.pallas_call(
        functools.partial(project_kernel, n, heads),
        out_shape=(
            jax.ShapeDtypeStruct((3, n, 2, rows // 2, cols), bf),
            jax.ShapeDtypeStruct((n, 2, rows // 2, cols), bf),
            jax.ShapeDtypeStruct((3, 2 * tok, cols), bf),
            jax.ShapeDtypeStruct((2, 2, 2 * tok, cols), bf),
        ),
        in_specs=[vmem, vmem, vmem, anywhere],
        out_specs=(anywhere,) * 4,
        scratch_shapes=[
            pltpu.VMEM((heads, tok, own), bf),
            pltpu.VMEM((2 * tok, D), bf),
            pltpu.VMEM((2, n, 2, rows // 2, width), bf),
            pltpu.VMEM((2, 2 * tok, width), bf),
            dma((4,)), dma((4, hops, 2)), dma((4, hops, 2)), dma((4, hops, 2)), dma((4, hops, 2)),
            dma((4,)), dma((4,)),
            dma((heads - 1,)), dma((heads - 1,)), dma, dma((2,)), dma((2,)),
            dma((2, 2)), dma((2, 2)), dma((2,)),
        ],
        compiler_params=pltpu.CompilerParams(
            collective_id=0, has_side_effects=True, vmem_limit_bytes=48 * MIB
        ),
    )(latent, probe, gain, weights)


def attend_kernel(tiles, mask_ref, q_ref, own_ref, low_ref, high_ref, out_ref, k_all, v_all):
    tok = tiles * TILE
    scale = HD ** (-0.5)
    for place, ref in enumerate((low_ref, own_ref, high_ref)):
        at = slice(place * tok, (place + 1) * tok)
        k_all[at, :HD] = ref[0, :tok, :]
        k_all[at, HD:] = ref[0, tok:, :]
        v_all[at, :HD] = ref[1, :tok, :]
        v_all[at, HD:] = ref[1, tok:, :]
    contract = (((1,), (1,)), ((), ()))
    band = 2 * tiles + 1
    for i in range(tiles):
        rows = slice(i * TILE, (i + 1) * TILE)
        rows_t = slice(tok + i * TILE, tok + (i + 1) * TILE)
        query = q_ref[0, rows, :]
        query_t = q_ref[0, rows_t, :]
        keys = k_all[i * TILE:(i + band) * TILE, :]
        scores = lax.dot_general(
            query, keys[:, :HD], contract, preferred_element_type=jnp.float32
        ) * scale
        scores_t = lax.dot_general(
            jnp.concatenate([query_t, query], 1), keys, contract,
            preferred_element_type=jnp.float32,
        ) * scale
        masked = jnp.concatenate(
            [
                jnp.where(
                    mask_ref[i, i + j] == 1, scores[:, j * TILE:(j + 1) * TILE], -1e30
                )
                for j in range(band)
            ],
            1,
        )
        highest = jnp.max(masked, -1, keepdims=True)
        expos = jnp.exp(masked - highest)
        probs = expos * (1.0 / jnp.sum(expos, -1, keepdims=True))
        weighed = probs * scores_t
        probs_t = weighed - probs * jnp.sum(weighed, -1, keepdims=True)
        probs_b = probs.astype(jnp.bfloat16)
        values = v_all[i * TILE:(i + band) * TILE, :]
        first = jnp.dot(probs_b, values, preferred_element_type=jnp.float32)
        second = first[:, HD:] + jnp.dot(
            probs_t.astype(jnp.bfloat16), values[:, :HD], preferred_element_type=jnp.float32
        )
        out_ref[rows, :] = first[:, :HD].astype(jnp.bfloat16)
        out_ref[rows_t, :] = second.astype(jnp.bfloat16)


def attend(tile_rows, proj, halo):
    rows, cols = proj.shape[1:]
    tok = rows // 2
    tiles = tok // TILE
    return pl.pallas_call(
        functools.partial(attend_kernel, tiles),
        grid=(cols // HD,),
        out_shape=jax.ShapeDtypeStruct((rows, cols), jnp.bfloat16),
        in_specs=[
            pl.BlockSpec(memory_space=pltpu.SMEM),
            pl.BlockSpec((1, rows, HD), lambda h: (2, 0, h)),
            pl.BlockSpec((2, rows, HD), lambda h: (0, 0, h)),
            pl.BlockSpec((None, 2, rows, HD), lambda h: (0, 0, 0, h)),
            pl.BlockSpec((None, 2, rows, HD), lambda h: (1, 0, 0, h)),
        ],
        out_specs=pl.BlockSpec((rows, HD), lambda h: (0, h)),
        scratch_shapes=[pltpu.VMEM((3 * tok, 2 * HD), jnp.bfloat16)] * 2,
        compiler_params=pltpu.CompilerParams(vmem_limit_bytes=32 * MIB),
    )(tile_rows, proj, proj, halo, halo)


def shards(latent, probe, norm_gain, w_query, w_key, w_value, w_out, tile_mask):
    tok_rows, own_cols = latent.shape
    weights = jnp.stack([w_key, w_value, w_query, w_out.T])
    _, wo_full, proj, halo = gather_and_project(latent, probe, norm_gain.reshape(1, D), weights)
    tiles_dev = tok_rows // TILE
    ctx_slot = lax.axis_index("ctx")
    mask_pad = jnp.pad(tile_mask, tiles_dev)
    tile_rows = lax.dynamic_slice(
        mask_pad,
        (ctx_slot * tiles_dev + tiles_dev, ctx_slot * tiles_dev),
        (tiles_dev, 3 * tiles_dev),
    )
    both_rows = attend(tile_rows, proj, halo)
    w_out_t = wo_full.reshape(D, w_out.shape[0])
    terms = lax.dot_general(
        both_rows, w_out_t, (((1,), (1,)), ((), ())), preferred_element_type=jnp.float32
    ).astype(jnp.bfloat16)
    summed = lax.psum_scatter(terms, "head", scatter_dimension=1, tiled=True).astype(jnp.float32)
    branch = summed[:tok_rows]
    branch_t = summed[tok_rows:]
    latent_f = latent.astype(jnp.float32)
    col_start = lax.axis_index("head") * own_cols
    tangent_own = lax.dynamic_slice_in_dim(probe, col_start, own_cols, 1).astype(jnp.float32)
    mixed = (latent_f + branch).astype(jnp.bfloat16)
    trace_terms = lax.psum(jnp.sum(tangent_own * branch_t, -1), "head")
    return (mixed, branch_t.astype(jnp.bfloat16), trace_terms)


def layer_kernel(
    layers, mask_ref, lat_ref, probe_ref, gain_ref, wk_ref, wv_ref, wq_ref, wo_ref,
    att_ref, ofull_ref, oz_ref,
    x_all, w_all, wq_all, k_all, v_all, q_blk, q_part, a_all, sums, sums_in,
    in_sem, a2a_send, a2a_recv, a2a_local, z_send, z_recv, s_send, s_recv,
    n_send, n_recv, d_send, d_recv, f_send, f_recv, h_send, h_recv,
    at_send, at_recv, at_local, o_send, o_recv, o_local, of_send, of_recv,
):
    tok, own = lat_ref.shape
    cols = w_all.shape[-1]
    nheads = cols // HD
    half = wo_ref.shape[0] // 2
    me = lax.axis_index("ctx")
    y = lax.axis_index("head")
    z = me // 4
    x = (me // 2) % 2
    c = me % 2
    base = z * 4
    q = 2 * x + c
    tq = 2 * x + 1 - c
    xq = 2 * (1 - x) + c
    dq = 2 * (1 - x) + 1 - c
    heads_at = 2
    outs_at = 2 + nheads
    items = outs_at + 2
    bf = jnp.bfloat16

    def at(ctx, head):
        return {"ctx": ctx, "head": head}

    barrier = pltpu.get_barrier_semaphore()
    for k in range(4):
        for j in range(2):
            if k or j:
                pl.semaphore_signal(
                    barrier, inc=1, device_id=at(base + (q + k) % 4, (y + j) % 2),
                    device_id_type=MESH,
                )

    @pl.when(z < layers - 1)
    def _():
        pl.semaphore_signal(barrier, inc=1, device_id=at(me + 4, y), device_id_type=MESH)

    @pl.when(z > 0)
    def _():
        pl.semaphore_signal(barrier, inc=1, device_id=at(me - 4, y), device_id_type=MESH)

    def load_in(p):
        if p == 0:
            source = lat_ref
        else:
            source = probe_ref.at[:, pl.ds(pl.multiple_of(y * own, own), own)]
        return pltpu.make_async_copy(
            source, x_all.at[q, y, pl.ds(p * tok, tok)], in_sem.at[p]
        )

    load_in(0).start()
    load_in(1).start()

    def quarter(w, k):
        if w < heads_at:
            return (wk_ref, wv_ref)[w].at[:, pl.ds(pl.multiple_of(k * cols, cols), cols)]
        first = pl.multiple_of(k * cols + (w - heads_at) * HD, HD)
        return wq_ref.at[:, pl.ds(first, HD)]

    def weight_at(w, zz):
        return w_all.at[w, zz] if w < heads_at else wq_all.at[w - heads_at, zz]

    def a2a_own(w):
        return pltpu.make_async_copy(quarter(w, q), weight_at(w, z).at[q], a2a_local.at[w])

    def a2a(w, k):
        to = (q + k) % 4
        return pltpu.make_async_remote_copy(
            src_ref=quarter(w, to), dst_ref=weight_at(w, z).at[q],
            send_sem=a2a_send.at[w, k - 1], recv_sem=a2a_recv.at[w, k - 1],
            device_id=at(base + to, y), device_id_type=MESH,
        )

    def a2a_start(w):
        a2a_own(w).start()
        for k in (2, 1, 3):
            a2a(w, k).start()

    def a2a_wait(w):
        a2a_own(w).wait()
        for k in (1, 2, 3):
            came = weight_at(w, z).at[(q + 4 - k) % 4]
            pltpu.make_async_remote_copy(
                src_ref=came, dst_ref=came,
                send_sem=a2a_send.at[w, k - 1], recv_sem=a2a_recv.at[w, k - 1],
                device_id=at(base + (q + k) % 4, y), device_id_type=MESH,
            ).wait_recv()

    def region(item, zz):
        return weight_at(item, zz) if item < outs_at else oz_ref.at[zz, item - outs_at]

    def z_copy(item, way, d):
        zz = z - d if way == 0 else z + d
        block = region(item, zz)
        mine = item >= outs_at and d == 0
        return pltpu.make_async_remote_copy(
            src_ref=wo_ref.at[pl.ds((item - outs_at) * half, half)] if mine else block,
            dst_ref=block,
            send_sem=z_send.at[item, way, d], recv_sem=z_recv.at[item, way, d],
            device_id=at(me + 4 if way == 0 else me - 4, y), device_id_type=MESH,
        )

    def z_has(way, d):
        return z >= d if way == 0 else z + d <= layers - 1

    def z_sends(way, d):
        if way == 0:
            return jnp.logical_and(z >= d, z < layers - 1)
        return jnp.logical_and(z + d <= layers - 1, z > 0)

    def z_edge(way):
        return z == layers - 2 if way == 0 else z == 1

    def z_begin(item, edge=None):
        for way in range(2):
            here = z_sends(way, 0)
            if edge is not None:
                here = jnp.logical_and(here, z_edge(way) == edge)

            @pl.when(here)
            def _(way=way):
                z_copy(item, way, 0).start()

    def z_pace(item):
        for way in range(2):
            for d in range(2):

                @pl.when(jnp.logical_and(z_sends(way, d), z_edge(way)))
                def _(way=way, d=d):
                    z_copy(item, way, d).wait_send()

    def z_came(item, way, d):
        block = region(item, z - d if way == 0 else z + d)
        pltpu.make_async_remote_copy(
            src_ref=block, dst_ref=block,
            send_sem=z_send.at[item, way, d - 1], recv_sem=z_recv.at[item, way, d - 1],
            device_id=at(me + 4 if way == 0 else me - 4, y), device_id_type=MESH,
        ).wait_recv()

    def z_relay(item, d):
        for way in range(2):

            @pl.when(z_sends(way, d))
            def _(way=way):
                z_came(item, way, d)
                z_copy(item, way, d).start()

    def z_ends(way, d):
        if way == 0:
            return jnp.logical_and(z >= d, z == layers - 1)
        return jnp.logical_and(z + d <= layers - 1, z == 0)

    def z_wait(item, *dists):
        for d in dists:
            for way in range(2):

                @pl.when(z_ends(way, d))
                def _(way=way, d=d):
                    z_came(item, way, d)

    def z_drain(item, paced):
        for way in range(2):
            for d in range(layers - 1):
                here = z_sends(way, d)
                if paced and d < 2:
                    here = jnp.logical_and(here, jnp.logical_not(z_edge(way)))

                @pl.when(here)
                def _(way=way, d=d):
                    z_copy(item, way, d).wait_send()

    def part(slot, side, p):
        return x_all.at[slot, side, pl.ds(p * tok, tok)]

    twin = at(base + tq, y)
    across = at(base + xq, y)
    over = at(me, 1 - y)

    def n_copy(way, p, slot=None, side=None):
        block = part(q, y, p) if slot is None else part(slot, side, p)
        return pltpu.make_async_remote_copy(
            src_ref=block, dst_ref=block,
            send_sem=n_send.at[way, p], recv_sem=n_recv.at[way, p],
            device_id=(twin, across, over)[way], device_id_type=MESH,
        )

    def d_copy(p, landing=False):
        if landing:
            block = part(xq, 1 - y, p)
        else:
            block = part(xq, y, p) if p == 0 else part(q, 1 - y, p)
        return pltpu.make_async_remote_copy(
            src_ref=block, dst_ref=block,
            send_sem=d_send.at[p], recv_sem=d_recv.at[p],
            device_id=over if p == 0 else across, device_id_type=MESH,
        )

    def f_copy(kind, p, landing=False):
        if landing:
            block = (part(dq, y, p), part(tq, 1 - y, p), part(dq, 1 - y, p))[kind]
        else:
            block = (part(xq, y, p), part(q, 1 - y, p), part(xq, 1 - y, p))[kind]
        return pltpu.make_async_remote_copy(
            src_ref=block, dst_ref=block,
            send_sem=f_send.at[kind, p], recv_sem=f_recv.at[kind, p],
            device_id=twin, device_id_type=MESH,
        )

    def s_copy():
        return pltpu.make_async_remote_copy(
            src_ref=sums, dst_ref=sums_in, send_sem=s_send, recv_sem=s_recv,
            device_id=over, device_id_type=MESH,
        )

    step = 16

    def norm_sums():
        @pl.loop(0, tok // step)
        def _(i):
            rows = pl.ds(pl.multiple_of(i * step, step), step)
            rows_t = pl.ds(pl.multiple_of(tok + i * step, step), step)
            lat = x_all[q, y, rows, :].astype(jnp.float32)
            tang = x_all[q, y, rows_t, :].astype(jnp.float32)
            squares = jnp.sum(lat * lat, -1, keepdims=True)
            crossed = jnp.sum(lat * tang, -1, keepdims=True)
            lane = lax.broadcasted_iota(jnp.int32, (step, HD), 1)
            sums[rows, :] = jnp.where(lane < HD // 2, squares, crossed)

    def norm_apply():
        @pl.loop(0, tok // step)
        def _(i):
            rows = pl.ds(pl.multiple_of(i * step, step), step)
            rows_t = pl.ds(pl.multiple_of(tok + i * step, step), step)
            both = sums[rows, :] + sums_in[rows, :]
            inverse = lax.rsqrt(both[:, 0:1] / D + 1e-06)
            along = both[:, HD // 2:HD // 2 + 1] / D
            second = inverse * inverse * inverse * along
            lat = x_all[q, y, rows, :].astype(jnp.float32)
            tang = x_all[q, y, rows_t, :].astype(jnp.float32)
            gain = gain_ref[y]
            x_all[q, y, rows, :] = (lat * inverse * gain).astype(bf)
            x_all[q, y, rows_t, :] = ((tang * inverse - lat * second) * gain).astype(bf)

    def multiply(weight, blk, p):
        acc = None
        for side in range(2):
            rows_in = weight[pl.ds(side * (layers // 2), layers // 2)]
            term = jnp.dot(
                x_all[blk, side, pl.ds(p * tok, tok), :], rows_in.reshape(own, -1),
                preferred_element_type=jnp.float32,
            )
            acc = term if acc is None else acc + term
        return acc.astype(bf)

    def project(w, blk):
        for p in range(2):
            res = multiply(w_all.at[w], blk, p)
            rows = pl.ds(pl.multiple_of(blk * tok + tok, tok), tok)
            for h in range(nheads):
                lanes = slice((2 * h + p) * HD, (2 * h + p + 1) * HD)
                (k_all, v_all)[w][rows, lanes] = res[:, h * HD:(h + 1) * HD]

    early = z // (layers // 2)

    def query_term(h, blk, side, p):
        rows_in = wq_all[h, pl.ds(side * (layers // 2), layers // 2)]
        return jnp.dot(
            x_all[blk, side, pl.ds(p * tok, tok), :], rows_in.reshape(own, HD),
            preferred_element_type=jnp.float32,
        )

    def query_begin(h):
        @pl.loop(0, 4)
        def _(blk):
            for p in range(2):
                q_part[blk, p] = query_term(h, blk, early, p)

    def project_query(h, blk):
        for p in range(2):
            lanes = slice(p * HD, (p + 1) * HD)
            if h == nheads - 1:
                q_blk[:, lanes] = (q_part[blk, p] + query_term(h, blk, 1 - early, p)).astype(bf)
            else:
                q_blk[:, lanes] = multiply(wq_all.at[h], blk, p)

    kv = (k_all, v_all)

    def halo(way, a, landing=False):
        if way == 0:
            source = pl.ds(4 * tok, tok)
            target = pl.ds(0, tok)
        else:
            source = pl.ds(tok, tok)
            target = pl.ds(5 * tok, tok)
        return pltpu.make_async_remote_copy(
            src_ref=kv[a].at[target if landing else source], dst_ref=kv[a].at[target],
            send_sem=h_send.at[way, a], recv_sem=h_recv.at[way, a],
            device_id=at(me + 4 if way == 0 else me - 4, y), device_id_type=MESH,
        )

    def halo_start(a):
        @pl.when(z < layers - 1)
        def _():
            halo(0, a).start()

        @pl.when(z > 0)
        def _():
            halo(1, a).start()

    def halo_wait(a):
        @pl.when(z > 0)
        def _():
            halo(0, a, True).wait_recv()

        @pl.when(z < layers - 1)
        def _():
            halo(1, a, True).wait_recv()

    def halo_fill():
        @pl.when(z == 0)
        def _():
            for a in range(2):
                kv[a][0:tok, :] = jnp.zeros((tok, 2 * cols), bf)

        @pl.when(z == layers - 1)
        def _():
            for a in range(2):
                kv[a][5 * tok:6 * tok, :] = jnp.zeros((tok, 2 * cols), bf)

    def halo_drain(a):
        @pl.when(z < layers - 1)
        def _():
            halo(0, a).wait_send()

        @pl.when(z > 0)
        def _():
            halo(1, a).wait_send()

    tiles = tok // TILE
    band = 2 * tiles + 1
    scale = HD ** (-0.5)
    contract = (((1,), (1,)), ((), ()))

    def hidden(tile, j):
        row = z * 4 * tiles + tile
        col = row - tiles + j
        total = layers * 4 * tiles
        inside = jnp.logical_and(col >= 0, col < total).astype(jnp.int32)
        seen = mask_ref[row, jnp.clip(col, 0, total - 1)] * inside
        return (seen - 1).astype(jnp.float32) * 1e30

    def attend_block(h, blk):
        lanes = slice(2 * h * HD, 2 * (h + 1) * HD)

        for i in range(tiles):
            tile = blk * tiles + i
            span = pl.ds(pl.multiple_of(tile * TILE, TILE), band * TILE)
            query = q_blk[i * TILE:(i + 1) * TILE, :]
            keys = k_all[span, lanes]
            left = jnp.concatenate(
                [
                    jnp.concatenate([query[:, :HD], query[:, HD:]], 0),
                    jnp.concatenate([jnp.zeros((TILE, HD), bf), query[:, :HD]], 0),
                ],
                1,
            )
            scores = lax.dot_general(left, keys, contract, preferred_element_type=jnp.float32)
            masked = jnp.concatenate(
                [
                    scores[:TILE, j * TILE:(j + 1) * TILE] * scale + hidden(tile, j)
                    for j in range(band)
                ],
                1,
            )
            highest = jnp.max(masked, -1, keepdims=True)
            expos = jnp.exp(masked - highest)
            probs = expos * (1.0 / jnp.sum(expos, -1, keepdims=True))
            weighed = probs * (scores[TILE:] * scale)
            probs_t = weighed - probs * jnp.sum(weighed, -1, keepdims=True)
            stacked = jnp.concatenate([probs.astype(bf), probs_t.astype(bf)], 0)
            out = jnp.dot(stacked, v_all[span, lanes], preferred_element_type=jnp.float32)
            into = slice(i * TILE, (i + 1) * TILE)
            a_all[h, blk, 0, into, :] = out[:TILE, :HD].astype(bf)
            a_all[h, blk, 1, into, :] = (out[:TILE, HD:] + out[TILE:, :HD]).astype(bf)

    def att_slot(h, head, slot):
        return att_ref.at[head, :, :, pl.ds(pl.multiple_of((slot * nheads + h) * HD, HD), HD)]

    def att_copy(h, k, j):
        blk = (q + k) % 4
        return pltpu.make_async_remote_copy(
            src_ref=a_all.at[h, blk], dst_ref=att_slot(h, y, q),
            send_sem=at_send.at[h, k, j], recv_sem=at_recv.at[h, k, j],
            device_id=at(base + blk, (y + j) % 2), device_id_type=MESH,
        )

    def att_own(h):
        return pltpu.make_async_copy(a_all.at[h, q], att_slot(h, y, q), at_local.at[h])

    def att_start(h, k, blk):
        att_copy(h, k, 1).start()

        @pl.when(k > 0)
        def _():
            att_copy(h, k, 0).start()

        @pl.when(k == 0)
        def _():
            att_own(h).start()

    def att_end(h):
        for k in range(4):
            for j in range(2):
                if k or j:
                    came = att_slot(h, (y + j) % 2, (q + 4 - k) % 4)
                    pltpu.make_async_remote_copy(
                        src_ref=came, dst_ref=came,
                        send_sem=at_send.at[h, k, j], recv_sem=at_recv.at[h, k, j],
                        device_id=at(base + (q + k) % 4, (y + j) % 2), device_id_type=MESH,
                    ).wait_recv()
                    att_copy(h, k, j).wait_send()
        att_own(h).wait()

    per = layers // 2

    def o_slot(zz, xs, cs, ys, h):
        return ofull_ref.at[ys, zz % per, xs, cs, pl.ds(h * half, half)]

    def o_source(zz, own_block, h):
        return wo_ref.at[pl.ds(h * half, half)] if own_block else oz_ref.at[zz, h]

    def o_far(zz, own_block, h):
        goal = zz // per
        return pltpu.make_async_remote_copy(
            src_ref=o_source(zz, own_block, h), dst_ref=o_slot(zz, x, c, y, h),
            send_sem=o_send.at[zz, h, 0], recv_sem=o_recv.at[zz % per, h, 1, (y + goal) % 2],
            device_id=at(base + xq, goal), device_id_type=MESH,
        )

    def o_near(zz, own_block, h):
        return pltpu.make_async_remote_copy(
            src_ref=o_source(zz, own_block, h), dst_ref=o_slot(zz, x, c, y, h),
            send_sem=o_send.at[zz, h, 1], recv_sem=o_recv.at[zz % per, h, 0, 1],
            device_id=over, device_id_type=MESH,
        )

    def o_self(zz, own_block, h):
        return pltpu.make_async_copy(
            o_source(zz, own_block, h), o_slot(zz, x, c, y, h), o_local.at[zz % per, h]
        )

    def o_give(zz, own_block, h):
        o_far(zz, own_block, h).start()

        @pl.when(zz // per == y)
        def _():
            o_self(zz, own_block, h).start()

        @pl.when(zz // per != y)
        def _():
            o_near(zz, own_block, h).start()

    def o_give_dist(d, among):
        for h in range(2):
            for way in range(2 if d else 1):

                @pl.when(among(way, d))
                def _(way=way, h=h):
                    o_give(z - d if way == 0 else z + d, d == 0, h)

    def o_drain():
        for d in range(layers):
            for h in range(2):
                for way in range(2 if d else 1):

                    @pl.when(z_has(way, d))
                    def _(way=way, h=h, d=d):
                        zz = z - d if way == 0 else z + d
                        o_far(zz, d == 0, h).wait_send()

                        @pl.when(zz // per != y)
                        def _():
                            o_near(zz, d == 0, h).wait_send()

    def o_flip(zz, h, dx, dy, landing=False):
        xs = (x + dx) % 2
        ys = (y + dy) % 2
        block = o_slot(zz, xs, 1 - c if landing else c, ys, h)
        return pltpu.make_async_remote_copy(
            src_ref=block, dst_ref=block,
            send_sem=of_send.at[zz % per, h, dx, dy], recv_sem=of_recv.at[zz % per, h, dx, dy],
            device_id=twin, device_id_type=MESH,
        )

    def o_take(zz, h):
        for dx in range(2):
            for dy in range(2):
                if dx or dy:
                    came = o_slot(zz, (x + dx) % 2, c, (y + dy) % 2, h)
                    pltpu.make_async_remote_copy(
                        src_ref=came, dst_ref=came,
                        send_sem=o_send.at[zz, h, 0], recv_sem=o_recv.at[zz % per, h, dx, dy],
                        device_id=twin, device_id_type=MESH,
                    ).wait_recv()
                else:
                    o_self(zz, False, h).wait()
                o_flip(zz, h, dx, dy).start()

    def o_take_end(zz, h):
        for dx in range(2):
            for dy in range(2):
                o_flip(zz, h, dx, dy, True).wait_recv()
                o_flip(zz, h, dx, dy).wait_send()

    ends = (z == 0).astype(jnp.int32) + (z == layers - 1).astype(jnp.int32)
    pl.semaphore_wait(barrier, 9 - ends)

    queries = [heads_at + h for h in range(nheads)]
    outs = [outs_at, outs_at + 1]
    every = range(1, layers)
    a2a_start(0)
    for w in outs:
        z_begin(w)
    load_in(0).wait()
    load_in(1).wait()
    norm_sums()
    s_copy().start()
    halo_fill()
    s_copy().wait()
    norm_apply()
    n_copy(1, 0).start()
    n_copy(2, 1).start()
    n_copy(0, 0).start()
    n_copy(0, 1).start()
    a2a_wait(0)
    z_begin(0)
    a2a_start(1)
    for w in outs:
        z_relay(w, 1)

    n_copy(1, 0, xq, y).wait_recv()
    n_copy(1, 1).start()
    f_copy(0, 0).start()
    n_copy(2, 1, q, 1 - y).wait_recv()
    n_copy(2, 0).start()
    f_copy(1, 1).start()

    z_relay(0, 1)
    for w in outs:
        z_relay(w, 2)
    a2a_wait(1)
    z_begin(1)

    n_copy(1, 1, xq, y).wait_recv()
    n_copy(2, 0, q, 1 - y).wait_recv()
    d_copy(0).start()
    d_copy(1).start()
    f_copy(0, 1).start()
    f_copy(1, 0).start()
    for w in queries:
        a2a_start(w)

    z_relay(0, 2)
    z_relay(1, 1)
    z_wait(0, *every)
    for p in range(2):
        n_copy(0, p, tq, y).wait_recv()
        f_copy(1, p, True).wait_recv()

    def project_pair(w, side):
        @pl.loop(0, 2)
        def _(j):
            project(w, 2 * side + j)

    project_pair(0, x)
    z_relay(1, 2)
    for p in range(2):
        d_copy(p, True).wait_recv()
        f_copy(2, p).start()
    for w in outs:
        z_wait(w, *every)
    for d in range(layers):
        o_give_dist(d, z_has)
    for w in queries:
        a2a_wait(w)
        z_begin(w, False)
    for p in range(2):
        f_copy(0, p, True).wait_recv()
        f_copy(2, p, True).wait_recv()
    project_pair(0, 1 - x)
    halo_start(0)
    z_wait(1, *every)
    project_pair(1, x)
    project_pair(1, 1 - x)
    halo_start(1)

    def o_take_all(early):
        for n in range(per):
            zz = per * y + n
            close = jnp.logical_and(zz - z <= 1, z - zz <= 1)

            @pl.when(close if early else jnp.logical_not(close))
            def _(zz=zz):
                for h in range(2):
                    o_take(zz, h)

    for h in range(nheads):
        last = h == nheads - 1
        if last:
            z_begin(queries[h], True)
        if h:
            z_pace(queries[h - 1])
        if not last:
            z_begin(queries[h], True)
        for d in every[:-1]:
            z_relay(queries[h], d)
        if h == 0:
            halo_wait(0)
            halo_wait(1)
        z_wait(queries[h], 1)
        if last:
            query_begin(h)
        z_wait(queries[h], *every[1:])
        @pl.loop(0, 4)
        def _(n, h=h):
            k = 3 - n
            blk = (q + k) % 4
            project_query(h, blk)
            attend_block(h, blk)
            att_start(h, k, blk)

        if h < 2:
            o_take_all(h == 0)
    for h in range(nheads):
        att_end(h)
    for zz in range(per):
        for h in range(2):
            o_take_end(per * y + zz, h)
    for w in range(outs_at):
        for k in (1, 2, 3):
            a2a(w, k).wait_send()
    for item in range(items):
        z_drain(item, item in queries[:-1])
    for p in range(2):
        for way in range(3):
            n_copy(way, p).wait_send()
        d_copy(p).wait_send()
        for kind in range(3):
            f_copy(kind, p).wait_send()
    halo_drain(0)
    halo_drain(1)
    o_drain()


def run_layers(tile_mask, latent, probe, gain, wk, wv, wq, wo):
    layers = lax.axis_size("ctx") // 4
    tok, own = latent.shape
    rows, width = wk.shape
    cols = width // 4
    nheads = cols // HD
    half = rows // 2
    dma = pltpu.SemaphoreType.DMA
    bf = jnp.bfloat16
    vmem = pl.BlockSpec(memory_space=pltpu.VMEM)
    smem = pl.BlockSpec(memory_space=pltpu.SMEM)
    anywhere = pl.BlockSpec(memory_space=pl.ANY)
    return pl.pallas_call(
        functools.partial(layer_kernel, layers),
        out_shape=(
            jax.ShapeDtypeStruct((2, 2, tok, width), bf),
            jax.ShapeDtypeStruct((layers // 2, 2, 2, 2, rows, width), bf),
            jax.ShapeDtypeStruct((layers, 2, half, width), bf),
        ),
        in_specs=[smem, anywhere, anywhere, vmem] + [anywhere] * 4,
        out_specs=(anywhere,) * 3,
        scratch_shapes=[
            pltpu.VMEM((4, 2, 2 * tok, own), bf),
            pltpu.VMEM((2, layers, 4, rows, cols), bf),
            pltpu.VMEM((nheads, layers, 4, rows, HD), bf),
            pltpu.VMEM((6 * tok, 2 * cols), bf),
            pltpu.VMEM((6 * tok, 2 * cols), bf),
            pltpu.VMEM((tok, 2 * HD), bf),
            pltpu.VMEM((4, 2, tok, HD), jnp.float32),
            pltpu.VMEM((nheads, 4, 2, tok, HD), bf),
            pltpu.VMEM((tok, HD), jnp.float32),
            pltpu.VMEM((tok, HD), jnp.float32),
            dma((2,)), dma((2 + nheads, 3)), dma((2 + nheads, 3)), dma((2 + nheads,)),
            dma((4 + nheads, 2, layers - 1)), dma((4 + nheads, 2, layers - 1)), dma, dma,
            dma((3, 2)), dma((3, 2)), dma((2,)), dma((2,)), dma((3, 2)), dma((3, 2)),
            dma((2, 2)), dma((2, 2)),
            dma((nheads, 4, 2)), dma((nheads, 4, 2)), dma((nheads,)),
            dma((layers, 2, 2)), dma((layers // 2, 2, 2, 2)), dma((layers // 2, 2)),
            dma((layers // 2, 2, 2, 2)), dma((layers // 2, 2, 2, 2)),
        ],
        compiler_params=pltpu.CompilerParams(
            collective_id=0, has_side_effects=True, vmem_limit_bytes=60 * MIB
        ),
    )(tile_mask, latent, probe, gain, wk, wv, wq, wo)


def finish_kernel(head_ref, att_ref, o_ref, lat_ref, probe_ref, mixed_ref, tang_ref, trace_ref):
    tok, chunk = lat_ref.shape
    contract = (((1,), (1,)), ((), ()))
    branch = None
    for ys in range(2):
        lhs = att_ref[ys].reshape(2 * tok, att_ref.shape[-1])
        term = lax.dot_general(lhs, o_ref[ys], contract, preferred_element_type=jnp.float32)
        term = term.astype(jnp.bfloat16).astype(jnp.float32)
        branch = term if branch is None else branch + term
    branch_t = branch[tok:]
    mixed_ref[...] = (lat_ref[...].astype(jnp.float32) + branch[:tok]).astype(jnp.bfloat16)
    tang_ref[...] = branch_t.astype(jnp.bfloat16)
    terms = jnp.sum(probe_ref[...].astype(jnp.float32) * branch_t, -1, keepdims=True)

    @pl.when(pl.program_id(0) == 0)
    def _():
        trace_ref[...] = jnp.zeros_like(trace_ref)

    trace_ref[...] += jnp.broadcast_to(terms, trace_ref.shape)


def finish(att, ofull, latent, probe):
    tok, own = latent.shape
    width = ofull.shape[-1]
    chunk = 512
    steps = own // chunk
    blocks = ofull.reshape(2, own, width)
    return pl.pallas_call(
        finish_kernel,
        grid_spec=pltpu.PrefetchScalarGridSpec(
            num_scalar_prefetch=1,
            grid=(steps,),
            in_specs=[
                pl.BlockSpec((2, 2, tok, width), lambda i, h: (0, 0, 0, 0)),
                pl.BlockSpec((2, chunk, width), lambda i, h: (0, i, 0)),
                pl.BlockSpec((tok, chunk), lambda i, h: (0, i)),
                pl.BlockSpec((tok, chunk), lambda i, h: (0, h[0] * steps + i)),
            ],
            out_specs=[
                pl.BlockSpec((tok, chunk), lambda i, h: (0, i)),
                pl.BlockSpec((tok, chunk), lambda i, h: (0, i)),
                pl.BlockSpec((tok, HD), lambda i, h: (0, 0)),
            ],
        ),
        out_shape=(
            jax.ShapeDtypeStruct((tok, own), jnp.bfloat16),
            jax.ShapeDtypeStruct((tok, own), jnp.bfloat16),
            jax.ShapeDtypeStruct((tok, HD), jnp.float32),
        ),
        compiler_params=pltpu.CompilerParams(vmem_limit_bytes=48 * MIB),
    )(lax.axis_index("head").reshape(1), att, blocks, latent, probe)


def layer_shards(latent, probe, norm_gain, w_query, w_key, w_value, w_out, tile_mask):
    att, ofull, _ = run_layers(
        tile_mask, latent, probe, norm_gain.reshape(2, 1, D // 2),
        w_key, w_value, w_query, w_out.T,
    )
    mixed, tangent, trace = finish(att, ofull, latent, probe)
    terms = trace[:, 0]
    return (mixed, tangent, terms + lax.ppermute(terms, "head", [(0, 1), (1, 0)]))


def solution(mesh):
    placed = (
        P("ctx", "head"),
        P("ctx", None),
        P(),
        P("ctx", "head"),
        P("ctx", "head"),
        P("ctx", "head"),
        P("head", "ctx"),
        P(),
    )
    by_layer = mesh.shape["ctx"] == 16 and mesh.shape["head"] == 2
    return jax.shard_map(
        layer_shards if by_layer else shards,
        mesh=mesh,
        in_specs=placed,
        out_specs=(P("ctx", "head"), P("ctx", "head"), P("ctx")),
        check_vma=False,
    )
```
